32 devices in a mesh: seq: 4 (over z), ctx: 2 (over x), wt: 4 (over y, core).
Axes of the slice: x: 2, y: 2, z: 4, core: 2. Of those that a mesh axis runs over, the one named last changes fastest.
Arguments:
- tokens: bfloat16 [16, 1024, 512], P(('seq', 'wt'), 'ctx'), may hold values from -6 to 6
- cotangent: bfloat16 [16, 1024, 512], P(('seq', 'wt'), 'ctx'), may hold values from -6 to 6
- deal: int32 [4], replicated, may hold values from 0 to 3, each once
- memory_len: int32 [16, 4], P(('seq', 'wt')), may hold values from 0 to 768, as said below
- neighbours: int32 [16, 1024, 4], P(('seq', 'wt'), 'ctx'), may hold values from 0 to 1023
- w_qkv: bfloat16 [512, 1536], P('wt'), may hold values from -0.25 to 0.25
- w_out: bfloat16 [512, 512], P('wt'), may hold values from -1 to 1
- w_up: bfloat16 [512, 2048], P('wt'), may hold values from -0.25 to 0.25
- w_down: bfloat16 [2048, 512], P('wt'), may hold values from -0.125 to 0.125
- w_memory: bfloat16 [512, 512], P('wt'), may hold values from -0.5 to 0.5
- gain_attn: bfloat16 [512], P('wt'), may hold values from 0.5 to 1.5
- gain_ffn: bfloat16 [512], P('wt'), may hold values from 0.5 to 1.5
- gate_vec: bfloat16 [512], P('wt'), may hold values from -0.25 to 0.25
- slopes: bfloat16 [8], P('wt'), may hold values from 0.019897461 to 0.5
Outputs:
- layer_out: bfloat16 [16, 1024, 512], P(('seq', 'wt'), 'ctx')
- grad_tokens: float32 [16, 1024, 512], P(('seq', 'wt'), 'ctx')
- grad_qkv: float32 [512, 1536], P('wt')
- grad_out: float32 [512, 512], P('wt')
- grad_up: float32 [512, 2048], P('wt')
- grad_down: float32 [2048, 512], P('wt')
- grad_memory: float32 [512, 512], P('wt')
- grad_gain_attn: float32 [512], P('wt')
- grad_gain_ffn: float32 [512], P('wt')
- grad_gate: float32 [512], P('wt')
- grad_slopes: float32 [8], P('wt')
The draws below stay inside these ranges and needn't reach their ends.
Inputs may be any that keep to these rules, and one draw needn't show every extreme that they name: deal is a permutation of the blocks; device c of ctx holds block slots 2c and 2c + 1. `memory_len`: block 3 of every sequence has the value 1024 - 256.
All inputs are finite; a program needn't handle non-finite values.
Results may differ from the reference program's by a relative error of at most 0.028.
Values may be sent and summed in bfloat16 or wider, within the bound.
No kernel may reach another device: no remote copies, remote signals or barrier semaphores. Data moves between devices by JAX's collectives and lax.ppermute only.
A program may use at most 256 MiB of HBM per device.

```python
import math
import jax
import jax.numpy as jnp
from jax import lax

D = 512
HEADS = 8
FF = 2048
BLK = 256
KNN = 4
NBLK = 4
LEN = 1024
SEQS = 16


def draw_memory_len(key, part):
    spans = jax.random.randint(key, (SEQS, NBLK), 0, LEN - BLK + 1, dtype=jnp.int32)
    column = jnp.arange(NBLK, dtype=jnp.int32)[None, :]
    return jnp.where(column == NBLK - 1, LEN - BLK, spans).astype(jnp.int32)


def touch_ends(drawn, rng, smallest, high):
    index_at = [jax.random.randint(jax.random.fold_in(rng, axis), (), 0, length) for axis, length in enumerate(drawn.shape)]
    main_axis = drawn.shape.index(max(drawn.shape))
    beside = index_at[:main_axis] + [(index_at[main_axis] + 1) % drawn.shape[main_axis]] + index_at[main_axis + 1:]
    return drawn.at[tuple(index_at)].set(smallest).at[tuple(beside)].set(high)


def shard_levels(key, extent, shards, low, top_value):
    def one(axis_at, shards_of):
        steps = jax.random.uniform(jax.random.fold_in(jax.random.fold_in(key, 6), axis_at), (shards_of,), jnp.float32, low / len(shards), top_value / len(shards))
        return jnp.repeat(jnp.exp(steps), extent[axis_at] // shards_of).reshape((-1,) + (1,) * (len(extent) - axis_at - 1))

    level = one(*shards[0])
    for cut in shards[1:]:
        level = level * one(*cut)
    return level


def scatter_about(own_key, extent, deviation, bound, cuts=(), held_as=jnp.bfloat16):
    drawn = jax.random.normal(own_key, extent, jnp.float32) * deviation
    if len(cuts) > 0:
        drawn = shard_levels(own_key, extent, cuts, -0.22, 0.18) * drawn
    return jnp.clip(drawn, min=-bound, max=bound).astype(held_as)


def setup_inputs(seed: int = 0) -> dict:
    arg_keys = jax.random.split(jax.random.key(seed), 15)
    tokens = scatter_about(arg_keys[0], (SEQS, LEN, D), 1.0, 6.0, ((0, 16), (1, 2)))
    cotangent = scatter_about(arg_keys[1], (SEQS, LEN, D), 1.0, 6.0, ((0, 16), (1, 2)))
    deal = jax.random.permutation(arg_keys[2], NBLK).astype(jnp.int32)
    memory_len = draw_memory_len(jax.random.fold_in(arg_keys[14], 71), 0)
    neighbours = touch_ends(jax.random.randint(arg_keys[4], (SEQS, LEN, KNN), 0, LEN), jax.random.fold_in(arg_keys[4], 1), 0, LEN - 1).astype(jnp.int32)
    w_qkv = scatter_about(arg_keys[5], (D, 3 * D), D ** -0.5, 0.25, ((0, 4),))
    w_out = scatter_about(arg_keys[6], (D, D), (D // 16) ** -0.5, 1.0, ((0, 4),))
    w_up = scatter_about(arg_keys[7], (D, FF), D ** -0.5, 0.25, ((0, 4),))
    w_down = scatter_about(arg_keys[8], (FF, D), FF ** -0.5, 0.125, ((0, 4),))
    w_memory = scatter_about(arg_keys[9], (D, D), (D // 4) ** -0.5, 0.5, ((0, 4),))
    gain_attn = jnp.clip(1.0 + 0.1 * jax.random.normal(arg_keys[10], (D,), jnp.float32), 0.5, 1.5).astype(jnp.bfloat16)
    gain_ffn = jnp.clip(1.0 + 0.1 * jax.random.normal(arg_keys[11], (D,), jnp.float32), 0.5, 1.5).astype(jnp.bfloat16)
    gate_vec = scatter_about(arg_keys[12], (D,), D ** -0.5, 0.25, ((0, 4),))
    slopes = jnp.clip(jnp.exp(math.log(0.5) - 3.224016 * jax.random.uniform(arg_keys[13], (HEADS,), jnp.float32) ** shard_levels(arg_keys[13], (HEADS,), ((0, 4),), -0.2, 0.2)), 0.019897461, 0.5).astype(jnp.bfloat16)
    return {"tokens": tokens, "cotangent": cotangent, "deal": deal, "memory_len": memory_len, "neighbours": neighbours, "w_qkv": w_qkv, "w_out": w_out, "w_up": w_up, "w_down": w_down, "w_memory": w_memory, "gain_attn": gain_attn, "gain_ffn": gain_ffn, "gate_vec": gate_vec, "slopes": slopes}


PRECISE = lax.Precision.HIGHEST
EPSILON = 1e-05

@jax.custom_vjp
def low(v):
    return lax.optimization_barrier(v.astype(jnp.bfloat16)).astype(jnp.float32)

@jax.custom_vjp
def low_back(v):
    return v

def low_keep(v):
    return (low(v), None)

def low_pass(kept, grad):
    return (grad,)

def back_keep(v):
    return (v, None)

def back_low(kept, grad):
    return (low(grad),)
low.defvjp(low_keep, low_pass)
low_back.defvjp(back_keep, back_low)

def layer_norm(values, gain):
    centred = values - lax.optimization_barrier(jnp.mean(values, axis=-1, keepdims=True))
    return centred * lax.rsqrt(lax.optimization_barrier(jnp.mean(centred * centred, axis=-1, keepdims=True)) + EPSILON) * gain

def recall(queries, near_keys, near_values, head_count):
    row_count, pick_count, model_width = near_keys.shape
    head_width = model_width // head_count
    q_heads = queries.reshape(row_count, head_count, head_width)
    k_heads = near_keys.reshape(row_count, pick_count, head_count, head_width)
    v_heads = near_values.reshape(row_count, pick_count, head_count, head_width)
    logits = jnp.einsum('rhd,rkhd->rhk', q_heads, k_heads, precision=PRECISE) * head_width ** (-0.5)
    weights = jnp.exp(logits - lax.optimization_barrier(jnp.max(logits, axis=-1, keepdims=True)))
    weights = weights / lax.optimization_barrier(jnp.sum(weights, axis=-1, keepdims=True))
    return jnp.einsum('rhk,rkhd->rhd', weights, v_heads, precision=PRECISE).reshape(row_count, model_width)

def attend_block(block, key_rows, value_rows, key_pos, slope_all):
    queries, query_pos, edge_low, edge_high = block
    row_count, model_width = queries.shape
    head_count = slope_all.shape[0]
    head_width = model_width // head_count
    q_heads = queries.reshape(row_count, head_count, head_width)
    k_heads = key_rows.reshape(key_rows.shape[0], head_count, head_width)
    v_heads = value_rows.reshape(value_rows.shape[0], head_count, head_width)
    distance = jnp.log1p(jnp.abs(query_pos[:, None] - key_pos[None, :]).astype(jnp.float32))
    visible = (key_pos[None, :] >= edge_low[:, None]) & (key_pos[None, :] < edge_high[:, None])
    scores = jnp.einsum('rhd,khd->hrk', q_heads, k_heads, precision=PRECISE) * head_width ** (-0.5)
    scores = scores - slope_all[:, None, None] * distance[None]
    scores = low_back(jnp.where(visible[None], scores, -1000000000.0))
    shifted = jnp.exp(scores - lax.optimization_barrier(jnp.max(scores, axis=-1, keepdims=True)))
    weights = low(shifted / lax.optimization_barrier(jnp.sum(shifted, axis=-1, keepdims=True)))
    return jnp.einsum('hrk,khd->rhd', weights, v_heads, precision=PRECISE).reshape(row_count, model_width)

def one_sequence(tokens, memory_len, neighbours, deal, params):
    w_qkv, w_out, w_up, w_down, w_memory, gain_attn, gain_ffn, gate_vec, slopes = params
    seq_len, model_width = tokens.shape
    block_count = deal.shape[0]
    block_len = seq_len // block_count
    head_count = slopes.shape[0]
    offsets = jnp.arange(block_len, dtype=jnp.int32)
    block_ids = jnp.arange(block_count, dtype=jnp.int32)
    starts = (deal * block_len).astype(jnp.int32)
    key_pos = (starts[:, None] + offsets[None, :]).reshape(seq_len)
    row_start = jnp.repeat(starts, block_len)
    row_memory = jnp.repeat(memory_len[deal], block_len)
    edge_low = row_start - row_memory
    edge_high = row_start + block_len
    normed = low(layer_norm(tokens, gain_attn))
    joined = low_back(low(jnp.dot(normed, w_qkv, precision=PRECISE)))
    queries = joined[:, :model_width]
    key_rows = joined[:, model_width:2 * model_width]
    value_rows = joined[:, 2 * model_width:]
    block_rows = min(512, seq_len)
    block_num = seq_len // block_rows
    attend = jax.checkpoint(lambda block: attend_block(block, key_rows, value_rows, key_pos, slopes))
    mixed = lax.map(attend, (queries.reshape(block_num, block_rows, model_width), key_pos.reshape(block_num, block_rows), edge_low.reshape(block_num, block_rows), edge_high.reshape(block_num, block_rows)))
    mixed = low_back(low(mixed.reshape(seq_len, model_width)))
    hidden = tokens + low_back(jnp.dot(mixed, w_out, precision=PRECISE))
    normed_two = low(layer_norm(hidden, gain_ffn))
    pre_act = low_back(jnp.dot(normed_two, w_up, precision=PRECISE))
    activated = low(jax.nn.gelu(pre_act))
    hidden_two = hidden + low_back(jnp.dot(activated, w_down, precision=PRECISE))
    inverse = lax.optimization_barrier(jnp.sum(block_ids[:, None] * (deal[:, None] == block_ids[None, :]).astype(jnp.int32), axis=0))
    near_rows = (inverse[neighbours // block_len] * block_len + neighbours % block_len).reshape(-1)
    pick_count = neighbours.shape[1]
    near_keys = key_rows[near_rows].reshape(seq_len, pick_count, model_width)
    near_values = value_rows[near_rows].reshape(seq_len, pick_count, model_width)
    recalled = low(recall(queries, near_keys, near_values, head_count))
    memory_out = low_back(jnp.dot(recalled, w_memory, precision=PRECISE))
    gate_open = jax.nn.sigmoid(jnp.dot(hidden_two, gate_vec, precision=PRECISE))[:, None]
    return hidden_two + gate_open * (memory_out - hidden_two)

def reference(tokens, cotangent, deal, memory_len, neighbours, w_qkv, w_out, w_up, w_down, w_memory, gain_attn, gain_ffn, gate_vec, slopes):
    params = tuple((item.astype(jnp.float32) for item in (w_qkv, w_out, w_up, w_down, w_memory, gain_attn, gain_ffn, gate_vec, slopes)))

    def forward(inputs, weights):
        return lax.map(lambda item: one_sequence(item[0], item[1], item[2], deal, weights), (inputs, memory_len, neighbours))
    result, pull = jax.vjp(forward, tokens.astype(jnp.float32), params)
    grad_inputs, grads = pull(cotangent.astype(jnp.float32))
    return (result.astype(jnp.bfloat16), grad_inputs, grads[0], grads[1], grads[2], grads[3], grads[4], grads[5], grads[6], grads[7], grads[8])
```

```python
import functools
import jax
import jax.numpy as jnp
from jax import lax
from jax.experimental import pallas as pl
from jax.experimental.pallas import tpu as pltpu
from jax.sharding import PartitionSpec as P

EPSILON = 1e-05
F32 = jnp.float32
BF16 = jnp.bfloat16
NT = (((1,), (1,)), ((), ()))
NN = (((1,), (0,)), ((), ()))
TN = (((0,), (0,)), ((), ()))
HIDDEN = 1e12
ABSENT = -1e30
VMEM = 56 * 1024 * 1024


def product(left, right, dims):
    return lax.dot_general(left, right, dims, preferred_element_type=F32)


def swap(value, axis, bit):
    size = lax.axis_size(axis)
    return lax.ppermute(value, axis, [(i, i ^ bit) for i in range(size)])


def bits_of(axis):
    size = lax.axis_size(axis)
    bits = []
    bit = 1
    while bit < size:
        bits.append(bit)
        bit *= 2
    return bits


def upper(axis, bit):
    return (lax.axis_index(axis) & bit) != 0


def gather_rows(shard, axis):
    rows, cols = shard.shape
    parts = shard.reshape(1, rows, cols)
    for bit in reversed(bits_of(axis)):
        other = swap(parts, axis, bit)
        high = upper(axis, bit)
        low_part = jnp.where(high, other, parts)
        high_part = jnp.where(high, parts, other)
        parts = jnp.stack([low_part, high_part], axis=1)
        parts = parts.reshape(-1, rows, cols)
    return parts.reshape(-1, cols)


def gather_near(block, axis):
    for bit in bits_of(axis):
        block = jnp.concatenate([block, swap(block, axis, bit)], axis=0)
    return block


def scatter_near(rows, axis):
    for bit in reversed(bits_of(axis)):
        half = rows.shape[0] // 2
        got = swap(rows[half:].astype(BF16), axis, bit)
        rows = rows[:half] + got.astype(F32)
    return rows


def halve(parts, axis, bit, place):
    high = upper(axis, bit)
    first = lax.index_in_dim(parts, 0, place, keepdims=False)
    second = lax.index_in_dim(parts, 1, place, keepdims=False)
    got = swap(jnp.where(high, first, second), axis, bit)
    return (jnp.where(high, second, first).astype(F32) + got.astype(F32)).astype(BF16)


def widen(part, axis, bit):
    other = swap(part, axis, bit)
    high = upper(axis, bit)
    return jnp.concatenate([jnp.where(high, other, part), jnp.where(high, part, other)], axis=0)


def add_both(part, axis, bit):
    return (part.astype(F32) + swap(part, axis, bit).astype(F32)).astype(BF16)


def sum_to_owner(grad, full_scatter):
    rows, cols = grad.shape
    bits = bits_of("wt")
    size = lax.axis_size("wt")
    parts = grad.astype(BF16).reshape([2] * len(bits) + [rows // size, cols])
    for n, bit in enumerate(bits):
        parts = halve(parts, "wt", bit, len(bits) - 1 - n)
    steps = [("ctx", bit) for bit in bits_of("ctx")]
    seq_steps = [("seq", bit) for bit in bits_of("seq")]
    if full_scatter:
        steps, seq_steps = steps + seq_steps, []
    for axis, bit in steps:
        parts = halve(parts.reshape(2, parts.shape[0] // 2, cols), axis, bit, 0)
    for axis, bit in seq_steps:
        parts = add_both(parts, axis, bit)
    for axis, bit in reversed(steps):
        parts = widen(parts, axis, bit)
    return parts.astype(F32)


def sum_small(vector):
    for axis in ("wt", "ctx", "seq"):
        for bit in bits_of(axis):
            vector = vector + swap(vector, axis, bit)
    return vector


def own_part(vector):
    size = lax.axis_size("wt")
    length = vector.shape[0] // size
    return lax.dynamic_slice_in_dim(vector, lax.axis_index("wt") * length, length, 0)


def forward_body(
    first_head, rows, slope_ref, q_ref, k_ref, v_ref, b_ref, c_ref, o_ref, m_ref, r1_ref, r2_ref, e1_ref, e2_ref
):
    pair = pl.program_id(0)
    low_lanes = lax.broadcasted_iota(jnp.int32, (rows, 128), 1) < 64
    for start in range(0, q_ref.shape[0], rows):
        at = pl.ds(start, rows)
        mixed = []
        for side in range(2):
            slope = slope_ref[0, first_head + 2 * pair + side]
            q_head = jnp.where(low_lanes == (side == 0), q_ref[at, :], 0).astype(BF16)
            raw = product(q_head, k_ref[...], NT)
            for values, table in ((raw - slope * b_ref[at, :], e1_ref), (raw + c_ref[at, :], e2_ref)):
                peak = jnp.max(values, axis=1, keepdims=True)
                shifted = jnp.exp(values - peak)
                total = jnp.sum(shifted, axis=1, keepdims=True)
                weights = shifted.astype(BF16)
                table[side, at, :] = weights
                mixed.append((product(weights, v_ref[...], NN), 1.0 / total))
        for slot, value_ref, recip_ref in ((0, o_ref, r1_ref), (1, m_ref, r2_ref)):
            recip = jnp.where(low_lanes, mixed[slot][1], mixed[2 + slot][1])
            recip_ref[at, :] = recip
            value_ref[at, :] = jnp.where(low_lanes, mixed[slot][0], mixed[2 + slot][0]) * recip


def attend_forward(slopes, q, k, v, bias, count, first, pairs):
    row_count = q.shape[0]
    key_count = k.shape[0]
    step_rows = max(64, min(row_count, (512 * 1024) // key_count))
    rows = min(256, step_rows)
    elements = 2 * pairs * row_count * key_count
    own = lambda p, i: (i, p)
    return pl.pallas_call(
        functools.partial(forward_body, 2 * first, rows),
        grid=(pairs, row_count // step_rows),
        in_specs=[
            pl.BlockSpec(memory_space=pltpu.SMEM),
            pl.BlockSpec((step_rows, 128), lambda p, i: (i, p + first)),
            pl.BlockSpec((key_count, 128), lambda p, i: (0, p + first)),
            pl.BlockSpec((key_count, 128), lambda p, i: (0, p + first)),
            pl.BlockSpec((step_rows, key_count), lambda p, i: (i, 0)),
            pl.BlockSpec((step_rows, key_count), lambda p, i: (i, 0)),
        ],
        out_specs=[pl.BlockSpec((step_rows, 128), own)] * 4
        + [pl.BlockSpec((2, step_rows, key_count), lambda p, i: (p, i, 0))] * 2,
        out_shape=[jax.ShapeDtypeStruct((row_count, 128 * pairs), F32)] * 4
        + [jax.ShapeDtypeStruct((2 * pairs, row_count, key_count), BF16)] * 2,
        compiler_params=pltpu.CompilerParams(vmem_limit_bytes=VMEM),
        cost_estimate=pl.CostEstimate(
            flops=elements * 64 * 2 * 3, transcendentals=2 * elements, bytes_accessed=4 * elements
        ),
        name="attend_forward",
    )(slopes, q, k, v, bias, count)


def backward_body(
    rows, q_ref, k_ref, v_ref, go_ref, gm_ref, o_ref, m_ref, r1_ref, r2_ref, b_ref, e1_ref, e2_ref,
    gq_ref, gk_ref, gv_ref, gs_ref,
):
    chunk = pl.program_id(1)
    low_lanes = lax.broadcasted_iota(jnp.int32, (rows, 128), 1) < 64
    keys = k_ref[...]
    vals = v_ref[...]
    for start in range(0, q_ref.shape[0], rows):
        at = pl.ds(start, rows)
        g1 = (go_ref[at, :].astype(F32) * r1_ref[at, :]).astype(BF16)
        g2 = (gm_ref[at, :].astype(F32) * r2_ref[at, :]).astype(BF16)
        t1 = g1.astype(F32) * o_ref[at, :]
        t2 = g2.astype(F32) * m_ref[at, :]
        q_turned = q_ref[at, :].T
        g1_turned = g1.T
        g2_turned = g2.T
        grads = []
        for side in range(2):
            mine = low_lanes == (side == 0)
            d1 = jnp.sum(jnp.where(mine, t1, 0.0), axis=1, keepdims=True)
            d2 = jnp.sum(jnp.where(mine, t2, 0.0), axis=1, keepdims=True)
            e1 = e1_ref[side, at, :]
            e2 = e2_ref[side, at, :]
            p1 = product(jnp.where(mine, g1, 0).astype(BF16), vals, NT)
            ds1 = e1.astype(F32) * (p1 - d1)
            slope_term = jnp.sum(ds1 * b_ref[at, :], axis=0, keepdims=True)
            p2 = product(jnp.where(mine, g2, 0).astype(BF16), vals, NT)
            ds = (ds1 + e2.astype(F32) * (p2 - d2)).astype(BF16)
            grads.append(product(ds, keys, NN))
            head = slice(64 * side, 64 * side + 64)
            gk = product(q_turned[head, :], ds, NN)
            gv = product(g1_turned[head, :], e1, NN) + product(g2_turned[head, :], e2, NN)
            if start == 0:
                gk_ref[head, :] = gk
                gv_ref[head, :] = gv
                gs_ref[pl.ds(side, 1), :] = slope_term
            else:
                gk_ref[head, :] += gk
                gv_ref[head, :] += gv
                gs_ref[pl.ds(side, 1), :] += slope_term
        gq = jnp.where(low_lanes, grads[0], grads[1]) * 0.125
        gq_ref[at, :] = jnp.where(chunk == 0, gq, gq_ref[at, :] + gq)


def attend_backward(q, k, v, go, gm, saved, bias, first, pairs):
    o, m, r1, r2, e1, e2 = saved
    row_count = q.shape[0]
    key_count = k.shape[0]
    step_keys = min(1024, key_count)
    elements = 2 * pairs * row_count * key_count
    wide = pl.BlockSpec((row_count, 128), lambda p, c: (0, p + first))
    own = pl.BlockSpec((row_count, 128), lambda p, c: (0, p))
    near = pl.BlockSpec((step_keys, 128), lambda p, c: (c, p + first))
    table = pl.BlockSpec((2, row_count, step_keys), lambda p, c: (p, 0, c))
    turned = pl.BlockSpec((128, step_keys), lambda p, c: (p, c))
    return pl.pallas_call(
        functools.partial(backward_body, 256),
        grid=(pairs, key_count // step_keys),
        in_specs=[wide, near, near, wide, wide, own, own, own, own]
        + [pl.BlockSpec((row_count, step_keys), lambda p, c: (0, c)), table, table],
        out_specs=[own, turned, turned, pl.BlockSpec((None, 2, step_keys), lambda p, c: (p, 0, c))],
        out_shape=[
            jax.ShapeDtypeStruct((row_count, 128 * pairs), F32),
            jax.ShapeDtypeStruct((128 * pairs, key_count), F32),
            jax.ShapeDtypeStruct((128 * pairs, key_count), F32),
            jax.ShapeDtypeStruct((pairs, 2, key_count), F32),
        ],
        compiler_params=pltpu.CompilerParams(vmem_limit_bytes=VMEM),
        cost_estimate=pl.CostEstimate(
            flops=elements * 64 * 2 * 6, transcendentals=0, bytes_accessed=4 * elements
        ),
        name="attend_backward",
    )(q, k, v, go, gm, o, m, r1, r2, bias, e1, e2)


def spread(values):
    mean = jnp.mean(values, axis=-1, keepdims=True)
    centred = values - mean
    scale = lax.rsqrt(jnp.mean(centred * centred, axis=-1, keepdims=True) + EPSILON)
    return centred * scale, scale


def spread_back(unit, scale, grad):
    along = jnp.mean(grad * unit, axis=-1, keepdims=True)
    return scale * (grad - jnp.mean(grad, axis=-1, keepdims=True) - unit * along)


def on_device(
    tokens,
    cotangent,
    deal,
    memory_len,
    neighbours,
    w_qkv,
    w_out,
    w_up,
    w_down,
    w_memory,
    gain_attn,
    gain_ffn,
    gate_vec,
    slopes,
):
    _, row_count, width = tokens.shape
    tokens = tokens.reshape(row_count, width)
    cotangent = cotangent.reshape(row_count, width)
    neighbours = neighbours.reshape(row_count, -1)
    block_count = deal.shape[0]
    ctx_size = lax.axis_size("ctx")
    wt_size = lax.axis_size("wt")
    own_blocks = block_count // ctx_size
    block_len = row_count // own_blocks
    shard = gain_attn.shape[0]
    heads_here = slopes.shape[0]
    head_count = heads_here * wt_size

    small = jnp.concatenate(
        [gain_attn, gain_ffn, gate_vec, slopes, jnp.zeros((shard - heads_here,), BF16)]
    ).reshape(1, 4 * shard)
    small_all = gather_rows(small, "wt").astype(F32)
    all_tokens = gather_near(tokens, "ctx")
    full_qkv = gather_rows(w_qkv, "wt")
    full_out = gather_rows(w_out, "wt")
    full_up = gather_rows(w_up, "wt")
    full_down = gather_rows(w_down, "wt")
    full_memory = gather_rows(w_memory, "wt")
    gain_one = small_all[:, :shard].reshape(1, width)
    gain_two = small_all[:, shard : 2 * shard].reshape(1, width)
    gate_full = small_all[:, 2 * shard : 3 * shard].reshape(1, width)
    slope_full = small_all[:, 3 * shard : 3 * shard + heads_here].reshape(1, head_count)

    offsets = jnp.arange(block_len, dtype=jnp.int32)
    owners = lax.axis_index("ctx") ^ jnp.arange(ctx_size, dtype=jnp.int32)
    slots = (owners[:, None] * own_blocks + jnp.arange(own_blocks, dtype=jnp.int32)[None, :]).reshape(-1)
    block_ids = jnp.arange(block_count, dtype=jnp.int32)
    slot_hot = (slots[:, None] == block_ids[None, :]).astype(jnp.int32)
    key_blocks = jnp.sum(slot_hot * deal[None, :], axis=1)
    key_pos = (key_blocks[:, None] * block_len + offsets[None, :]).reshape(-1)
    my_blocks = key_blocks[:own_blocks]
    row_pos = key_pos[:row_count]
    memory_hot = (my_blocks[:, None] == block_ids[None, :]).astype(jnp.int32)
    my_memory = jnp.sum(memory_hot * memory_len, axis=1)
    row_start = jnp.repeat(my_blocks * block_len, block_len)
    row_low = row_start - jnp.repeat(my_memory, block_len)
    distance = jnp.log1p(jnp.abs(row_pos[:, None] - key_pos[None, :]).astype(F32))
    visible = (key_pos[None, :] >= row_low[:, None]) & (key_pos[None, :] < (row_start + block_len)[:, None])
    bias = jnp.where(visible, distance, HIDDEN)
    hits = jnp.sum((neighbours[:, :, None] == key_pos[None, None, :]).astype(F32), axis=1)
    count = jnp.where(hits > 0.0, jnp.log(jnp.maximum(hits, 1.0)), ABSENT)

    x_all = all_tokens.astype(F32)
    unit_all, scale_all = spread(x_all)
    a1_all = (unit_all * gain_one).astype(BF16)
    a1 = a1_all[:row_count]
    q = (product(a1, full_qkv[:, :width], NN).astype(BF16).astype(F32) * 0.125).astype(BF16)
    kv = product(a1_all, full_qkv[:, width:], NN).astype(BF16)
    k = kv[:, :width]
    v = kv[:, width:]

    pairs = width // 128
    saved = attend_forward(slope_full, q, k, v, bias, count, 0, pairs)
    o, m = saved[0], saved[1]
    o_low = o.astype(BF16)
    m_low = m.astype(BF16)

    x_own = tokens.astype(F32)
    h1 = x_own + product(o_low, full_out, NN)
    unit_two, scale_two = spread(h1)
    a2 = (unit_two * gain_two).astype(BF16)
    u = product(a2, full_up, NN)
    active, gelu_back = jax.vjp(jax.nn.gelu, u)
    act = active.astype(BF16)
    h2 = h1 + product(act, full_down, NN)
    mem = product(m_low, full_memory, NN)
    gate = jax.nn.sigmoid(jnp.sum(h2 * gate_full, axis=1, keepdims=True))
    layer_out = h2 + gate * (mem - h2)

    c = cotangent.astype(F32)
    grad_mem = (c * gate).astype(BF16)
    dz = jnp.sum(c * (mem - h2), axis=1, keepdims=True) * gate * (1.0 - gate)
    gh2 = c * (1.0 - gate) + dz * gate_full
    grad_gate = jnp.sum(dz * h2, axis=0)
    gf = gh2.astype(BF16)
    gu = gelu_back(product(gf, full_down, NT))[0].astype(BF16)
    ga2 = product(gu, full_up, NT)
    gh1 = gh2 + spread_back(unit_two, scale_two, ga2 * gain_two)
    ga = gh1.astype(BF16)
    go = product(ga, full_out, NT).astype(BF16)
    gm = product(grad_mem, full_memory, NT).astype(BF16)
    g_down = product(act, gf, TN)
    g_up = product(a2, gu, TN)
    g_memory = product(m_low, grad_mem, TN)
    g_out = product(o_low, ga, TN)

    t_down = sum_to_owner(g_down, True)
    t_up = sum_to_owner(g_up, True)
    t_memory = sum_to_owner(g_memory, True)
    t_out = sum_to_owner(g_out, True)
    t_gate = own_part(sum_small(grad_gate))

    gq, gk, gv, gs = attend_backward(q, k, v, go, gm, saved, bias, 0, pairs)
    gq = gq.astype(BF16)
    gk = gk.astype(BF16)
    gv = gv.astype(BF16)
    grad_slopes = -jnp.sum(gs, axis=2).reshape(head_count)

    part = product(gk, full_qkv[:, width : 2 * width], (((0,), (1,)), ((), ()))) + product(
        gv, full_qkv[:, 2 * width :], (((0,), (1,)), ((), ()))
    )
    ga1 = scatter_near(part, "ctx") + product(gq, full_qkv[:, :width], NT)
    g_qkv = jnp.concatenate(
        [
            product(a1, gq, TN),
            product(a1_all, gk, (((0,), (1,)), ((), ()))),
            product(a1_all, gv, (((0,), (1,)), ((), ()))),
        ],
        axis=1,
    )
    t_qkv = sum_to_owner(g_qkv, False)
    t_slopes = own_part(sum_small(grad_slopes))
    grad_tokens = gh1 + spread_back(unit_all[:row_count], scale_all[:row_count], ga1 * gain_one)

    t_gain_one = jnp.sum(t_qkv * w_qkv.astype(F32), axis=1) / gain_attn.astype(F32)
    t_gain_two = jnp.sum(t_up * w_up.astype(F32), axis=1) / gain_ffn.astype(F32)
    return (
        layer_out.astype(BF16)[None],
        grad_tokens[None],
        t_qkv,
        t_out,
        t_up,
        t_down,
        t_memory,
        t_gain_one,
        t_gain_two,
        t_gate,
        t_slopes,
    )


def solution(mesh):
    rows = P(("seq", "wt"), "ctx", None)
    weight = P("wt", None)
    vector = P("wt")
    return jax.shard_map(
        on_device,
        mesh=mesh,
        in_specs=(rows, rows, P(), P(("seq", "wt"), None), rows)
        + (weight,) * 5
        + (vector,) * 4,
        out_specs=(rows, rows) + (weight,) * 5 + (vector,) * 4,
        check_vma=False,
    )
```

```python
import functools
import math
import jax
import jax.numpy as jnp
from jax import lax
from jax.experimental import pallas as pl
from jax.experimental.pallas import tpu as pltpu
from jax.sharding import PartitionSpec as P

EPSILON = 1e-05
F32 = jnp.float32
BF16 = jnp.bfloat16
NT = (((1,), (1,)), ((), ()))
NN = (((1,), (0,)), ((), ()))
HIDDEN = 1e12
ABSENT = -1e30
VMEM = 56 * 1024 * 1024
CURVE = math.sqrt(2.0 / math.pi)
CUBIC = 0.044715


def product(left, right, dims=NN):
    return lax.dot_general(left, right, dims, preferred_element_type=F32)


def params():
    return pltpu.CompilerParams(vmem_limit_bytes=VMEM)


def like(shape, dtype):
    return jax.ShapeDtypeStruct(shape, dtype)


def in_place():
    return pl.BlockSpec(memory_space=pl.ANY)


def scalar():
    return pl.BlockSpec(memory_space=pltpu.SMEM)


def swap(value, axis, bit):
    size = lax.axis_size(axis)
    return lax.ppermute(value, axis, [(i, i ^ bit) for i in range(size)])


def bits_of(axis):
    bits = []
    bit = 1
    while bit < lax.axis_size(axis):
        bits.append(bit)
        bit *= 2
    return bits


def side_of(axis, bit):
    return (lax.axis_index(axis) // bit) % 2


def hold(value, *before):
    return lax.optimization_barrier((value,) + before)[0]


def add_low(left, right):
    return (left.astype(F32) + right.astype(F32)).astype(BF16)


def halve(part, axis, bit):
    side = side_of(axis, bit)
    both = part.reshape((2, part.shape[0] // 2) + part.shape[1:])
    got = swap(lax.dynamic_index_in_dim(both, 1 - side, 0, False), axis, bit)
    return add_low(lax.dynamic_index_in_dim(both, side, 0, False), got)


def widen(part, axis, bit):
    other = swap(part, axis, bit)
    high = side_of(axis, bit) == 1
    return jnp.concatenate([jnp.where(high, other, part), jnp.where(high, part, other)], axis=0)


def near_halves(part):
    for bit in bits_of("ctx"):
        part = halve(part, "ctx", bit)
    return part


def near_whole(part):
    for bit in reversed(bits_of("ctx")):
        part = widen(part, "ctx", bit)
    return part


def far_halves(part):
    for bit in bits_of("seq"):
        part = halve(part, "seq", bit)
    return part


def far_whole(part):
    for bit in reversed(bits_of("seq")):
        part = widen(part, "seq", bit)
    return part


def far_both(part):
    for bit in bits_of("seq"):
        part = add_low(part, swap(part, "seq", bit))
    return part


def spread(values):
    centred = values - jnp.mean(values, axis=-1, keepdims=True)
    scale = lax.rsqrt(jnp.mean(centred * centred, axis=-1, keepdims=True) + EPSILON)
    return centred * scale, scale


def spread_back(unit, scale, grad):
    along = jnp.mean(grad * unit, axis=-1, keepdims=True)
    return scale * (grad - jnp.mean(grad, axis=-1, keepdims=True) - unit * along)


def lay_rows(width, pieces):
    arrays = [piece[0] for piece in pieces]

    def body(*refs):
        first = 0
        for ref, (_, col) in zip(refs, pieces):
            refs[-1][first : first + ref.shape[0], :] = ref[:, col : col + width]
            first += ref.shape[0]

    total = sum(array.shape[0] for array in arrays)
    vmem = pl.BlockSpec(memory_space=pltpu.VMEM)
    return pl.pallas_call(
        body,
        in_specs=[vmem] * len(arrays),
        out_specs=vmem,
        out_shape=like((total, width), BF16),
        compiler_params=params(),
        cost_estimate=pl.CostEstimate(flops=0, transcendentals=0, bytes_accessed=4 * total * width),
        name="lay_rows",
    )(*arrays)


def project_body(me_ref, own_ref, other_ref, p0, p1, p2, p3, q_ref, k_ref, v_ref, turned_ref, w_ref, small_ref, few, sem):
    step = pl.program_id(0)
    width = own_ref.shape[1]
    shard = p0.shape[0]

    @pl.when(step == 0)
    def _():
        copies = []
        for r, pack in enumerate((p0, p1, p2, p3)):
            place = pl.multiple_of((me_ref[0] ^ r) * shard, shard)
            copies.append(
                pltpu.make_async_copy(pack.at[:, 0 : 3 * width], w_ref.at[pl.ds(place, shard), :], sem.at[2 * r])
            )
            copies.append(
                pltpu.make_async_copy(
                    pack.at[0:16, 3 * width : 3 * width + shard], few.at[:, pl.ds(place, shard)], sem.at[2 * r + 1]
                )
            )
        for copy in copies:
            copy.start()
        for copy in copies:
            copy.wait()
        small_ref[...] = few[...].astype(F32)

    tokens = jnp.where(step == 0, own_ref[...], other_ref[...]).astype(F32)
    unit, _ = spread(tokens)
    a1 = (unit * few[0:1, :].astype(F32)).astype(BF16)
    turned_ref[...] = a1.T

    @pl.when(step == 0)
    def _():
        q = product(a1, w_ref[:, 0:width]).astype(BF16)
        q_ref[...] = (q.astype(F32) * 0.125).astype(BF16)

    k_ref[...] = product(a1, w_ref[:, width : 2 * width]).astype(BF16)
    v_ref[...] = product(a1, w_ref[:, 2 * width : 3 * width]).astype(BF16)


def project(me, own, others, packs):
    rows, width = own.shape
    steps = 1 + others.shape[0] // rows
    whole = lambda i: (0, 0)
    return pl.pallas_call(
        project_body,
        grid=(steps,),
        in_specs=[
            scalar(),
            pl.BlockSpec((rows, width), whole),
            pl.BlockSpec((rows, width), lambda i: (jnp.maximum(i - 1, 0), 0)),
        ]
        + [in_place()] * 4,
        out_specs=[
            pl.BlockSpec((rows, width), whole),
            pl.BlockSpec((rows, width), lambda i: (i, 0)),
            pl.BlockSpec((rows, width), lambda i: (i, 0)),
            pl.BlockSpec((width, rows), lambda i: (0, i)),
            pl.BlockSpec((width, 3 * width), whole),
            pl.BlockSpec((16, width), whole),
        ],
        out_shape=[
            like((rows, width), BF16),
            like((rows * steps, width), BF16),
            like((rows * steps, width), BF16),
            like((width, rows * steps), BF16),
            like((width, 3 * width), BF16),
            like((16, width), F32),
        ],
        scratch_shapes=[pltpu.VMEM((16, width), BF16), pltpu.SemaphoreType.DMA((8,))],
        compiler_params=params(),
        cost_estimate=pl.CostEstimate(flops=6 * rows * steps * width * width, transcendentals=0, bytes_accessed=6000000),
        name="project",
    )(me, own, others, *packs)


def forward_body(rows, small_ref, q_ref, k_ref, v_ref, b_ref, c_ref, o_ref, m_ref, r1_ref, r2_ref, e1_ref, e2_ref):
    low_lanes = lax.broadcasted_iota(jnp.int32, (rows, 128), 1) < 64
    for start in range(0, q_ref.shape[0], rows):
        at = pl.ds(start, rows)
        mixed = []
        for side in range(2):
            slope = small_ref[3:4, side : side + 1]
            q_head = jnp.where(low_lanes == (side == 0), q_ref[at, :], 0).astype(BF16)
            raw = product(q_head, k_ref[...], NT)
            for table in (e1_ref, e2_ref):
                values = raw - slope * b_ref[at, :] if table is e1_ref else raw + c_ref[at, :]
                peak = jnp.max(values, axis=1, keepdims=True)
                shifted = jnp.exp(values - peak)
                total = jnp.sum(shifted, axis=1, keepdims=True)
                weights = shifted.astype(BF16)
                table[side, at, :] = weights
                mixed.append((product(weights, v_ref[...]), 1.0 / total))
        for slot, value_ref, recip_ref in ((0, o_ref, r1_ref), (1, m_ref, r2_ref)):
            recip = jnp.where(low_lanes, mixed[slot][1], mixed[2 + slot][1])
            recip_ref[at, :] = recip
            value_ref[at, :] = jnp.where(low_lanes, mixed[slot][0], mixed[2 + slot][0]) * recip


def attend_forward(small, q, k, v, bias, count):
    row_count, width = q.shape
    key_count = k.shape[0]
    pairs = width // 128
    step_rows = max(64, min(row_count, (512 * 1024) // key_count))
    rows = min(256, step_rows)
    elements = 2 * pairs * row_count * key_count
    own = lambda p, i: (i, p)
    return pl.pallas_call(
        functools.partial(forward_body, rows),
        grid=(pairs, row_count // step_rows),
        in_specs=[
            pl.BlockSpec((16, 128), lambda p, i: (0, p)),
            pl.BlockSpec((step_rows, 128), own),
            pl.BlockSpec((key_count, 128), lambda p, i: (0, p)),
            pl.BlockSpec((key_count, 128), lambda p, i: (0, p)),
            pl.BlockSpec((step_rows, key_count), lambda p, i: (i, 0)),
            pl.BlockSpec((step_rows, key_count), lambda p, i: (i, 0)),
        ],
        out_specs=[pl.BlockSpec((step_rows, 128), own)] * 4
        + [pl.BlockSpec((2, step_rows, key_count), lambda p, i: (p, i, 0))] * 2,
        out_shape=[like((row_count, width), F32)] * 4 + [like((2 * pairs, row_count, key_count), BF16)] * 2,
        compiler_params=params(),
        cost_estimate=pl.CostEstimate(
            flops=elements * 64 * 2 * 3, transcendentals=2 * elements, bytes_accessed=4 * elements
        ),
        name="attend_forward",
    )(small, q, k, v, bias, count)


def middle_body(
    me_ref, small_ref, tokens_ref, cot_ref, o_ref, m_ref, p0, p1, p2, p3,
    out_ref, gh1_ref, go_ref, gm_ref, gate_ref, g0, g1, g2, g3, h0, h1_ref, h2_ref, h3,
    w_out, w_memory, w_down, w_up, act, slope, gu, a2_turned, o_turned, m_turned, sem,
):
    rows, width = tokens_ref.shape
    shard = width // 4
    groups = w_down.shape[0] // width
    copies = []
    for r, pack in enumerate((p0, p1, p2, p3)):
        device = me_ref[0] ^ r
        place = pl.ds(pl.multiple_of(device * shard, shard), shard)
        down = pl.ds(pl.multiple_of(device * width, width), width)
        targets = [w_out.at[place], w_memory.at[place]] + [w_up.at[group, place] for group in range(groups)]
        pieces = [(pack.at[n * shard : (n + 1) * shard], target) for n, target in enumerate(targets)]
        pieces.append((pack.at[len(targets) * shard : len(targets) * shard + width], w_down.at[down]))
        copies.append([pltpu.make_async_copy(*piece, sem.at[r, n]) for n, piece in enumerate(pieces)])
    for part in zip(*copies):
        for copy in part:
            copy.start()
    gain = small_ref[1:2, :]
    gate_vec = small_ref[2:3, :]
    o_low = o_ref[...].astype(BF16)
    m_low = m_ref[...].astype(BF16)
    for copy in copies:
        copy[0].wait()
        copy[1].wait()
    h1 = tokens_ref[...].astype(F32) + product(o_low, w_out[...])
    mem = product(m_low, w_memory[...])
    o_turned[...] = o_low.T
    m_turned[...] = m_low.T
    unit, scale = spread(h1)
    a2 = (unit * gain).astype(BF16)
    a2_turned[...] = a2.T
    for copy in copies:
        for piece in copy[2:]:
            piece.wait()
    h2 = h1
    for group in range(groups):
        u = product(a2, w_up[group])
        square = u * u
        bent = jnp.tanh(CURVE * u * (1.0 + CUBIC * square))
        half = 0.5 * (1.0 + bent)
        active = (u * half).astype(BF16)
        slope[group] = half + 0.5 * u * (1.0 - bent * bent) * (CURVE * (1.0 + 3.0 * CUBIC * square))
        act[group] = active.T
        h2 = h2 + product(active, w_down[group * width : (group + 1) * width, :])
    gate = jax.nn.sigmoid(jnp.sum(h2 * gate_vec, axis=1, keepdims=True))
    apart = mem - h2
    out_ref[...] = (h2 + gate * apart).astype(BF16)
    c = cot_ref[...].astype(F32)
    grad_mem = (c * gate).astype(BF16)
    dz = jnp.sum(c * apart, axis=1, keepdims=True) * gate * (1.0 - gate)
    gh2 = c * (1.0 - gate) + dz * gate_vec
    gate_ref[...] = jnp.broadcast_to(jnp.sum(dz * h2, axis=0, keepdims=True), gate_ref.shape)
    gf = gh2.astype(BF16)
    gm_ref[...] = product(grad_mem, w_memory[...], NT).astype(BF16)
    ga2 = None
    for group in range(groups):
        back = product(gf, w_down[group * width : (group + 1) * width, :], NT)
        low = (back * slope[group]).astype(BF16)
        gu[group] = low
        more = product(low, w_up[group], NT)
        ga2 = more if ga2 is None else ga2 + more
    gh1 = gh2 + spread_back(unit, scale, ga2 * gain)
    gh1_ref[...] = gh1
    ga = gh1.astype(BF16)
    go_ref[...] = product(ga, w_out[...], NT).astype(BF16)
    for r, (grad_ref, up_ref) in enumerate(((g0, h0), (g1, h1_ref), (g2, h2_ref), (g3, h3))):
        device = me_ref[0] ^ r
        place = pl.ds(pl.multiple_of(device * shard, shard), shard)
        grad_ref[0:shard, :] = product(o_turned[place, :], ga).astype(BF16)
        grad_ref[shard : 2 * shard, :] = product(m_turned[place, :], grad_mem).astype(BF16)
        grad_ref[2 * shard : 2 * shard + width, :] = product(act[device], gf).astype(BF16)
        for group in range(groups):
            first = group * shard
            up_ref[first : first + shard, :] = product(a2_turned[place, :], gu[group]).astype(BF16)


def middle(me, small, tokens, cotangent, o, m, packs, groups):
    rows, width = tokens.shape
    shard = width // 4
    vmem = pl.BlockSpec(memory_space=pltpu.VMEM)
    square = lambda dtype: pltpu.VMEM((width, width), dtype)
    return pl.pallas_call(
        middle_body,
        in_specs=[scalar()] + [vmem] * 5 + [in_place()] * 4,
        out_specs=[vmem] * 13,
        out_shape=[
            like((rows, width), BF16),
            like((rows, width), F32),
            like((rows, width), BF16),
            like((rows, width), BF16),
            like((8, width), F32),
        ]
        + [like((2 * shard + width, width), BF16)] * 4
        + [like((groups * shard, width), BF16)] * 4,
        scratch_shapes=[
            square(BF16),
            square(BF16),
            pltpu.VMEM((groups * width, width), BF16),
            pltpu.VMEM((groups, width, width), BF16),
            pltpu.VMEM((groups, width, rows), BF16),
            pltpu.VMEM((groups, rows, width), F32),
            pltpu.VMEM((groups, rows, width), BF16),
            pltpu.VMEM((width, rows), BF16),
            pltpu.VMEM((width, rows), BF16),
            pltpu.VMEM((width, rows), BF16),
            pltpu.SemaphoreType.DMA((4, 3 + groups)),
        ],
        compiler_params=params(),
        cost_estimate=pl.CostEstimate(
            flops=2 * rows * width * width * 3 * 10, transcendentals=4 * rows * width, bytes_accessed=16000000
        ),
        name="middle",
    )(me, small, tokens, cotangent, o, m, *packs)


def backward_body(
    several, rows, q_ref, k_ref, v_ref, go_ref, gm_ref, o_ref, m_ref, r1_ref, r2_ref, b_ref, e1_ref, e2_ref,
    gq_ref, gk_ref, gv_ref, gs_ref,
):
    low_lanes = lax.broadcasted_iota(jnp.int32, (rows, 128), 1) < 64
    keys = k_ref[...]
    vals = v_ref[...]
    totals = [None, None]
    for start in range(0, q_ref.shape[0], rows):
        at = pl.ds(start, rows)
        g1 = (go_ref[at, :].astype(F32) * r1_ref[at, :]).astype(BF16)
        g2 = (gm_ref[at, :].astype(F32) * r2_ref[at, :]).astype(BF16)
        t1 = g1.astype(F32) * o_ref[at, :]
        t2 = g2.astype(F32) * m_ref[at, :]
        q_turned = q_ref[at, :].T
        g1_turned = g1.T
        g2_turned = g2.T
        grads = []
        for side in range(2):
            mine = low_lanes == (side == 0)
            d1 = jnp.sum(jnp.where(mine, t1, 0.0), axis=1, keepdims=True)
            d2 = jnp.sum(jnp.where(mine, t2, 0.0), axis=1, keepdims=True)
            e1 = e1_ref[side, at, :]
            e2 = e2_ref[side, at, :]
            p1 = product(jnp.where(mine, g1, 0).astype(BF16), vals, NT)
            ds1 = e1.astype(F32) * (p1 - d1)
            slope_term = jnp.sum(ds1 * b_ref[at, :], axis=0, keepdims=True)
            p2 = product(jnp.where(mine, g2, 0).astype(BF16), vals, NT)
            ds = (ds1 + e2.astype(F32) * (p2 - d2)).astype(BF16)
            grads.append(product(ds, keys))
            head = slice(64 * side, 64 * side + 64)
            gk = product(q_turned[head, :], ds)
            gv = product(g1_turned[head, :], e1) + product(g2_turned[head, :], e2)
            if start > 0:
                gk, gv, slope_term = (have + more for have, more in zip(totals[side], (gk, gv, slope_term)))
            totals[side] = (gk, gv, slope_term)
        gq = jnp.where(low_lanes, grads[0], grads[1]) * 0.125
        if not several:
            gq_ref[at, :] = gq.astype(gq_ref.dtype)
        else:
            gq_ref[at, :] = jnp.where(pl.program_id(1) == 0, gq, gq_ref[at, :] + gq)
    gk_ref[...] = jnp.concatenate([totals[0][0], totals[1][0]], axis=0).astype(BF16).T
    gv_ref[...] = jnp.concatenate([totals[0][1], totals[1][1]], axis=0).astype(BF16).T
    for side in range(2):
        term = totals[side][2]
        parts = term[:, 0:128]
        for first in range(128, term.shape[1], 128):
            parts = parts + term[:, first : first + 128]
        if not several:
            gs_ref[side : side + 1, :] = parts
        else:
            gs_ref[side : side + 1, :] = jnp.where(pl.program_id(1) == 0, parts, gs_ref[side : side + 1, :] + parts)


def attend_backward(q, k, v, go, gm, saved, bias, first, pairs):
    o, m, r1, r2, e1, e2 = saved
    row_count = q.shape[0]
    key_count = k.shape[0]
    step_keys = min(1024, key_count)
    several = key_count > step_keys
    elements = 2 * pairs * row_count * key_count
    wide = pl.BlockSpec((row_count, 128), lambda p, c: (0, p + first))
    near = pl.BlockSpec((step_keys, 128), lambda p, c: (c, p + first))
    table = pl.BlockSpec((2, row_count, step_keys), lambda p, c: (p + first, 0, c))
    own = pl.BlockSpec((step_keys, 128), lambda p, c: (c, p))
    return pl.pallas_call(
        functools.partial(backward_body, several, 256),
        grid=(pairs, key_count // step_keys),
        in_specs=[wide, near, near, wide, wide, wide, wide, wide, wide]
        + [pl.BlockSpec((row_count, step_keys), lambda p, c: (0, c)), table, table],
        out_specs=[
            pl.BlockSpec((row_count, 128), lambda p, c: (0, p)),
            own,
            own,
            pl.BlockSpec((None, 8, 128), lambda p, c: (p, 0, 0)),
        ],
        out_shape=[
            like((row_count, 128 * pairs), F32 if several else BF16),
            like((key_count, 128 * pairs), BF16),
            like((key_count, 128 * pairs), BF16),
            like((pairs, 8, 128), F32),
        ],
        compiler_params=params(),
        cost_estimate=pl.CostEstimate(flops=elements * 64 * 2 * 6, transcendentals=0, bytes_accessed=4 * elements),
        name="attend_backward",
    )(q, k, v, go, gm, o, m, r1, r2, bias, e1, e2)


def last_body(me_ref, turned_ref, gq_ref, gk_ref, gv_ref, w_ref, gs_ref, gate_ref, near_ref, own_ref, g0, g1, g2, g3):
    rows, width = gq_ref.shape
    shard = width // 4
    gq = gq_ref[...].astype(BF16)
    w_q = w_ref[:, 0:width]
    w_k = w_ref[:, width : 2 * width]
    w_v = w_ref[:, 2 * width : 3 * width]
    for first in range(rows, gk_ref.shape[0], rows):
        at = slice(first, first + rows)
        part = product(gk_ref[at, :], w_k, NT) + product(gv_ref[at, :], w_v, NT)
        near_ref[first - rows : first, :] = part.astype(BF16)
    own_ref[...] = product(gq, w_q, NT) + product(gk_ref[0:rows, :], w_k, NT) + product(gv_ref[0:rows, :], w_v, NT)
    lane = lax.broadcasted_iota(jnp.int32, (16, shard), 1)
    row = lax.broadcasted_iota(jnp.int32, (16, shard), 0)
    for r, grad_ref in enumerate((g0, g1, g2, g3)):
        device = me_ref[0] ^ r
        start = pl.multiple_of(device * shard, shard)
        a1 = turned_ref[pl.ds(start, shard), :]
        grad_ref[:, 0:width] = product(a1[:, 0:rows], gq).astype(BF16)
        grad_ref[:, width : 2 * width] = product(a1, gk_ref[...]).astype(BF16)
        grad_ref[:, 2 * width : 3 * width] = product(a1, gv_ref[...]).astype(BF16)
        sums = -jnp.sum(gs_ref[device, 0:2, :], axis=1, keepdims=True)
        block = jnp.where((row == 0) & (lane == 0), sums[0:1, :], 0.0)
        block = jnp.where((row == 0) & (lane == 1), sums[1:2, :], block)
        block = jnp.where(row == 1, gate_ref[0:1, pl.ds(start, shard)], block)
        grad_ref[:, 3 * width : 3 * width + shard] = jnp.zeros((shard, shard), BF16)
        grad_ref[0:16, 3 * width : 3 * width + shard] = block.astype(BF16)


def last(me, turned, gq, gk, gv, w, gs, gate):
    rows, width = gq.shape
    shard = width // 4
    vmem = pl.BlockSpec(memory_space=pltpu.VMEM)
    return pl.pallas_call(
        last_body,
        in_specs=[scalar()] + [vmem] * 7,
        out_specs=[vmem] * 6,
        out_shape=[like((gk.shape[0] - rows, width), BF16), like((rows, width), F32)]
        + [like((shard, 3 * width + shard), BF16)] * 4,
        compiler_params=params(),
        cost_estimate=pl.CostEstimate(
            flops=12 * gk.shape[0] * width * width, transcendentals=0, bytes_accessed=10000000
        ),
        name="last",
    )(me, turned, gq, gk, gv, w, gs, gate)


def finish_body(tokens_ref, small_ref, gh1_ref, own_ref, away_ref, out_ref):
    unit, scale = spread(tokens_ref[...].astype(F32))
    grad = (own_ref[...] + away_ref[...].astype(F32)) * small_ref[0:1, :]
    out_ref[...] = gh1_ref[...] + spread_back(unit, scale, grad)


def finish(tokens, small, gh1, own, away):
    vmem = pl.BlockSpec(memory_space=pltpu.VMEM)
    return pl.pallas_call(
        finish_body,
        in_specs=[vmem] * 5,
        out_specs=vmem,
        out_shape=like(gh1.shape, F32),
        compiler_params=params(),
        cost_estimate=pl.CostEstimate(flops=0, transcendentals=0, bytes_accessed=4000000),
        name="finish",
    )(tokens, small, gh1, own, away)


def on_device(
    tokens, cotangent, deal, memory_len, neighbours,
    w_qkv, w_out, w_up, w_down, w_memory, gain_attn, gain_ffn, gate_vec, slopes,
):
    _, row_count, width = tokens.shape
    tokens = tokens.reshape(row_count, width)
    cotangent = cotangent.reshape(row_count, width)
    neighbours = neighbours.reshape(row_count, -1)
    block_count = deal.shape[0]
    ctx_size = lax.axis_size("ctx")
    own_blocks = block_count // ctx_size
    block_len = row_count // own_blocks
    shard = gain_attn.shape[0]
    heads_here = slopes.shape[0]
    groups = w_up.shape[1] // width
    me = lax.axis_index("wt").astype(jnp.int32).reshape(1)

    short = jnp.concatenate(
        [gain_attn[None], gain_ffn[None], gate_vec[None], jnp.pad(slopes, (0, shard - heads_here))[None]], axis=0
    )
    pack = jnp.concatenate([w_qkv, jnp.pad(short, ((0, shard - 4), (0, 0)))], axis=1)
    pack_far = swap(pack, "wt", 2)
    others = swap(tokens, "ctx", 1)
    for bit in bits_of("ctx")[1:]:
        both = jnp.concatenate([tokens, others], axis=0)
        others = jnp.concatenate([others, swap(both, "ctx", bit)], axis=0)
    pack_near = swap(pack, "wt", 1)
    wide = lay_rows(width, [(w_out, 0), (w_memory, 0)] + [(w_up, width * g) for g in range(groups)] + [(w_down, 0)])

    offsets = jnp.arange(block_len, dtype=jnp.int32)
    owners = lax.axis_index("ctx") ^ jnp.arange(ctx_size, dtype=jnp.int32)
    slots = (owners[:, None] * own_blocks + jnp.arange(own_blocks, dtype=jnp.int32)[None, :]).reshape(-1)
    block_ids = jnp.arange(block_count, dtype=jnp.int32)
    slot_hot = (slots[:, None] == block_ids[None, :]).astype(jnp.int32)
    key_blocks = jnp.sum(slot_hot * deal[None, :], axis=1)
    key_pos = (key_blocks[:, None] * block_len + offsets[None, :]).reshape(-1)
    my_blocks = key_blocks[:own_blocks]
    row_pos = key_pos[:row_count]
    memory_hot = (my_blocks[:, None] == block_ids[None, :]).astype(jnp.int32)
    my_memory = jnp.sum(memory_hot * memory_len, axis=1)
    row_start = jnp.repeat(my_blocks * block_len, block_len)
    row_low = row_start - jnp.repeat(my_memory, block_len)
    distance = jnp.log1p(jnp.abs(row_pos[:, None] - key_pos[None, :]).astype(F32))
    visible = (key_pos[None, :] >= row_low[:, None]) & (key_pos[None, :] < (row_start + block_len)[:, None])
    bias = jnp.where(visible, distance, HIDDEN)
    hits = jnp.sum((neighbours[:, :, None] == key_pos[None, None, :]).astype(F32), axis=1)
    count = jnp.where(hits > 0.0, jnp.log(jnp.maximum(hits, 1.0)), ABSENT)

    pack_both = swap(hold(pack_far, bias, count), "wt", 1)
    wide_far = swap(hold(wide, pack_far), "wt", 2)
    wide_near = swap(wide, "wt", 1)

    q, k, v, turned, full_qkv, small = project(me, tokens, others, (pack, pack_near, pack_far, pack_both))
    saved = attend_forward(small, q, k, v, bias, count)
    wide_both = swap(hold(wide_far, saved[0]), "wt", 1)
    wides = (wide, wide_near, wide_far, wide_both)
    layer_out, gh1, go, gm, gate, g0, g1, g2, g3, h0, h1, h2, h3 = middle(
        me, small, tokens, cotangent, saved[0], saved[1], wides, groups
    )

    g_far = add_low(g2, swap(g3, "wt", 1))
    g_one = swap(g1, "wt", 1)
    g_got = swap(g_far, "wt", 2)
    gq, gk, gv, gs = attend_backward(q, k, v, hold(go, g_far), gm, saved, bias, 0, width // 128)
    g_sum = add_low(add_low(g0, g_one), g_got)
    h1, h3 = (hold(value, gq) for value in (h1, h3))
    h_far = add_low(h2, swap(h3, "wt", 1))
    h_one = swap(h1, "wt", 1)
    h_got = swap(h_far, "wt", 2)
    near, own, q0, q1, q2, q3 = last(me, turned, hold(gq, g_got), gk, gv, full_qkv, gs, gate)
    h_sum = add_low(add_low(h0, h_one), h_got)
    q_three = swap(q3, "wt", 1)
    q_one = swap(q1, "wt", 1)
    for bit in reversed(bits_of("ctx")[1:]):
        both = jnp.concatenate([own.astype(BF16), near], axis=0)
        fold = bit * row_count
        folded = both[:fold].astype(F32) + swap(both[fold:], "ctx", bit).astype(F32)
        own, near = folded[:row_count], folded[row_count:].astype(BF16)
    away = swap(near, "ctx", 1)
    q_far = swap(add_low(q2, q_three), "wt", 2)
    q_sum = add_low(add_low(q0, q_one), q_far)
    q_sum = near_whole(far_both(near_halves(q_sum)))
    g_sum = near_whole(far_whole(far_halves(near_halves(g_sum))))
    h_sum = near_whole(far_whole(far_halves(near_halves(h_sum))))
    grad_tokens = finish(tokens, small, gh1, own, away)

    t_qkv = q_sum[:, : 3 * width].astype(F32)
    t_slopes = q_sum[0, 3 * width : 3 * width + heads_here].astype(F32)
    t_gate = q_sum[1, 3 * width : 3 * width + shard].astype(F32)
    t_out = g_sum[:shard].astype(F32)
    t_memory = g_sum[shard : 2 * shard].astype(F32)
    t_down = g_sum[2 * shard : 2 * shard + width].astype(F32)
    t_up = jnp.concatenate([h_sum[shard * g : shard * (g + 1)] for g in range(groups)], axis=1).astype(F32)
    t_gain_one = jnp.sum(t_qkv * w_qkv.astype(F32), axis=1) / gain_attn.astype(F32)
    t_gain_two = jnp.sum(t_up * w_up.astype(F32), axis=1) / gain_ffn.astype(F32)
    return (
        layer_out[None], grad_tokens[None], t_qkv, t_out, t_up, t_down, t_memory,
        t_gain_one, t_gain_two, t_gate, t_slopes,
    )


def solution(mesh):
    rows = P(("seq", "wt"), "ctx", None)
    weight = P("wt", None)
    vector = P("wt")
    return jax.shard_map(
        on_device,
        mesh=mesh,
        in_specs=(rows, rows, P(), P(("seq", "wt"), None), rows) + (weight,) * 5 + (vector,) * 4,
        out_specs=(rows, rows) + (weight,) * 5 + (vector,) * 4,
        check_vma=False,
    )
```

```python
import functools
import math
import jax
import jax.numpy as jnp
from jax import lax
from jax.experimental import pallas as pl
from jax.experimental.pallas import tpu as pltpu
from jax.sharding import PartitionSpec as P

EPSILON = 1e-05
F32 = jnp.float32
BF16 = jnp.bfloat16
NT = (((1,), (1,)), ((), ()))
NN = (((1,), (0,)), ((), ()))
HIDDEN = 1e12
ABSENT = -1e30
VMEM = 56 * 1024 * 1024
CURVE = math.sqrt(2.0 / math.pi)
CUBIC = 0.044715


def product(left, right, dims=NN):
    return lax.dot_general(left, right, dims, preferred_element_type=F32)


def params():
    return pltpu.CompilerParams(vmem_limit_bytes=VMEM)


def like(shape, dtype):
    return jax.ShapeDtypeStruct(shape, dtype)


def in_place():
    return pl.BlockSpec(memory_space=pl.ANY)


def scalar():
    return pl.BlockSpec(memory_space=pltpu.SMEM)


def swap(value, axis, bit):
    size = lax.axis_size(axis)
    return lax.ppermute(value, axis, [(i, i ^ bit) for i in range(size)])


def bits_of(axis):
    bits = []
    bit = 1
    while bit < lax.axis_size(axis):
        bits.append(bit)
        bit *= 2
    return bits


def side_of(axis, bit):
    return (lax.axis_index(axis) // bit) % 2


def hold(value, *before):
    return lax.optimization_barrier((value,) + before)[0]


class Order:
    def __init__(self):
        self.before = ()

    def arrive(self, *values):
        held = lax.optimization_barrier(values + self.before)[: len(values)]
        self.before = held[:1]
        return held if len(held) > 1 else held[0]


def send_half(part, axis, bit):
    side = side_of(axis, bit)
    both = part.reshape((2, part.shape[0] // 2) + part.shape[1:])
    got = swap(lax.dynamic_index_in_dim(both, 1 - side, 0, False), axis, bit)
    return lax.dynamic_index_in_dim(both, side, 0, False), got


def place_half(part, other, axis, bit):
    high = side_of(axis, bit) == 1
    return jnp.concatenate([jnp.where(high, other, part), jnp.where(high, part, other)], axis=0)


def add_all(own, got):
    total = own.astype(F32)
    for value in got:
        total = total + value.astype(F32)
    return total.astype(BF16)


def add_low(left, right):
    return (left.astype(F32) + right.astype(F32)).astype(BF16)


def halve(part, axis, bit):
    side = side_of(axis, bit)
    both = part.reshape((2, part.shape[0] // 2) + part.shape[1:])
    got = swap(lax.dynamic_index_in_dim(both, 1 - side, 0, False), axis, bit)
    return add_low(lax.dynamic_index_in_dim(both, side, 0, False), got)


def widen(part, axis, bit):
    other = swap(part, axis, bit)
    high = side_of(axis, bit) == 1
    return jnp.concatenate([jnp.where(high, other, part), jnp.where(high, part, other)], axis=0)


def near_halves(part):
    for bit in bits_of("ctx"):
        part = halve(part, "ctx", bit)
    return part


def near_whole(part):
    for bit in reversed(bits_of("ctx")):
        part = widen(part, "ctx", bit)
    return part


def far_halves(part):
    for bit in bits_of("seq"):
        part = halve(part, "seq", bit)
    return part


def far_whole(part):
    for bit in reversed(bits_of("seq")):
        part = widen(part, "seq", bit)
    return part


def far_both(part):
    for bit in bits_of("seq"):
        part = add_low(part, swap(part, "seq", bit))
    return part


def spread(values):
    centred = values - jnp.mean(values, axis=-1, keepdims=True)
    scale = lax.rsqrt(jnp.mean(centred * centred, axis=-1, keepdims=True) + EPSILON)
    return centred * scale, scale


def spread_back(unit, scale, grad):
    along = jnp.mean(grad * unit, axis=-1, keepdims=True)
    return scale * (grad - jnp.mean(grad, axis=-1, keepdims=True) - unit * along)


def lay_rows(width, pieces):
    arrays = [piece[0] for piece in pieces]

    def body(*refs):
        first = 0
        for ref, (_, col) in zip(refs, pieces):
            refs[-1][first : first + ref.shape[0], :] = ref[:, col : col + width]
            first += ref.shape[0]

    total = sum(array.shape[0] for array in arrays)
    vmem = pl.BlockSpec(memory_space=pltpu.VMEM)
    return pl.pallas_call(
        body,
        in_specs=[vmem] * len(arrays),
        out_specs=vmem,
        out_shape=like((total, width), BF16),
        compiler_params=params(),
        cost_estimate=pl.CostEstimate(flops=0, transcendentals=0, bytes_accessed=4 * total * width),
        name="lay_rows",
    )(*arrays)


def project_body(me_ref, own_ref, other_ref, p0, p1, p2, p3, q_ref, k_ref, v_ref, turned_ref, w_ref, small_ref, few, sem):
    step = pl.program_id(0)
    width = own_ref.shape[1]
    shard = p0.shape[0]

    @pl.when(step == 0)
    def _():
        copies = []
        for r, pack in enumerate((p0, p1, p2, p3)):
            place = pl.multiple_of((me_ref[0] ^ r) * shard, shard)
            copies.append(
                pltpu.make_async_copy(pack.at[:, 0 : 3 * width], w_ref.at[pl.ds(place, shard), :], sem.at[2 * r])
            )
            copies.append(
                pltpu.make_async_copy(
                    pack.at[0:16, 3 * width : 3 * width + shard], few.at[:, pl.ds(place, shard)], sem.at[2 * r + 1]
                )
            )
        for copy in copies:
            copy.start()
        for copy in copies:
            copy.wait()
        small_ref[...] = few[...].astype(F32)

    tokens = jnp.where(step == 0, own_ref[...], other_ref[...]).astype(F32)
    unit, _ = spread(tokens)
    a1 = (unit * few[0:1, :].astype(F32)).astype(BF16)
    turned_ref[...] = a1.T

    @pl.when(step == 0)
    def _():
        q = product(a1, w_ref[:, 0:width]).astype(BF16)
        q_ref[...] = (q.astype(F32) * 0.125).astype(BF16)

    k_ref[...] = product(a1, w_ref[:, width : 2 * width]).astype(BF16)
    v_ref[...] = product(a1, w_ref[:, 2 * width : 3 * width]).astype(BF16)


def project(me, own, others, packs):
    rows, width = own.shape
    steps = 1 + others.shape[0] // rows
    whole = lambda i: (0, 0)
    return pl.pallas_call(
        project_body,
        grid=(steps,),
        in_specs=[
            scalar(),
            pl.BlockSpec((rows, width), whole),
            pl.BlockSpec((rows, width), lambda i: (jnp.maximum(i - 1, 0), 0)),
        ]
        + [in_place()] * 4,
        out_specs=[
            pl.BlockSpec((rows, width), whole),
            pl.BlockSpec((rows, width), lambda i: (i, 0)),
            pl.BlockSpec((rows, width), lambda i: (i, 0)),
            pl.BlockSpec((width, rows), lambda i: (0, i)),
            pl.BlockSpec((width, 3 * width), whole),
            pl.BlockSpec((16, width), whole),
        ],
        out_shape=[
            like((rows, width), BF16),
            like((rows * steps, width), BF16),
            like((rows * steps, width), BF16),
            like((width, rows * steps), BF16),
            like((width, 3 * width), BF16),
            like((16, width), F32),
        ],
        scratch_shapes=[pltpu.VMEM((16, width), BF16), pltpu.SemaphoreType.DMA((8,))],
        compiler_params=params(),
        cost_estimate=pl.CostEstimate(flops=6 * rows * steps * width * width, transcendentals=0, bytes_accessed=6000000),
        name="project",
    )(me, own, others, *packs)


def forward_body(rows, small_ref, q_ref, k_ref, v_ref, b_ref, c_ref, o_ref, m_ref, r1_ref, r2_ref, e1_ref, e2_ref):
    low_lanes = lax.broadcasted_iota(jnp.int32, (rows, 128), 1) < 64
    for start in range(0, q_ref.shape[0], rows):
        at = pl.ds(start, rows)
        mixed = []
        for side in range(2):
            slope = small_ref[3:4, side : side + 1]
            q_head = jnp.where(low_lanes == (side == 0), q_ref[at, :], 0).astype(BF16)
            raw = product(q_head, k_ref[...], NT)
            for table in (e1_ref, e2_ref):
                values = raw - slope * b_ref[at, :] if table is e1_ref else raw + c_ref[at, :]
                peak = jnp.max(values, axis=1, keepdims=True)
                shifted = jnp.exp(values - peak)
                total = jnp.sum(shifted, axis=1, keepdims=True)
                weights = shifted.astype(BF16)
                table[side, at, :] = weights
                mixed.append((product(weights, v_ref[...]), 1.0 / total))
        for slot, value_ref, recip_ref in ((0, o_ref, r1_ref), (1, m_ref, r2_ref)):
            recip = jnp.where(low_lanes, mixed[slot][1], mixed[2 + slot][1])
            recip_ref[at, :] = recip
            value_ref[at, :] = jnp.where(low_lanes, mixed[slot][0], mixed[2 + slot][0]) * recip


def attend_forward(small, q, k, v, bias, count):
    row_count, width = q.shape
    key_count = k.shape[0]
    pairs = width // 128
    step_rows = max(64, min(row_count, (512 * 1024) // key_count))
    rows = min(256, step_rows)
    elements = 2 * pairs * row_count * key_count
    own = lambda p, i: (i, p)
    return pl.pallas_call(
        functools.partial(forward_body, rows),
        grid=(pairs, row_count // step_rows),
        in_specs=[
            pl.BlockSpec((16, 128), lambda p, i: (0, p)),
            pl.BlockSpec((step_rows, 128), own),
            pl.BlockSpec((key_count, 128), lambda p, i: (0, p)),
            pl.BlockSpec((key_count, 128), lambda p, i: (0, p)),
            pl.BlockSpec((step_rows, key_count), lambda p, i: (i, 0)),
            pl.BlockSpec((step_rows, key_count), lambda p, i: (i, 0)),
        ],
        out_specs=[pl.BlockSpec((step_rows, 128), own)] * 4
        + [pl.BlockSpec((2, step_rows, key_count), lambda p, i: (p, i, 0))] * 2,
        out_shape=[like((row_count, width), F32)] * 4 + [like((2 * pairs, row_count, key_count), BF16)] * 2,
        compiler_params=params(),
        cost_estimate=pl.CostEstimate(
            flops=elements * 64 * 2 * 3, transcendentals=2 * elements, bytes_accessed=4 * elements
        ),
        name="attend_forward",
    )(small, q, k, v, bias, count)


def middle_body(
    slices, me_ref, small_ref, tokens_ref, cot_ref, o_ref, m_ref, p0, p1, p2, p3,
    out_ref, gh1_ref, go_ref, gm_ref, gate_ref, g0, g1, g2, g3, h0, h1_ref, h2_ref, h3,
    w_out, w_memory, w_down, w_up, act, slope, gu, a2_turned, o_turned, m_turned, sem,
):
    rows, width = tokens_ref.shape
    shard = width // 4
    groups = w_down.shape[0] // width
    copies = []
    for r, pack in enumerate((p0, p1, p2, p3)):
        device = me_ref[0] ^ r
        place = pl.ds(pl.multiple_of(device * shard, shard), shard)
        down = pl.ds(pl.multiple_of(device * width, width), width)
        targets = [w_out.at[place], w_memory.at[place]] + [w_up.at[group, place] for group in range(groups)]
        pieces = [(pack.at[n * shard : (n + 1) * shard], target) for n, target in enumerate(targets)]
        pieces.append((pack.at[len(targets) * shard : len(targets) * shard + width], w_down.at[down]))
        copies.append([pltpu.make_async_copy(*piece, sem.at[r, n]) for n, piece in enumerate(pieces)])
    for part in zip(*copies):
        for copy in part:
            copy.start()
    gain = small_ref[1:2, :]
    gate_vec = small_ref[2:3, :]
    o_low = o_ref[...].astype(BF16)
    m_low = m_ref[...].astype(BF16)
    for copy in copies:
        copy[0].wait()
        copy[1].wait()
    h1 = tokens_ref[...].astype(F32) + product(o_low, w_out[...])
    mem = product(m_low, w_memory[...])
    o_turned[...] = o_low.T
    m_turned[...] = m_low.T
    unit, scale = spread(h1)
    a2 = (unit * gain).astype(BF16)
    a2_turned[...] = a2.T
    for copy in copies:
        for piece in copy[2:]:
            piece.wait()
    h2 = h1
    for group in range(groups):
        u = product(a2, w_up[group])
        square = u * u
        bent = jnp.tanh(CURVE * u * (1.0 + CUBIC * square))
        half = 0.5 * (1.0 + bent)
        active = (u * half).astype(BF16)
        slope[group] = half + 0.5 * u * (1.0 - bent * bent) * (CURVE * (1.0 + 3.0 * CUBIC * square))
        act[group] = active.T
        h2 = h2 + product(active, w_down[group * width : (group + 1) * width, :])
    gate = jax.nn.sigmoid(jnp.sum(h2 * gate_vec, axis=1, keepdims=True))
    apart = mem - h2
    out_ref[...] = (h2 + gate * apart).astype(BF16)
    c = cot_ref[...].astype(F32)
    grad_mem = (c * gate).astype(BF16)
    dz = jnp.sum(c * apart, axis=1, keepdims=True) * gate * (1.0 - gate)
    gh2 = c * (1.0 - gate) + dz * gate_vec
    gate_ref[...] = jnp.broadcast_to(jnp.sum(dz * h2, axis=0, keepdims=True), gate_ref.shape)
    gf = gh2.astype(BF16)
    gm_ref[...] = product(grad_mem, w_memory[...], NT).astype(BF16)
    ga2 = None
    for group in range(groups):
        back = product(gf, w_down[group * width : (group + 1) * width, :], NT)
        low = (back * slope[group]).astype(BF16)
        gu[group] = low
        more = product(low, w_up[group], NT)
        ga2 = more if ga2 is None else ga2 + more
    gh1 = gh2 + spread_back(unit, scale, ga2 * gain)
    gh1_ref[...] = gh1
    ga = gh1.astype(BF16)
    go_ref[...] = product(ga, w_out[...], NT).astype(BF16)
    for r, (grad_ref, up_ref) in enumerate(((g0, h0), (g1, h1_ref), (g2, h2_ref), (g3, h3))):
        device = me_ref[0] ^ r
        place = pl.ds(pl.multiple_of(device * shard, shard), shard)
        parts = [product(o_turned[place, :], ga), product(m_turned[place, :], grad_mem), product(act[device], gf)]
        lay_slices(grad_ref, slices, [part.astype(BF16) for part in parts])
        parts = [product(a2_turned[place, :], gu[group]) for group in range(groups)]
        lay_slices(up_ref, slices, [part.astype(BF16) for part in parts])


def lay_slices(target, slices, parts):
    first = 0
    for n in range(slices):
        for part in parts:
            height = part.shape[0] // slices
            target[first : first + height, :] = part[n * height : (n + 1) * height, :]
            first += height


def middle(slices, me, small, tokens, cotangent, o, m, packs, groups):
    rows, width = tokens.shape
    shard = width // 4
    vmem = pl.BlockSpec(memory_space=pltpu.VMEM)
    square = lambda dtype: pltpu.VMEM((width, width), dtype)
    return pl.pallas_call(
        functools.partial(middle_body, slices),
        in_specs=[scalar()] + [vmem] * 5 + [in_place()] * 4,
        out_specs=[vmem] * 13,
        out_shape=[
            like((rows, width), BF16),
            like((rows, width), F32),
            like((rows, width), BF16),
            like((rows, width), BF16),
            like((8, width), F32),
        ]
        + [like((2 * shard + width, width), BF16)] * 4
        + [like((groups * shard, width), BF16)] * 4,
        scratch_shapes=[
            square(BF16),
            square(BF16),
            pltpu.VMEM((groups * width, width), BF16),
            pltpu.VMEM((groups, width, width), BF16),
            pltpu.VMEM((groups, width, rows), BF16),
            pltpu.VMEM((groups, rows, width), F32),
            pltpu.VMEM((groups, rows, width), BF16),
            pltpu.VMEM((width, rows), BF16),
            pltpu.VMEM((width, rows), BF16),
            pltpu.VMEM((width, rows), BF16),
            pltpu.SemaphoreType.DMA((4, 3 + groups)),
        ],
        compiler_params=params(),
        cost_estimate=pl.CostEstimate(
            flops=2 * rows * width * width * 3 * 10, transcendentals=4 * rows * width, bytes_accessed=16000000
        ),
        name="middle",
    )(me, small, tokens, cotangent, o, m, *packs)


def backward_body(
    several, rows, q_ref, k_ref, v_ref, go_ref, gm_ref, o_ref, m_ref, r1_ref, r2_ref, b_ref, e1_ref, e2_ref,
    gq_ref, gk_ref, gv_ref, gs_ref,
):
    low_lanes = lax.broadcasted_iota(jnp.int32, (rows, 128), 1) < 64
    keys = k_ref[...]
    vals = v_ref[...]
    totals = [None, None]
    for start in range(0, q_ref.shape[0], rows):
        at = pl.ds(start, rows)
        g1 = (go_ref[at, :].astype(F32) * r1_ref[at, :]).astype(BF16)
        g2 = (gm_ref[at, :].astype(F32) * r2_ref[at, :]).astype(BF16)
        t1 = g1.astype(F32) * o_ref[at, :]
        t2 = g2.astype(F32) * m_ref[at, :]
        q_turned = q_ref[at, :].T
        g1_turned = g1.T
        g2_turned = g2.T
        grads = []
        for side in range(2):
            mine = low_lanes == (side == 0)
            d1 = jnp.sum(jnp.where(mine, t1, 0.0), axis=1, keepdims=True)
            d2 = jnp.sum(jnp.where(mine, t2, 0.0), axis=1, keepdims=True)
            e1 = e1_ref[side, at, :]
            e2 = e2_ref[side, at, :]
            p1 = product(jnp.where(mine, g1, 0).astype(BF16), vals, NT)
            ds1 = e1.astype(F32) * (p1 - d1)
            slope_term = jnp.sum(ds1 * b_ref[at, :], axis=0, keepdims=True)
            p2 = product(jnp.where(mine, g2, 0).astype(BF16), vals, NT)
            ds = (ds1 + e2.astype(F32) * (p2 - d2)).astype(BF16)
            grads.append(product(ds, keys))
            head = slice(64 * side, 64 * side + 64)
            gk = product(q_turned[head, :], ds)
            gv = product(g1_turned[head, :], e1) + product(g2_turned[head, :], e2)
            if start > 0:
                gk, gv, slope_term = (have + more for have, more in zip(totals[side], (gk, gv, slope_term)))
            totals[side] = (gk, gv, slope_term)
        gq = jnp.where(low_lanes, grads[0], grads[1]) * 0.125
        if not several:
            gq_ref[at, :] = gq.astype(gq_ref.dtype)
        else:
            gq_ref[at, :] = jnp.where(pl.program_id(1) == 0, gq, gq_ref[at, :] + gq)
    gk_ref[...] = jnp.concatenate([totals[0][0], totals[1][0]], axis=0).astype(BF16).T
    gv_ref[...] = jnp.concatenate([totals[0][1], totals[1][1]], axis=0).astype(BF16).T
    for side in range(2):
        term = totals[side][2]
        parts = term[:, 0:128]
        for first in range(128, term.shape[1], 128):
            parts = parts + term[:, first : first + 128]
        if not several:
            gs_ref[side : side + 1, :] = parts
        else:
            gs_ref[side : side + 1, :] = jnp.where(pl.program_id(1) == 0, parts, gs_ref[side : side + 1, :] + parts)


def attend_backward(q, k, v, go, gm, saved, bias, first, pairs):
    o, m, r1, r2, e1, e2 = saved
    row_count = q.shape[0]
    key_count = k.shape[0]
    step_keys = min(1024, key_count)
    several = key_count > step_keys
    elements = 2 * pairs * row_count * key_count
    wide = pl.BlockSpec((row_count, 128), lambda p, c: (0, p + first))
    near = pl.BlockSpec((step_keys, 128), lambda p, c: (c, p + first))
    table = pl.BlockSpec((2, row_count, step_keys), lambda p, c: (p + first, 0, c))
    own = pl.BlockSpec((step_keys, 128), lambda p, c: (c, p))
    return pl.pallas_call(
        functools.partial(backward_body, several, 256),
        grid=(pairs, key_count // step_keys),
        in_specs=[wide, near, near, wide, wide, wide, wide, wide, wide]
        + [pl.BlockSpec((row_count, step_keys), lambda p, c: (0, c)), table, table],
        out_specs=[
            pl.BlockSpec((row_count, 128), lambda p, c: (0, p)),
            own,
            own,
            pl.BlockSpec((None, 8, 128), lambda p, c: (p, 0, 0)),
        ],
        out_shape=[
            like((row_count, 128 * pairs), F32 if several else BF16),
            like((key_count, 128 * pairs), BF16),
            like((key_count, 128 * pairs), BF16),
            like((pairs, 8, 128), F32),
        ],
        compiler_params=params(),
        cost_estimate=pl.CostEstimate(flops=elements * 64 * 2 * 6, transcendentals=0, bytes_accessed=4 * elements),
        name="attend_backward",
    )(q, k, v, go, gm, o, m, r1, r2, bias, e1, e2)


def weights_body(me_ref, turned_ref, gq_ref, gk_ref, gv_ref, gs_ref, gate_ref, *grad_refs):
    rows, width = gq_ref.shape
    shard = width // 4
    lane = lax.broadcasted_iota(jnp.int32, (16, shard), 1)
    row = lax.broadcasted_iota(jnp.int32, (16, shard), 0)
    for r in range(4):
        grad_ref = grad_refs[r]
        device = me_ref[0] ^ r
        start = pl.multiple_of(device * shard, shard)
        a1 = turned_ref[pl.ds(start, shard), :]
        grad_ref[:, 0:width] = product(a1[:, 0:rows], gq_ref[...].astype(BF16)).astype(BF16)
        grad_ref[:, width : 2 * width] = product(a1, gk_ref[...]).astype(BF16)
        grad_ref[:, 2 * width : 3 * width] = product(a1, gv_ref[...]).astype(BF16)
        sums = -jnp.sum(gs_ref[device, 0:2, :], axis=1, keepdims=True)
        block = jnp.where((row == 0) & (lane == 0), sums[0:1, :], 0.0)
        block = jnp.where((row == 0) & (lane == 1), sums[1:2, :], block)
        block = jnp.where(row == 1, gate_ref[0:1, pl.ds(start, shard)], block)
        grad_ref[:, 3 * width : 3 * width + shard] = jnp.zeros((shard, shard), BF16)
        grad_ref[0:16, 3 * width : 3 * width + shard] = block.astype(BF16)


def weight_grads(me, turned, gq, gk, gv, gs, gate):
    rows, width = gq.shape
    shard = width // 4
    vmem = pl.BlockSpec(memory_space=pltpu.VMEM)
    return pl.pallas_call(
        weights_body,
        in_specs=[scalar()] + [vmem] * 6,
        out_specs=[vmem] * 4,
        out_shape=[like((shard, 3 * width + shard), BF16)] * 4,
        compiler_params=params(),
        cost_estimate=pl.CostEstimate(
            flops=6 * gk.shape[0] * width * width, transcendentals=0, bytes_accessed=6000000
        ),
        name="weight_grads",
    )(me, turned, gq, gk, gv, gs, gate)


def rows_body(gq_ref, gk_ref, gv_ref, w_ref, near_ref, own_ref):
    rows, width = gq_ref.shape
    w_k = w_ref[:, width : 2 * width]
    w_v = w_ref[:, 2 * width : 3 * width]
    for first in range(rows, gk_ref.shape[0], rows):
        at = slice(first, first + rows)
        part = product(gk_ref[at, :], w_k, NT) + product(gv_ref[at, :], w_v, NT)
        near_ref[first - rows : first, :] = part.astype(BF16)
    own = product(gq_ref[...].astype(BF16), w_ref[:, 0:width], NT)
    own_ref[...] = own + product(gk_ref[0:rows, :], w_k, NT) + product(gv_ref[0:rows, :], w_v, NT)


def row_grads(gq, gk, gv, w):
    rows, width = gq.shape
    vmem = pl.BlockSpec(memory_space=pltpu.VMEM)
    return pl.pallas_call(
        rows_body,
        in_specs=[vmem] * 4,
        out_specs=[vmem] * 2,
        out_shape=[like((gk.shape[0] - rows, width), BF16), like((rows, width), F32)],
        compiler_params=params(),
        cost_estimate=pl.CostEstimate(
            flops=6 * gk.shape[0] * width * width, transcendentals=0, bytes_accessed=6000000
        ),
        name="row_grads",
    )(gq, gk, gv, w)


def row_sums(table, weight_ref, gain_ref):
    ones = jnp.ones((8, table.shape[1]), F32)
    sums = lax.dot_general(
        ones, table * weight_ref[...].astype(F32), NT, precision=lax.Precision.HIGHEST, preferred_element_type=F32
    )
    return sums[0:1, :] / gain_ref[...].astype(F32)


def assemble_body(
    near_ref, far_ref, own_a, own_b, other_a, other_b, up_w_ref, gain_ref, out_ref, memory_ref, down_ref, up_ref, sum_ref
):
    width = out_ref.shape[1]
    groups = up_ref.shape[1] // width
    short = out_ref.shape[0] // 8
    tall = down_ref.shape[0] // 8
    size = own_a.shape[0] // 2
    for n, part_ref in enumerate((own_a, own_b, other_a, other_b)):
        side = near_ref[0] if n < 2 else 1 - near_ref[0]
        pair = far_ref[0] if n % 2 == 0 else 1 - far_ref[0]
        for p in range(2):
            place = 4 * side + 2 * pair + p
            at = pl.ds(pl.multiple_of(place * short, short), short)
            piece = part_ref[p * size : (p + 1) * size, :].astype(F32)
            out_ref[at, :] = piece[0:short, :]
            memory_ref[at, :] = piece[short : 2 * short, :]
            down_ref[pl.ds(pl.multiple_of(place * tall, tall), tall), :] = piece[2 * short : 2 * short + tall, :]
            for group in range(groups):
                first = 2 * short + tall + group * short
                up_ref[at, group * width : (group + 1) * width] = piece[first : first + short, :]
    sum_ref[...] = row_sums(up_ref[...], up_w_ref, gain_ref)


def assemble(near, far, parts, w_up, gain):
    width = parts[0].shape[1]
    shard, columns = w_up.shape
    vmem = pl.BlockSpec(memory_space=pltpu.VMEM)
    return pl.pallas_call(
        assemble_body,
        in_specs=[scalar(), scalar()] + [vmem] * 6,
        out_specs=[vmem] * 5,
        out_shape=[like((shard, width), F32)] * 2
        + [like((width, width), F32), like((shard, columns), F32), like((1, shard), F32)],
        compiler_params=params(),
        cost_estimate=pl.CostEstimate(flops=0, transcendentals=0, bytes_accessed=4000000),
        name="assemble",
    )(near, far, *parts, w_up, gain[None])


def close_body(near_ref, own_ref, other_ref, w_ref, gain_ref, qkv_ref, gain_sum_ref, gate_ref, slope_ref):
    half = own_ref.shape[0]
    wide = qkv_ref.shape[1]
    for n, part_ref in enumerate((own_ref, other_ref)):
        side = near_ref[0] if n == 0 else 1 - near_ref[0]
        qkv_ref[pl.ds(pl.multiple_of(side * half, half), half), :] = part_ref[:, 0:wide].astype(F32)
    first = jnp.where(near_ref[0] == 0, own_ref[0:16, wide:].astype(F32), other_ref[0:16, wide:].astype(F32))
    slope_ref[...] = first[0:1, 0 : slope_ref.shape[1]]
    gate_ref[...] = first[1:2, :]
    gain_sum_ref[...] = row_sums(qkv_ref[...], w_ref, gain_ref)


def close(near, own, other, w_qkv, gain, heads):
    shard, wide = w_qkv.shape
    vmem = pl.BlockSpec(memory_space=pltpu.VMEM)
    return pl.pallas_call(
        close_body,
        in_specs=[scalar()] + [vmem] * 4,
        out_specs=[vmem] * 4,
        out_shape=[like((shard, wide), F32), like((1, shard), F32), like((1, shard), F32), like((1, heads), F32)],
        compiler_params=params(),
        cost_estimate=pl.CostEstimate(flops=0, transcendentals=0, bytes_accessed=2000000),
        name="close",
    )(near, own, other, w_qkv, gain[None])


def finish_body(tokens_ref, small_ref, gh1_ref, own_ref, away_ref, out_ref):
    unit, scale = spread(tokens_ref[...].astype(F32))
    grad = (own_ref[...] + away_ref[...].astype(F32)) * small_ref[0:1, :]
    out_ref[...] = gh1_ref[...] + spread_back(unit, scale, grad)


def finish(tokens, small, gh1, own, away):
    vmem = pl.BlockSpec(memory_space=pltpu.VMEM)
    return pl.pallas_call(
        finish_body,
        in_specs=[vmem] * 5,
        out_specs=vmem,
        out_shape=like(gh1.shape, F32),
        compiler_params=params(),
        cost_estimate=pl.CostEstimate(flops=0, transcendentals=0, bytes_accessed=4000000),
        name="finish",
    )(tokens, small, gh1, own, away)


def on_device(
    tokens, cotangent, deal, memory_len, neighbours,
    w_qkv, w_out, w_up, w_down, w_memory, gain_attn, gain_ffn, gate_vec, slopes,
):
    _, row_count, width = tokens.shape
    tokens = tokens.reshape(row_count, width)
    cotangent = cotangent.reshape(row_count, width)
    neighbours = neighbours.reshape(row_count, -1)
    block_count = deal.shape[0]
    ctx_size = lax.axis_size("ctx")
    own_blocks = block_count // ctx_size
    block_len = row_count // own_blocks
    shard = gain_attn.shape[0]
    heads_here = slopes.shape[0]
    groups = w_up.shape[1] // width
    me = lax.axis_index("wt").astype(jnp.int32).reshape(1)
    fast = ctx_size == 2 and lax.axis_size("seq") == 4
    slices = 8 if fast else 1

    short = jnp.concatenate(
        [gain_attn[None], gain_ffn[None], gate_vec[None], jnp.pad(slopes, (0, shard - heads_here))[None]], axis=0
    )
    pack = jnp.concatenate([w_qkv, jnp.pad(short, ((0, shard - 4), (0, 0)))], axis=1)
    others = swap(tokens, "ctx", 1)
    for bit in bits_of("ctx")[1:]:
        both = jnp.concatenate([tokens, others], axis=0)
        others = jnp.concatenate([others, swap(both, "ctx", bit)], axis=0)
    pack_far = swap(pack, "wt", 2)
    pack_near = swap(pack, "wt", 1)
    wide = lay_rows(width, [(w_out, 0), (w_memory, 0)] + [(w_up, width * g) for g in range(groups)] + [(w_down, 0)])
    neighbours = hold(neighbours, wide)

    offsets = jnp.arange(block_len, dtype=jnp.int32)
    owners = lax.axis_index("ctx") ^ jnp.arange(ctx_size, dtype=jnp.int32)
    slots = (owners[:, None] * own_blocks + jnp.arange(own_blocks, dtype=jnp.int32)[None, :]).reshape(-1)
    block_ids = jnp.arange(block_count, dtype=jnp.int32)
    slot_hot = (slots[:, None] == block_ids[None, :]).astype(jnp.int32)
    key_blocks = jnp.sum(slot_hot * deal[None, :], axis=1)
    key_pos = (key_blocks[:, None] * block_len + offsets[None, :]).reshape(-1)
    my_blocks = key_blocks[:own_blocks]
    row_pos = key_pos[:row_count]
    memory_hot = (my_blocks[:, None] == block_ids[None, :]).astype(jnp.int32)
    my_memory = jnp.sum(memory_hot * memory_len, axis=1)
    row_start = jnp.repeat(my_blocks * block_len, block_len)
    row_low = row_start - jnp.repeat(my_memory, block_len)
    hits = jnp.sum((neighbours[:, :, None] == key_pos[None, None, :]).astype(F32), axis=1)
    count = jnp.where(hits > 0.0, jnp.log(jnp.maximum(hits, 1.0)), ABSENT)
    pack_far, wide = lax.optimization_barrier((pack_far, wide, count))[:2]
    pack_both = swap(pack_far, "wt", 1)
    wide_far = swap(wide, "wt", 2)
    wide_near = swap(wide, "wt", 1)
    row_pos = hold(row_pos, pack_far)
    distance = jnp.log1p(jnp.abs(row_pos[:, None] - key_pos[None, :]).astype(F32))
    visible = (key_pos[None, :] >= row_low[:, None]) & (key_pos[None, :] < (row_start + block_len)[:, None])
    bias = jnp.where(visible, distance, HIDDEN)

    q, k, v, turned, full_qkv, small = project(
        me, tokens, hold(others, bias), (pack, pack_near, pack_far, pack_both)
    )
    saved = attend_forward(small, q, k, v, bias, count)
    wide_both = swap(hold(wide_far, saved[0]), "wt", 1)
    wides = (wide, wide_near, wide_far, wide_both)
    layer_out, gh1, go, gm, gate, g0, g1, g2, g3, h0, h1, h2, h3 = middle(
        slices, me, small, tokens, cotangent, saved[0], saved[1], wides, groups
    )

    all_pairs = width // 128
    g_far = add_low(g2, swap(g3, "wt", 1))
    g_one = swap(g1, "wt", 1)
    if fast:
        h_far = add_low(h2, swap(h3, "wt", 1))
        h_own = add_low(h0, swap(h1, "wt", 1))
        g_got = swap(g_far, "wt", 2)
        far_keep, far_got = send_half(h_far, "ctx", 1)
        own_keep, own_got = send_half(h_own, "ctx", 1)
        gq, gk, gv, gs = attend_backward(q, k, v, hold(go, g_far, h_far, h_own), gm, saved, bias, 0, all_pairs)
        gq, gk, gv, gs, g_got, far_got, own_got = lax.optimization_barrier(
            (gq, gk, gv, gs, g_got, far_got, own_got)
        )
        h_got = swap(add_low(far_keep, far_got), "wt", 2)
        g_keep, g_near = send_half(add_all(g0, [g_one, g_got]), "ctx", 1)
        q0, q1, q2, q3 = weight_grads(me, turned, hold(gq, g_keep), gk, gv, gs, gate)
        q_three, q_one = swap(q3, "wt", 1), swap(q1, "wt", 1)
        gq, q0, q2, g_near, h_got = lax.optimization_barrier((gq, q0, q2, g_near, h_got))
        q_far = add_low(q2, q_three)
        lower = add_low(g_keep, g_near).reshape(4, -1, width)
        higher = add_all(own_keep, [own_got, h_got]).reshape(4, -1, width)
        gh_keep, gh_got = send_half(jnp.concatenate([lower, higher], axis=1).reshape(-1, width), "seq", 1)
        near, own = row_grads(hold(gq, q_far, gh_keep), gk, gv, full_qkv)
        q_far = swap(q_far, "wt", 2)
        order = Order()
        near, gh_got = order.arrive(near, gh_got)
        gh = add_low(gh_keep, gh_got)
        gh_keep, gh_got = send_half(gh, "seq", 2)
        q_keep, q_got = send_half(add_all(q0, [q_one, order.arrive(q_far)]), "ctx", 1)
        gh = add_low(gh_keep, order.arrive(gh_got))
        gh_other = swap(gh, "seq", 2)
        q_sum = add_low(q_keep, order.arrive(q_got))
        q_got = swap(q_sum, "seq", 1)
        away = swap(hold(near, q_sum), "ctx", 1)
        own_a = place_half(gh, order.arrive(gh_other), "seq", 2)
        own_b = swap(own_a, "seq", 1)
        q_sum = add_low(q_sum, order.arrive(q_got))
        q_got = swap(q_sum, "seq", 2)
        away = order.arrive(away)
        other_a = swap(hold(own_a, away), "ctx", 1)
        grad_tokens = finish(tokens, small, gh1, own, away)
        order.before = (grad_tokens,)
        own_b = order.arrive(own_b)
        other_b = swap(own_b, "ctx", 1)
        q_sum = add_low(q_sum, order.arrive(q_got))
        q_other = swap(q_sum, "ctx", 1)
        side = lax.axis_index("ctx").astype(jnp.int32).reshape(1)
        pair = side_of("seq", 1).astype(jnp.int32).reshape(1)
        other_a, other_b = order.arrive(other_a, other_b)
        t_out, t_memory, t_down, t_up, t_gain_two = assemble(
            side, pair, (own_a, own_b, other_a, other_b), w_up, gain_ffn
        )
        order.before = (t_gain_two,)
        t_qkv, *shorts = close(side, q_sum, order.arrive(q_other), w_qkv, gain_attn, heads_here)
        t_gain_one, t_gate, t_slopes, t_gain_two = (value.reshape(-1) for value in (*shorts, t_gain_two))
    else:
        h_far = add_low(h2, swap(h3, "wt", 1))
        h_one = swap(h1, "wt", 1)
        g_sum = add_all(g0, [g_one, swap(g_far, "wt", 2)])
        h_sum = add_all(h0, [h_one, swap(h_far, "wt", 2)])
        gq, gk, gv, gs = attend_backward(q, k, v, go, gm, saved, bias, 0, all_pairs)
        grads = weight_grads(me, turned, gq, gk, gv, gs, gate)
        near, own = row_grads(gq, gk, gv, full_qkv)
        for bit in reversed(bits_of("ctx")[1:]):
            both = jnp.concatenate([own.astype(BF16), near], axis=0)
            fold = bit * row_count
            folded = both[:fold].astype(F32) + swap(both[fold:], "ctx", bit).astype(F32)
            own, near = folded[:row_count], folded[row_count:].astype(BF16)
        away = swap(near, "ctx", 1)
        q_far = swap(add_low(grads[2], swap(grads[3], "wt", 1)), "wt", 2)
        q_sum = add_all(grads[0], [swap(grads[1], "wt", 1), q_far])
        q_sum = near_whole(far_both(near_halves(q_sum)))
        g_sum = near_whole(far_whole(far_halves(near_halves(g_sum))))
        h_sum = near_whole(far_whole(far_halves(near_halves(h_sum))))
        grad_tokens = finish(tokens, small, gh1, own, away)
        t_out = g_sum[:shard].astype(F32)
        t_memory = g_sum[shard : 2 * shard].astype(F32)
        t_down = g_sum[2 * shard : 2 * shard + width].astype(F32)
        t_up = jnp.concatenate([h_sum[shard * g : shard * (g + 1)] for g in range(groups)], axis=1).astype(F32)
        t_qkv = q_sum[:, : 3 * width].astype(F32)
        t_slopes = q_sum[0, 3 * width : 3 * width + heads_here].astype(F32)
        t_gate = q_sum[1, 3 * width : 3 * width + shard].astype(F32)
        t_gain_one = jnp.sum(t_qkv * w_qkv.astype(F32), axis=1) / gain_attn.astype(F32)
        t_gain_two = jnp.sum(t_up * w_up.astype(F32), axis=1) / gain_ffn.astype(F32)


    return (
        layer_out[None], grad_tokens[None], t_qkv, t_out, t_up, t_down, t_memory,
        t_gain_one, t_gain_two, t_gate, t_slopes,
    )


def solution(mesh):
    rows = P(("seq", "wt"), "ctx", None)
    weight = P("wt", None)
    vector = P("wt")
    return jax.shard_map(
        on_device,
        mesh=mesh,
        in_specs=(rows, rows, P(), P(("seq", "wt"), None), rows) + (weight,) * 5 + (vector,) * 4,
        out_specs=(rows, rows) + (weight,) * 5 + (vector,) * 4,
        check_vma=False,
    )
```

```python
import functools
import math
import jax
import jax.numpy as jnp
from jax import lax
from jax.experimental import pallas as pl
from jax.experimental.pallas import tpu as pltpu
from jax.sharding import PartitionSpec as P

EPSILON = 1e-05
F32 = jnp.float32
BF16 = jnp.bfloat16
NT = (((1,), (1,)), ((), ()))
NN = (((1,), (0,)), ((), ()))
HIDDEN = 1e12
ABSENT = -1e30
VMEM = 56 * 1024 * 1024
CURVE = math.sqrt(2.0 / math.pi)
CUBIC = 0.044715


def product(left, right, dims=NN):
    return lax.dot_general(left, right, dims, preferred_element_type=F32)


def params(limit=VMEM):
    return pltpu.CompilerParams(vmem_limit_bytes=limit)


def like(shape, dtype):
    return jax.ShapeDtypeStruct(shape, dtype)


def in_place():
    return pl.BlockSpec(memory_space=pl.ANY)


def on_chip(*values):
    return [pltpu.with_memory_space_constraint(value, pltpu.VMEM) for value in values]


def scalar():
    return pl.BlockSpec(memory_space=pltpu.SMEM)


def swap(value, axis, bit):
    size = lax.axis_size(axis)
    return lax.ppermute(value, axis, [(i, i ^ bit) for i in range(size)])


def bits_of(axis):
    bits = []
    bit = 1
    while bit < lax.axis_size(axis):
        bits.append(bit)
        bit *= 2
    return bits


def side_of(axis, bit):
    return (lax.axis_index(axis) // bit) % 2


def hold(value, *before):
    return lax.optimization_barrier((value,) + before)[0]


class Order:
    def __init__(self):
        self.before = ()

    def arrive(self, *values):
        held = lax.optimization_barrier(values + self.before)[: len(values)]
        self.before = held[:1]
        return held if len(held) > 1 else held[0]


def send_half(part, axis, bit):
    side = side_of(axis, bit)
    both = part.reshape((2, part.shape[0] // 2) + part.shape[1:])
    got = swap(lax.dynamic_index_in_dim(both, 1 - side, 0, False), axis, bit)
    return lax.dynamic_index_in_dim(both, side, 0, False), got


def place_half(part, other, axis, bit):
    high = side_of(axis, bit) == 1
    return jnp.concatenate([jnp.where(high, other, part), jnp.where(high, part, other)], axis=0)


def add_all(own, got):
    total = own.astype(F32)
    for value in got:
        total = total + value.astype(F32)
    return total.astype(BF16)


def add_low(left, right):
    return (left.astype(F32) + right.astype(F32)).astype(BF16)


def halve(part, axis, bit):
    side = side_of(axis, bit)
    both = part.reshape((2, part.shape[0] // 2) + part.shape[1:])
    got = swap(lax.dynamic_index_in_dim(both, 1 - side, 0, False), axis, bit)
    return add_low(lax.dynamic_index_in_dim(both, side, 0, False), got)


def widen(part, axis, bit):
    other = swap(part, axis, bit)
    high = side_of(axis, bit) == 1
    return jnp.concatenate([jnp.where(high, other, part), jnp.where(high, part, other)], axis=0)


def near_halves(part):
    for bit in bits_of("ctx"):
        part = halve(part, "ctx", bit)
    return part


def near_whole(part):
    for bit in reversed(bits_of("ctx")):
        part = widen(part, "ctx", bit)
    return part


def far_halves(part):
    for bit in bits_of("seq"):
        part = halve(part, "seq", bit)
    return part


def far_whole(part):
    for bit in reversed(bits_of("seq")):
        part = widen(part, "seq", bit)
    return part


def far_both(part):
    for bit in bits_of("seq"):
        part = add_low(part, swap(part, "seq", bit))
    return part


def spread(values):
    centred = values - jnp.mean(values, axis=-1, keepdims=True)
    scale = lax.rsqrt(jnp.mean(centred * centred, axis=-1, keepdims=True) + EPSILON)
    return centred * scale, scale


def spread_back(unit, scale, grad):
    along = jnp.mean(grad * unit, axis=-1, keepdims=True)
    return scale * (grad - jnp.mean(grad, axis=-1, keepdims=True) - unit * along)


def lay_rows(width, pieces):
    arrays = [piece[0] for piece in pieces]
    total = sum(array.shape[0] for array in arrays)

    def body(*refs):
        target, sem = refs[len(pieces) :]
        copies = []
        first = 0
        for n, (ref, (_, col)) in enumerate(zip(refs, pieces)):
            source = ref.at[:, col : col + width]
            copies.append(pltpu.make_async_copy(source, target.at[first : first + ref.shape[0]], sem.at[n]))
            first += ref.shape[0]
        for copy in copies:
            copy.start()
        for copy in copies:
            copy.wait()

    vmem = pl.BlockSpec(memory_space=pltpu.VMEM)
    return pl.pallas_call(
        body,
        in_specs=[vmem] * len(arrays),
        out_specs=in_place(),
        out_shape=like((total, width), BF16),
        scratch_shapes=[pltpu.SemaphoreType.DMA((len(arrays),))],
        compiler_params=params(),
        cost_estimate=pl.CostEstimate(flops=0, transcendentals=0, bytes_accessed=4 * total * width),
        name="lay_rows",
    )(*arrays)


def project_body(me_ref, own_ref, other_ref, p0, p1, p2, p3, q_ref, k_ref, v_ref, turned_ref, w_ref, small_ref, few, sem):
    step = pl.program_id(0)
    width = own_ref.shape[1]
    shard = p0.shape[0]

    @pl.when(step == 0)
    def _():
        copies = []
        for r, pack in enumerate((p0, p1, p2, p3)):
            place = pl.multiple_of((me_ref[0] ^ r) * shard, shard)
            copies.append(
                pltpu.make_async_copy(pack.at[:, 0 : 3 * width], w_ref.at[pl.ds(place, shard), :], sem.at[2 * r])
            )
            copies.append(
                pltpu.make_async_copy(
                    pack.at[0:16, 3 * width : 3 * width + shard], few.at[:, pl.ds(place, shard)], sem.at[2 * r + 1]
                )
            )
        for copy in copies:
            copy.start()
        for copy in copies:
            copy.wait()
        small_ref[...] = few[...].astype(F32)

    tokens = jnp.where(step == 0, own_ref[...], other_ref[...]).astype(F32)
    unit, _ = spread(tokens)
    a1 = (unit * few[0:1, :].astype(F32)).astype(BF16)
    turned_ref[...] = a1.T

    @pl.when(step == 0)
    def _():
        q = product(a1, w_ref[:, 0:width]).astype(BF16)
        q_ref[...] = (q.astype(F32) * 0.125).astype(BF16)

    k_ref[...] = product(a1, w_ref[:, width : 2 * width]).astype(BF16)
    v_ref[...] = product(a1, w_ref[:, 2 * width : 3 * width]).astype(BF16)


def project(me, own, others, packs):
    rows, width = own.shape
    steps = 1 + others.shape[0] // rows
    whole = lambda i: (0, 0)
    return pl.pallas_call(
        project_body,
        grid=(steps,),
        in_specs=[
            scalar(),
            pl.BlockSpec((rows, width), whole),
            pl.BlockSpec((rows, width), lambda i: (jnp.maximum(i - 1, 0), 0)),
        ]
        + [in_place()] * 4,
        out_specs=[
            pl.BlockSpec((rows, width), whole),
            pl.BlockSpec((rows, width), lambda i: (i, 0)),
            pl.BlockSpec((rows, width), lambda i: (i, 0)),
            pl.BlockSpec((width, rows), lambda i: (0, i)),
            pl.BlockSpec((width, 3 * width), whole),
            pl.BlockSpec((16, width), whole),
        ],
        out_shape=[
            like((rows, width), BF16),
            like((rows * steps, width), BF16),
            like((rows * steps, width), BF16),
            like((width, rows * steps), BF16),
            like((width, 3 * width), BF16),
            like((16, width), F32),
        ],
        scratch_shapes=[pltpu.VMEM((16, width), BF16), pltpu.SemaphoreType.DMA((8,))],
        compiler_params=params(),
        cost_estimate=pl.CostEstimate(flops=6 * rows * steps * width * width, transcendentals=0, bytes_accessed=6000000),
        name="project",
    )(me, own, others, *packs)


def forward_body(
    rows, small_ref, q_ref, k_ref, v_ref, b_ref, c_ref, o_ref, m_ref, r1_ref, r2_ref, e1_ref, e2_ref, first, second
):
    low_lanes = lax.broadcasted_iota(jnp.int32, (rows, 128), 1) < 64
    values = jnp.concatenate([v_ref[...], jnp.ones(v_ref.shape, BF16)], axis=1)
    items = [(pl.ds(start, rows), side) for start in range(0, q_ref.shape[0], rows) for side in range(2)]

    def scores(n):
        at, side = items[n]
        slope = small_ref[3:4, side : side + 1]
        q_head = jnp.where(low_lanes == (side == 0), q_ref[at, :], 0).astype(BF16)
        raw = product(q_head, k_ref[...], NT)
        first[n % 2] = raw - slope * b_ref[at, :]
        second[n % 2] = raw + c_ref[at, :]
        return [jnp.max(table[n % 2], axis=1, keepdims=True) for table in (first, second)]

    mixed = {}
    peaks = scores(0)
    for n, (at, side) in enumerate(items):
        later = scores(n + 1) if n + 1 < len(items) else None
        for slot, (table, kept_ref) in enumerate(((first, e1_ref), (second, e2_ref))):
            weights = jnp.exp(table[n % 2] - peaks[slot]).astype(BF16)
            kept_ref[side, at, :] = weights
            both = product(weights, values)
            mixed[side, slot] = (both[:, :128], 1.0 / both[:, 128:])
        peaks = later
        if side == 1:
            for slot, value_ref, recip_ref in ((0, o_ref, r1_ref), (1, m_ref, r2_ref)):
                recip = jnp.where(low_lanes, mixed[0, slot][1], mixed[1, slot][1])
                recip_ref[at, :] = recip
                value_ref[at, :] = jnp.where(low_lanes, mixed[0, slot][0], mixed[1, slot][0]) * recip


def attend_forward(small, q, k, v, bias, count):
    row_count, width = q.shape
    key_count = k.shape[0]
    pairs = width // 128
    step_rows = max(64, min(row_count, (512 * 1024) // key_count))
    rows = min(256, step_rows)
    elements = 2 * pairs * row_count * key_count
    own = lambda p, i: (i, p)
    return pl.pallas_call(
        functools.partial(forward_body, rows),
        grid=(pairs, row_count // step_rows),
        in_specs=[
            pl.BlockSpec((16, 128), lambda p, i: (0, p)),
            pl.BlockSpec((step_rows, 128), own),
            pl.BlockSpec((key_count, 128), lambda p, i: (0, p)),
            pl.BlockSpec((key_count, 128), lambda p, i: (0, p)),
            pl.BlockSpec((step_rows, key_count), lambda p, i: (i, 0)),
            pl.BlockSpec((step_rows, key_count), lambda p, i: (i, 0)),
        ],
        out_specs=[pl.BlockSpec((step_rows, 128), own)] * 4
        + [pl.BlockSpec((2, step_rows, key_count), lambda p, i: (p, i, 0))] * 2,
        out_shape=[like((row_count, width), F32)] * 4 + [like((2 * pairs, row_count, key_count), BF16)] * 2,
        scratch_shapes=[pltpu.VMEM((2, rows, key_count), F32)] * 2,
        compiler_params=params(),
        cost_estimate=pl.CostEstimate(
            flops=elements * 64 * 2 * 3, transcendentals=2 * elements, bytes_accessed=4 * elements
        ),
        name="attend_forward",
    )(small, q, k, v, bias, count)


def middle_body(
    slices, me_ref, small_ref, tokens_ref, cot_ref, o_ref, m_ref, p0, p1, p2, p3,
    out_ref, gh1_ref, go_ref, gm_ref, gate_ref, g0, g1, g2, g3, h0, h1_ref, h2_ref, h3,
    w_out, w_memory, w_down, w_up, act, slope, gu, a2_turned, o_turned, m_turned, sem,
):
    rows, width = tokens_ref.shape
    shard = width // 4
    groups = w_down.shape[0] // width
    copies = []
    for r, pack in enumerate((p0, p1, p2, p3)):
        device = me_ref[0] ^ r
        place = pl.ds(pl.multiple_of(device * shard, shard), shard)
        down = pl.ds(pl.multiple_of(device * width, width), width)
        targets = [w_out.at[place], w_memory.at[place]] + [w_up.at[group, place] for group in range(groups)]
        pieces = [(pack.at[n * shard : (n + 1) * shard], target) for n, target in enumerate(targets)]
        pieces.append((pack.at[len(targets) * shard : len(targets) * shard + width], w_down.at[down]))
        copies.append([pltpu.make_async_copy(*piece, sem.at[r, n]) for n, piece in enumerate(pieces)])
    for part in zip(*copies):
        for copy in part:
            copy.start()
    gain = small_ref[1:2, :]
    gate_vec = small_ref[2:3, :]
    o_low = o_ref[...].astype(BF16)
    m_low = m_ref[...].astype(BF16)
    for copy in copies:
        copy[0].wait()
        copy[1].wait()
    h1 = tokens_ref[...].astype(F32) + product(o_low, w_out[...])
    mem = product(m_low, w_memory[...])
    o_turned[...] = o_low.T
    m_turned[...] = m_low.T
    unit, scale = spread(h1)
    a2 = (unit * gain).astype(BF16)
    a2_turned[...] = a2.T
    for copy in copies:
        for piece in copy[2:]:
            piece.wait()
    h2 = h1
    for group in range(groups):
        u = product(a2, w_up[group])
        square = u * u
        bent = jnp.tanh(CURVE * u * (1.0 + CUBIC * square))
        half = 0.5 * (1.0 + bent)
        active = (u * half).astype(BF16)
        slope[group] = half + 0.5 * u * (1.0 - bent * bent) * (CURVE * (1.0 + 3.0 * CUBIC * square))
        act[group] = active.T
        h2 = h2 + product(active, w_down[group * width : (group + 1) * width, :])
    gate = jax.nn.sigmoid(jnp.sum(h2 * gate_vec, axis=1, keepdims=True))
    apart = mem - h2
    out_ref[...] = (h2 + gate * apart).astype(BF16)
    c = cot_ref[...].astype(F32)
    grad_mem = (c * gate).astype(BF16)
    dz = jnp.sum(c * apart, axis=1, keepdims=True) * gate * (1.0 - gate)
    gh2 = c * (1.0 - gate) + dz * gate_vec
    gate_ref[...] = jnp.broadcast_to(jnp.sum(dz * h2, axis=0, keepdims=True), gate_ref.shape)
    gf = gh2.astype(BF16)
    gm_ref[...] = product(grad_mem, w_memory[...], NT).astype(BF16)
    ga2 = None
    for group in range(groups):
        back = product(gf, w_down[group * width : (group + 1) * width, :], NT)
        low = (back * slope[group]).astype(BF16)
        gu[group] = low
        more = product(low, w_up[group], NT)
        ga2 = more if ga2 is None else ga2 + more
    gh1 = gh2 + spread_back(unit, scale, ga2 * gain)
    gh1_ref[...] = gh1
    ga = gh1.astype(BF16)
    go_ref[...] = product(ga, w_out[...], NT).astype(BF16)
    for r, (grad_ref, up_ref) in enumerate(((g0, h0), (g1, h1_ref), (g2, h2_ref), (g3, h3))):
        device = me_ref[0] ^ r
        place = pl.ds(pl.multiple_of(device * shard, shard), shard)
        parts = [product(o_turned[place, :], ga), product(m_turned[place, :], grad_mem), product(act[device], gf)]
        lay_slices(grad_ref, slices, [part.astype(BF16) for part in parts])
        parts = [product(a2_turned[place, :], gu[group]) for group in range(groups)]
        lay_slices(up_ref, slices, [part.astype(BF16) for part in parts])


def lay_slices(target, slices, parts):
    first = 0
    for n in range(slices):
        for part in parts:
            height = part.shape[0] // slices
            target[first : first + height, :] = part[n * height : (n + 1) * height, :]
            first += height


def middle(slices, me, small, tokens, cotangent, o, m, packs, groups):
    rows, width = tokens.shape
    shard = width // 4
    vmem = pl.BlockSpec(memory_space=pltpu.VMEM)
    square = lambda dtype: pltpu.VMEM((width, width), dtype)
    return pl.pallas_call(
        functools.partial(middle_body, slices),
        in_specs=[scalar()] + [vmem] * 5 + [in_place()] * 4,
        out_specs=[vmem] * 13,
        out_shape=[
            like((rows, width), BF16),
            like((rows, width), F32),
            like((rows, width), BF16),
            like((rows, width), BF16),
            like((8, width), F32),
        ]
        + [like((2 * shard + width, width), BF16)] * 4
        + [like((groups * shard, width), BF16)] * 4,
        scratch_shapes=[
            square(BF16),
            square(BF16),
            pltpu.VMEM((groups * width, width), BF16),
            pltpu.VMEM((groups, width, width), BF16),
            pltpu.VMEM((groups, width, rows), BF16),
            pltpu.VMEM((groups, rows, width), F32),
            pltpu.VMEM((groups, rows, width), BF16),
            pltpu.VMEM((width, rows), BF16),
            pltpu.VMEM((width, rows), BF16),
            pltpu.VMEM((width, rows), BF16),
            pltpu.SemaphoreType.DMA((4, 3 + groups)),
        ],
        compiler_params=params(),
        cost_estimate=pl.CostEstimate(
            flops=2 * rows * width * width * 3 * 10, transcendentals=4 * rows * width, bytes_accessed=16000000
        ),
        name="middle",
    )(me, small, tokens, cotangent, o, m, *packs)


def backward_body(
    several, rows, q_ref, k_ref, v_ref, go_ref, gm_ref, o_ref, m_ref, r1_ref, r2_ref, b_ref, e1_ref, e2_ref,
    gq_ref, gk_ref, gv_ref, gs_ref,
):
    low_lanes = lax.broadcasted_iota(jnp.int32, (rows, 128), 1) < 64
    keys = k_ref[...]
    vals = v_ref[...]
    totals = [None, None]
    for start in range(0, q_ref.shape[0], rows):
        at = pl.ds(start, rows)
        g1 = (go_ref[at, :].astype(F32) * r1_ref[at, :]).astype(BF16)
        g2 = (gm_ref[at, :].astype(F32) * r2_ref[at, :]).astype(BF16)
        t1 = g1.astype(F32) * o_ref[at, :]
        t2 = g2.astype(F32) * m_ref[at, :]
        q_turned = q_ref[at, :].T
        g1_turned = g1.T
        g2_turned = g2.T
        grads = []
        for side in range(2):
            mine = low_lanes == (side == 0)
            d1 = jnp.sum(jnp.where(mine, t1, 0.0), axis=1, keepdims=True)
            d2 = jnp.sum(jnp.where(mine, t2, 0.0), axis=1, keepdims=True)
            e1 = e1_ref[side, at, :]
            e2 = e2_ref[side, at, :]
            p1 = product(jnp.where(mine, g1, 0).astype(BF16), vals, NT)
            ds1 = e1.astype(F32) * (p1 - d1)
            slope_term = jnp.sum(ds1 * b_ref[at, :], axis=0, keepdims=True)
            p2 = product(jnp.where(mine, g2, 0).astype(BF16), vals, NT)
            ds = (ds1 + e2.astype(F32) * (p2 - d2)).astype(BF16)
            grads.append(product(ds, keys))
            head = slice(64 * side, 64 * side + 64)
            gk = product(q_turned[head, :], ds)
            gv = product(g1_turned[head, :], e1) + product(g2_turned[head, :], e2)
            if start > 0:
                gk, gv, slope_term = (have + more for have, more in zip(totals[side], (gk, gv, slope_term)))
            totals[side] = (gk, gv, slope_term)
        gq = jnp.where(low_lanes, grads[0], grads[1]) * 0.125
        if not several:
            gq_ref[at, :] = gq.astype(gq_ref.dtype)
        else:
            gq_ref[at, :] = jnp.where(pl.program_id(1) == 0, gq, gq_ref[at, :] + gq)
    gk_ref[...] = jnp.concatenate([totals[0][0], totals[1][0]], axis=0).astype(BF16).T
    gv_ref[...] = jnp.concatenate([totals[0][1], totals[1][1]], axis=0).astype(BF16).T
    for side in range(2):
        term = totals[side][2]
        parts = term[:, 0:128]
        for first in range(128, term.shape[1], 128):
            parts = parts + term[:, first : first + 128]
        if not several:
            gs_ref[side : side + 1, :] = parts
        else:
            gs_ref[side : side + 1, :] = jnp.where(pl.program_id(1) == 0, parts, gs_ref[side : side + 1, :] + parts)


def attend_backward(q, k, v, go, gm, saved, bias, first, pairs):
    o, m, r1, r2, e1, e2 = saved
    row_count = q.shape[0]
    key_count = k.shape[0]
    step_keys = min(1024, key_count)
    several = key_count > step_keys
    elements = 2 * pairs * row_count * key_count
    wide = pl.BlockSpec((row_count, 128), lambda p, c: (0, p + first))
    near = pl.BlockSpec((step_keys, 128), lambda p, c: (c, p + first))
    table = pl.BlockSpec((2, row_count, step_keys), lambda p, c: (p + first, 0, c))
    own = pl.BlockSpec((step_keys, 128), lambda p, c: (c, p))
    return pl.pallas_call(
        functools.partial(backward_body, several, 256),
        grid=(pairs, key_count // step_keys),
        in_specs=[wide, near, near, wide, wide, wide, wide, wide, wide]
        + [pl.BlockSpec((row_count, step_keys), lambda p, c: (0, c)), table, table],
        out_specs=[
            pl.BlockSpec((row_count, 128), lambda p, c: (0, p)),
            own,
            own,
            pl.BlockSpec((None, 8, 128), lambda p, c: (p, 0, 0)),
        ],
        out_shape=[
            like((row_count, 128 * pairs), F32 if several else BF16),
            like((key_count, 128 * pairs), BF16),
            like((key_count, 128 * pairs), BF16),
            like((pairs, 8, 128), F32),
        ],
        compiler_params=params(),
        cost_estimate=pl.CostEstimate(flops=elements * 64 * 2 * 6, transcendentals=0, bytes_accessed=4 * elements),
        name="attend_backward",
    )(q, k, v, go, gm, o, m, r1, r2, bias, e1, e2)


def weights_body(me_ref, turned_ref, gq_ref, gk_ref, gv_ref, gs_ref, gate_ref, *grad_refs):
    rows, width = gq_ref.shape
    shard = width // 4
    lane = lax.broadcasted_iota(jnp.int32, (16, shard), 1)
    row = lax.broadcasted_iota(jnp.int32, (16, shard), 0)
    for r in range(4):
        grad_ref = grad_refs[r]
        device = me_ref[0] ^ r
        start = pl.multiple_of(device * shard, shard)
        a1 = turned_ref[pl.ds(start, shard), :]
        grad_ref[:, 0:width] = product(a1[:, 0:rows], gq_ref[...].astype(BF16)).astype(BF16)
        grad_ref[:, width : 2 * width] = product(a1, gk_ref[...]).astype(BF16)
        grad_ref[:, 2 * width : 3 * width] = product(a1, gv_ref[...]).astype(BF16)
        sums = -jnp.sum(gs_ref[device, 0:2, :], axis=1, keepdims=True)
        block = jnp.where((row == 0) & (lane == 0), sums[0:1, :], 0.0)
        block = jnp.where((row == 0) & (lane == 1), sums[1:2, :], block)
        block = jnp.where(row == 1, gate_ref[0:1, pl.ds(start, shard)], block)
        grad_ref[:, 3 * width : 3 * width + shard] = jnp.zeros((shard, shard), BF16)
        grad_ref[0:16, 3 * width : 3 * width + shard] = block.astype(BF16)


def weight_grads(me, turned, gq, gk, gv, gs, gate):
    rows, width = gq.shape
    shard = width // 4
    vmem = pl.BlockSpec(memory_space=pltpu.VMEM)
    return pl.pallas_call(
        weights_body,
        in_specs=[scalar()] + [vmem] * 6,
        out_specs=[vmem] * 4,
        out_shape=[like((shard, 3 * width + shard), BF16)] * 4,
        compiler_params=params(),
        cost_estimate=pl.CostEstimate(
            flops=6 * gk.shape[0] * width * width, transcendentals=0, bytes_accessed=6000000
        ),
        name="weight_grads",
    )(me, turned, gq, gk, gv, gs, gate)


def rows_body(gq_ref, gk_ref, gv_ref, w_ref, near_ref, own_ref):
    rows, width = gq_ref.shape
    w_k = w_ref[:, width : 2 * width]
    w_v = w_ref[:, 2 * width : 3 * width]
    for first in range(rows, gk_ref.shape[0], rows):
        at = slice(first, first + rows)
        part = product(gk_ref[at, :], w_k, NT) + product(gv_ref[at, :], w_v, NT)
        near_ref[first - rows : first, :] = part.astype(BF16)
    own = product(gq_ref[...].astype(BF16), w_ref[:, 0:width], NT)
    own_ref[...] = own + product(gk_ref[0:rows, :], w_k, NT) + product(gv_ref[0:rows, :], w_v, NT)


def row_grads(gq, gk, gv, w):
    rows, width = gq.shape
    vmem = pl.BlockSpec(memory_space=pltpu.VMEM)
    return pl.pallas_call(
        rows_body,
        in_specs=[vmem] * 4,
        out_specs=[vmem] * 2,
        out_shape=[like((gk.shape[0] - rows, width), BF16), like((rows, width), F32)],
        compiler_params=params(),
        cost_estimate=pl.CostEstimate(
            flops=6 * gk.shape[0] * width * width, transcendentals=0, bytes_accessed=6000000
        ),
        name="row_grads",
    )(gq, gk, gv, w)


def row_sums(table, weight_ref, gain_ref):
    ones = jnp.ones((8, table.shape[1]), F32)
    sums = lax.dot_general(
        ones, table * weight_ref[...].astype(F32), NT, precision=lax.Precision.HIGHEST, preferred_element_type=F32
    )
    return sums[0:1, :] / gain_ref[...].astype(F32)


def assemble_body(
    near_ref, far_ref, own_a, own_b, other_a, by_ctx, by_seq, up_w_ref, gain_ref, out_ref, memory_ref, down_ref, up_ref, sum_ref
):
    width = out_ref.shape[1]
    groups = up_ref.shape[1] // width
    short = out_ref.shape[0] // 8
    tall = down_ref.shape[0] // 8
    size = own_a.shape[0] // 2
    for n, (part_ref, first_part) in enumerate(((own_a, 0), (own_b, 0), (other_a, 0), (by_ctx, 0), (by_seq, 1))):
        side = near_ref[0] if n < 2 else 1 - near_ref[0]
        pair = far_ref[0] if n % 2 == 0 and n < 4 else 1 - far_ref[0]
        for p in range(part_ref.shape[0] // size):
            place = 4 * side + 2 * pair + first_part + p
            at = pl.ds(pl.multiple_of(place * short, short), short)
            piece = part_ref[p * size : (p + 1) * size, :].astype(F32)
            out_ref[at, :] = piece[0:short, :]
            memory_ref[at, :] = piece[short : 2 * short, :]
            down_ref[pl.ds(pl.multiple_of(place * tall, tall), tall), :] = piece[2 * short : 2 * short + tall, :]
            for group in range(groups):
                first = 2 * short + tall + group * short
                up_ref[at, group * width : (group + 1) * width] = piece[first : first + short, :]
    sum_ref[...] = row_sums(up_ref[...], up_w_ref, gain_ref)


def assemble(near, far, parts, w_up, gain):
    width = parts[0].shape[1]
    shard, columns = w_up.shape
    vmem = pl.BlockSpec(memory_space=pltpu.VMEM)
    return pl.pallas_call(
        assemble_body,
        in_specs=[scalar(), scalar()] + [vmem] * 7,
        out_specs=[vmem] * 5,
        out_shape=[like((shard, width), F32)] * 2
        + [like((width, width), F32), like((shard, columns), F32), like((1, shard), F32)],
        compiler_params=params(),
        cost_estimate=pl.CostEstimate(flops=0, transcendentals=0, bytes_accessed=4000000),
        name="assemble",
    )(near, far, *on_chip(*parts), w_up, gain[None])


def close_body(near_ref, own_ref, other_ref, w_ref, gain_ref, qkv_ref, gain_sum_ref, gate_ref, slope_ref):
    half = own_ref.shape[0]
    wide = qkv_ref.shape[1]
    for n, part_ref in enumerate((own_ref, other_ref)):
        side = near_ref[0] if n == 0 else 1 - near_ref[0]
        qkv_ref[pl.ds(pl.multiple_of(side * half, half), half), :] = part_ref[:, 0:wide].astype(F32)
    first = jnp.where(near_ref[0] == 0, own_ref[0:16, wide:].astype(F32), other_ref[0:16, wide:].astype(F32))
    slope_ref[...] = first[0:1, 0 : slope_ref.shape[1]]
    gate_ref[...] = first[1:2, :]
    gain_sum_ref[...] = row_sums(qkv_ref[...], w_ref, gain_ref)


def close(near, own, other, w_qkv, gain, heads):
    shard, wide = w_qkv.shape
    vmem = pl.BlockSpec(memory_space=pltpu.VMEM)
    return pl.pallas_call(
        close_body,
        in_specs=[scalar()] + [vmem] * 4,
        out_specs=[vmem] * 4,
        out_shape=[like((shard, wide), F32), like((1, shard), F32), like((1, shard), F32), like((1, heads), F32)],
        compiler_params=params(),
        cost_estimate=pl.CostEstimate(flops=0, transcendentals=0, bytes_accessed=2000000),
        name="close",
    )(near, *on_chip(own, other), w_qkv, gain[None])


def finish_body(tokens_ref, small_ref, gh1_ref, own_ref, away_ref, out_ref):
    unit, scale = spread(tokens_ref[...].astype(F32))
    grad = (own_ref[...] + away_ref[...].astype(F32)) * small_ref[0:1, :]
    out_ref[...] = gh1_ref[...] + spread_back(unit, scale, grad)


def finish(tokens, small, gh1, own, away):
    vmem = pl.BlockSpec(memory_space=pltpu.VMEM)
    return pl.pallas_call(
        finish_body,
        in_specs=[vmem] * 5,
        out_specs=vmem,
        out_shape=like(gh1.shape, F32),
        compiler_params=params(),
        cost_estimate=pl.CostEstimate(flops=0, transcendentals=0, bytes_accessed=4000000),
        name="finish",
    )(tokens, small, gh1, own, *on_chip(away))


def on_device(
    tokens, cotangent, deal, memory_len, neighbours,
    w_qkv, w_out, w_up, w_down, w_memory, gain_attn, gain_ffn, gate_vec, slopes,
):
    _, row_count, width = tokens.shape
    tokens = tokens.reshape(row_count, width)
    cotangent = cotangent.reshape(row_count, width)
    neighbours = neighbours.reshape(row_count, -1)
    block_count = deal.shape[0]
    ctx_size = lax.axis_size("ctx")
    own_blocks = block_count // ctx_size
    block_len = row_count // own_blocks
    shard = gain_attn.shape[0]
    heads_here = slopes.shape[0]
    groups = w_up.shape[1] // width
    me = lax.axis_index("wt").astype(jnp.int32).reshape(1)
    fast = ctx_size == 2 and lax.axis_size("seq") == 4
    slices = 8 if fast else 1

    short = jnp.concatenate(
        [gain_attn[None], gain_ffn[None], gate_vec[None], jnp.pad(slopes, (0, shard - heads_here))[None]], axis=0
    )
    pack = jnp.concatenate([w_qkv, jnp.pad(short, ((0, shard - 4), (0, 0)))], axis=1)
    others = swap(tokens, "ctx", 1)
    for bit in bits_of("ctx")[1:]:
        both = jnp.concatenate([tokens, others], axis=0)
        others = jnp.concatenate([others, swap(both, "ctx", bit)], axis=0)
    pack_far = swap(pack, "wt", 2)
    pack_near = swap(pack, "wt", 1)
    wide = lay_rows(width, [(w_out, 0), (w_memory, 0)] + [(w_up, width * g) for g in range(groups)] + [(w_down, 0)])
    neighbours = hold(neighbours, wide)

    offsets = jnp.arange(block_len, dtype=jnp.int32)
    owners = lax.axis_index("ctx") ^ jnp.arange(ctx_size, dtype=jnp.int32)
    slots = (owners[:, None] * own_blocks + jnp.arange(own_blocks, dtype=jnp.int32)[None, :]).reshape(-1)
    block_ids = jnp.arange(block_count, dtype=jnp.int32)
    slot_hot = (slots[:, None] == block_ids[None, :]).astype(jnp.int32)
    key_blocks = jnp.sum(slot_hot * deal[None, :], axis=1)
    key_pos = (key_blocks[:, None] * block_len + offsets[None, :]).reshape(-1)
    my_blocks = key_blocks[:own_blocks]
    row_pos = key_pos[:row_count]
    memory_hot = (my_blocks[:, None] == block_ids[None, :]).astype(jnp.int32)
    my_memory = jnp.sum(memory_hot * memory_len, axis=1)
    row_start = jnp.repeat(my_blocks * block_len, block_len)
    row_low = row_start - jnp.repeat(my_memory, block_len)
    picks = neighbours.shape[1]
    hits = sum((neighbours[:, n : n + 1] == key_pos[None, :]).astype(F32) for n in range(picks))
    count = jnp.where(hits == 1.0, 0.0, ABSENT)
    for times in range(2, picks + 1):
        count = jnp.where(hits == float(times), math.log(times), count)
    pack_far, wide = lax.optimization_barrier((pack_far, wide, count))[:2]
    pack_both = swap(pack_far, "wt", 1)
    wide_far = swap(wide, "wt", 2)
    wide_near = swap(wide, "wt", 1)
    row_pos = hold(row_pos, pack_far)
    distance = jnp.log(jnp.abs(row_pos[:, None] - key_pos[None, :]).astype(F32) + 1.0)
    visible = (key_pos[None, :] >= row_low[:, None]) & (key_pos[None, :] < (row_start + block_len)[:, None])
    bias = jnp.where(visible, distance, HIDDEN)

    q, k, v, turned, full_qkv, small = project(
        me, tokens, hold(others, bias), (pack, pack_near, pack_far, pack_both)
    )
    saved = attend_forward(small, q, k, v, bias, count)
    wide_both = swap(hold(wide_far, saved[0]), "wt", 1)
    wides = (wide, wide_near, wide_far, wide_both)
    layer_out, gh1, go, gm, gate, g0, g1, g2, g3, h0, h1, h2, h3 = middle(
        slices, me, small, tokens, cotangent, saved[0], saved[1], wides, groups
    )

    all_pairs = width // 128
    g_far = add_low(g2, swap(g3, "wt", 1))
    g_one = swap(g1, "wt", 1)
    if fast:
        h_far = add_low(h2, swap(h3, "wt", 1))
        h_own = add_low(h0, swap(h1, "wt", 1))
        g_got = swap(g_far, "wt", 2)
        far_keep, far_got = send_half(h_far, "ctx", 1)
        own_keep, own_got = send_half(h_own, "ctx", 1)
        gq, gk, gv, gs = attend_backward(q, k, v, hold(go, g_far, h_far, h_own), gm, saved, bias, 0, all_pairs)
        gq, gk, gv, gs, g_got, far_got, own_got = lax.optimization_barrier(
            (gq, gk, gv, gs, g_got, far_got, own_got)
        )
        h_got = swap(add_low(far_keep, far_got), "wt", 2)
        g_keep, g_near = send_half(add_all(g0, [g_one, g_got]), "ctx", 1)
        q0, q1, q2, q3 = weight_grads(me, turned, hold(gq, g_keep), gk, gv, gs, gate)
        q_three, q_one = swap(q3, "wt", 1), swap(q1, "wt", 1)
        gq, q0, q2, g_near, h_got = lax.optimization_barrier((gq, q0, q2, g_near, h_got))
        q_far = add_low(q2, q_three)
        lower = add_low(g_keep, g_near).reshape(4, -1, width)
        higher = add_all(own_keep, [own_got, h_got]).reshape(4, -1, width)
        gh_keep, gh_got = send_half(jnp.concatenate([lower, higher], axis=1).reshape(-1, width), "seq", 1)
        near, own = row_grads(hold(gq, q_far, gh_keep), gk, gv, full_qkv)
        q_far = swap(q_far, "wt", 2)
        order = Order()
        near, gh_got = order.arrive(near, gh_got)
        gh = add_low(gh_keep, gh_got)
        gh_got = swap(gh, "seq", 2)
        q_keep, q_got = send_half(add_all(q0, [q_one, order.arrive(q_far)]), "ctx", 1)
        q_sum = add_low(q_keep, order.arrive(q_got))
        q_got = swap(q_sum, "seq", 1)
        away = swap(hold(near, q_sum), "ctx", 1)
        q_sum = add_low(q_sum, order.arrive(q_got))
        q_got = swap(q_sum, "seq", 2)
        own_a = add_low(gh, order.arrive(gh_got))
        own_b = swap(own_a, "seq", 1)
        other_a = swap(own_a, "ctx", 1)
        away = order.arrive(away)
        grad_tokens = finish(tokens, small, gh1, own, away)
        order.before = (grad_tokens,)
        q_sum = add_low(q_sum, order.arrive(q_got))
        q_other = swap(q_sum, "ctx", 1)
        own_b = order.arrive(own_b)
        other_a = order.arrive(other_a)
        cut = own_b.shape[0] // 2
        by_seq = swap(other_a[cut:], "seq", 1)
        by_ctx = swap(own_b[:cut], "ctx", 1)
        side = lax.axis_index("ctx").astype(jnp.int32).reshape(1)
        pair = side_of("seq", 1).astype(jnp.int32).reshape(1)
        by_ctx, by_seq = order.arrive(by_ctx, by_seq)
        t_out, t_memory, t_down, t_up, t_gain_two = assemble(
            side, pair, (own_a, own_b, other_a, by_ctx, by_seq), w_up, gain_ffn
        )
        order.before = (t_gain_two,)
        t_qkv, *shorts = close(side, q_sum, order.arrive(q_other), w_qkv, gain_attn, heads_here)
        t_gain_one, t_gate, t_slopes, t_gain_two = (value.reshape(-1) for value in (*shorts, t_gain_two))
    else:
        h_far = add_low(h2, swap(h3, "wt", 1))
        h_one = swap(h1, "wt", 1)
        g_sum = add_all(g0, [g_one, swap(g_far, "wt", 2)])
        h_sum = add_all(h0, [h_one, swap(h_far, "wt", 2)])
        gq, gk, gv, gs = attend_backward(q, k, v, go, gm, saved, bias, 0, all_pairs)
        grads = weight_grads(me, turned, gq, gk, gv, gs, gate)
        near, own = row_grads(gq, gk, gv, full_qkv)
        for bit in reversed(bits_of("ctx")[1:]):
            both = jnp.concatenate([own.astype(BF16), near], axis=0)
            fold = bit * row_count
            folded = both[:fold].astype(F32) + swap(both[fold:], "ctx", bit).astype(F32)
            own, near = folded[:row_count], folded[row_count:].astype(BF16)
        away = swap(near, "ctx", 1)
        q_far = swap(add_low(grads[2], swap(grads[3], "wt", 1)), "wt", 2)
        q_sum = add_all(grads[0], [swap(grads[1], "wt", 1), q_far])
        q_sum = near_whole(far_both(near_halves(q_sum)))
        g_sum = near_whole(far_whole(far_halves(near_halves(g_sum))))
        h_sum = near_whole(far_whole(far_halves(near_halves(h_sum))))
        grad_tokens = finish(tokens, small, gh1, own, away)
        t_out = g_sum[:shard].astype(F32)
        t_memory = g_sum[shard : 2 * shard].astype(F32)
        t_down = g_sum[2 * shard : 2 * shard + width].astype(F32)
        t_up = jnp.concatenate([h_sum[shard * g : shard * (g + 1)] for g in range(groups)], axis=1).astype(F32)
        t_qkv = q_sum[:, : 3 * width].astype(F32)
        t_slopes = q_sum[0, 3 * width : 3 * width + heads_here].astype(F32)
        t_gate = q_sum[1, 3 * width : 3 * width + shard].astype(F32)
        t_gain_one = jnp.sum(t_qkv * w_qkv.astype(F32), axis=1) / gain_attn.astype(F32)
        t_gain_two = jnp.sum(t_up * w_up.astype(F32), axis=1) / gain_ffn.astype(F32)


    return (
        layer_out[None], grad_tokens[None], t_qkv, t_out, t_up, t_down, t_memory,
        t_gain_one, t_gain_two, t_gate, t_slopes,
    )


def solution(mesh):
    rows = P(("seq", "wt"), "ctx", None)
    weight = P("wt", None)
    vector = P("wt")
    return jax.shard_map(
        on_device,
        mesh=mesh,
        in_specs=(rows, rows, P(), P(("seq", "wt"), None), rows) + (weight,) * 5 + (vector,) * 4,
        out_specs=(rows, rows) + (weight,) * 5 + (vector,) * 4,
        check_vma=False,
    )
```

```python
import functools
import math
import jax
import jax.numpy as jnp
from jax import lax
from jax.experimental import pallas as pl
from jax.experimental.pallas import tpu as pltpu
from jax.sharding import PartitionSpec as P

EPSILON = 1e-05
F32 = jnp.float32
BF16 = jnp.bfloat16
NT = (((1,), (1,)), ((), ()))
NN = (((1,), (0,)), ((), ()))
HIDDEN = 1e12
ABSENT = -1e30
VMEM = 56 * 1024 * 1024
CURVE = math.sqrt(2.0 / math.pi)
CUBIC = 0.044715


def product(left, right, dims=NN):
    return lax.dot_general(left, right, dims, preferred_element_type=F32)


def params(limit=VMEM):
    return pltpu.CompilerParams(vmem_limit_bytes=limit)


def like(shape, dtype):
    return jax.ShapeDtypeStruct(shape, dtype)


def in_place():
    return pl.BlockSpec(memory_space=pl.ANY)


def on_chip(*values):
    return [pltpu.with_memory_space_constraint(value, pltpu.VMEM) for value in values]


def scalar():
    return pl.BlockSpec(memory_space=pltpu.SMEM)


def swap(value, axis, bit):
    size = lax.axis_size(axis)
    return lax.ppermute(value, axis, [(i, i ^ bit) for i in range(size)])


def bits_of(axis):
    bits = []
    bit = 1
    while bit < lax.axis_size(axis):
        bits.append(bit)
        bit *= 2
    return bits


def side_of(axis, bit):
    return (lax.axis_index(axis) // bit) % 2


def hold(value, *before):
    return lax.optimization_barrier((value,) + before)[0]


class Order:
    def __init__(self):
        self.before = ()

    def arrive(self, *values):
        held = lax.optimization_barrier(values + self.before)[: len(values)]
        self.before = held[:1]
        return held if len(held) > 1 else held[0]


def send_half(part, axis, bit):
    side = side_of(axis, bit)
    both = part.reshape((2, part.shape[0] // 2) + part.shape[1:])
    got = swap(lax.dynamic_index_in_dim(both, 1 - side, 0, False), axis, bit)
    return lax.dynamic_index_in_dim(both, side, 0, False), got


def place_half(part, other, axis, bit):
    high = side_of(axis, bit) == 1
    return jnp.concatenate([jnp.where(high, other, part), jnp.where(high, part, other)], axis=0)


def add_all(own, got):
    total = own.astype(F32)
    for value in got:
        total = total + value.astype(F32)
    return total.astype(BF16)


def add_low(left, right):
    return (left.astype(F32) + right.astype(F32)).astype(BF16)


def halve(part, axis, bit):
    side = side_of(axis, bit)
    both = part.reshape((2, part.shape[0] // 2) + part.shape[1:])
    got = swap(lax.dynamic_index_in_dim(both, 1 - side, 0, False), axis, bit)
    return add_low(lax.dynamic_index_in_dim(both, side, 0, False), got)


def widen(part, axis, bit):
    other = swap(part, axis, bit)
    high = side_of(axis, bit) == 1
    return jnp.concatenate([jnp.where(high, other, part), jnp.where(high, part, other)], axis=0)


def near_halves(part):
    for bit in bits_of("ctx"):
        part = halve(part, "ctx", bit)
    return part


def near_whole(part):
    for bit in reversed(bits_of("ctx")):
        part = widen(part, "ctx", bit)
    return part


def far_halves(part):
    for bit in bits_of("seq"):
        part = halve(part, "seq", bit)
    return part


def far_whole(part):
    for bit in reversed(bits_of("seq")):
        part = widen(part, "seq", bit)
    return part


def far_both(part):
    for bit in bits_of("seq"):
        part = add_low(part, swap(part, "seq", bit))
    return part


def spread(values):
    centred = values - jnp.mean(values, axis=-1, keepdims=True)
    scale = lax.rsqrt(jnp.mean(centred * centred, axis=-1, keepdims=True) + EPSILON)
    return centred * scale, scale


def spread_back(unit, scale, grad):
    along = jnp.mean(grad * unit, axis=-1, keepdims=True)
    return scale * (grad - jnp.mean(grad, axis=-1, keepdims=True) - unit * along)


def lay_rows(width, pieces):
    arrays = [piece[0] for piece in pieces]
    total = sum(array.shape[0] for array in arrays)

    def body(*refs):
        target, sem = refs[len(pieces) :]
        copies = []
        first = 0
        for n, (ref, (_, col)) in enumerate(zip(refs, pieces)):
            source = ref.at[:, col : col + width]
            copies.append(pltpu.make_async_copy(source, target.at[first : first + ref.shape[0]], sem.at[n]))
            first += ref.shape[0]
        for copy in copies:
            copy.start()
        for copy in copies:
            copy.wait()

    vmem = pl.BlockSpec(memory_space=pltpu.VMEM)
    return pl.pallas_call(
        body,
        in_specs=[vmem] * len(arrays),
        out_specs=in_place(),
        out_shape=like((total, width), BF16),
        scratch_shapes=[pltpu.SemaphoreType.DMA((len(arrays),))],
        compiler_params=params(),
        cost_estimate=pl.CostEstimate(flops=0, transcendentals=0, bytes_accessed=4 * total * width),
        name="lay_rows",
    )(*arrays)


def project_body(me_ref, own_ref, other_ref, p0, p1, p2, p3, q_ref, k_ref, v_ref, turned_ref, w_ref, small_ref, few, sem):
    step = pl.program_id(0)
    width = own_ref.shape[1]
    shard = p0.shape[0]

    copies = []
    shorts = []
    for r, pack in enumerate((p0, p1, p2, p3)):
        place = pl.multiple_of((me_ref[0] ^ r) * shard, shard)
        copies.append(pltpu.make_async_copy(pack.at[:, 0 : 3 * width], w_ref.at[pl.ds(place, shard), :], sem.at[2 * r]))
        source = pack.at[0:16, 3 * width : 3 * width + shard]
        shorts.append(pltpu.make_async_copy(source, few.at[:, pl.ds(place, shard)], sem.at[2 * r + 1]))

    @pl.when(step == 0)
    def _():
        for copy in shorts + copies:
            copy.start()

    tokens = jnp.where(step == 0, own_ref[...], other_ref[...]).astype(F32)
    unit, _ = spread(tokens)

    @pl.when(step == 0)
    def _():
        for copy in shorts:
            copy.wait()
        small_ref[...] = few[...].astype(F32)

    a1 = (unit * few[0:1, :].astype(F32)).astype(BF16)
    turned_ref[...] = a1.T

    @pl.when(step == 0)
    def _():
        for copy in copies:
            copy.wait()
        q = product(a1, w_ref[:, 0:width]).astype(BF16)
        q_ref[...] = (q.astype(F32) * 0.125).astype(BF16)

    k_ref[...] = product(a1, w_ref[:, width : 2 * width]).astype(BF16)
    v_ref[...] = product(a1, w_ref[:, 2 * width : 3 * width]).astype(BF16)


def project(me, own, others, packs):
    rows, width = own.shape
    steps = 1 + others.shape[0] // rows
    whole = lambda i: (0, 0)
    return pl.pallas_call(
        project_body,
        grid=(steps,),
        in_specs=[
            scalar(),
            pl.BlockSpec((rows, width), whole),
            pl.BlockSpec((rows, width), lambda i: (jnp.maximum(i - 1, 0), 0)),
        ]
        + [in_place()] * 4,
        out_specs=[
            pl.BlockSpec((rows, width), whole),
            pl.BlockSpec((rows, width), lambda i: (i, 0)),
            pl.BlockSpec((rows, width), lambda i: (i, 0)),
            pl.BlockSpec((width, rows), lambda i: (0, i)),
            pl.BlockSpec((width, 3 * width), whole),
            pl.BlockSpec((16, width), whole),
        ],
        out_shape=[
            like((rows, width), BF16),
            like((rows * steps, width), BF16),
            like((rows * steps, width), BF16),
            like((width, rows * steps), BF16),
            like((width, 3 * width), BF16),
            like((16, width), F32),
        ],
        scratch_shapes=[pltpu.VMEM((16, width), BF16), pltpu.SemaphoreType.DMA((8,))],
        compiler_params=params(),
        cost_estimate=pl.CostEstimate(flops=6 * rows * steps * width * width, transcendentals=0, bytes_accessed=6000000),
        name="project",
    )(me, own, others, *packs)


def forward_body(
    rows, small_ref, q_ref, k_ref, v_ref, b_ref, c_ref, o_ref, m_ref, r1_ref, r2_ref, e1_ref, e2_ref, first, second
):
    low_lanes = lax.broadcasted_iota(jnp.int32, (rows, 128), 1) < 64
    values = jnp.concatenate([v_ref[...], jnp.ones(v_ref.shape, BF16)], axis=1)
    items = [(pl.ds(start, rows), side) for start in range(0, q_ref.shape[0], rows) for side in range(2)]

    def scores(n):
        at, side = items[n]
        slope = small_ref[3:4, side : side + 1]
        q_head = jnp.where(low_lanes == (side == 0), q_ref[at, :], 0).astype(BF16)
        raw = product(q_head, k_ref[...], NT)
        first[n % 2] = raw - slope * b_ref[at, :]
        second[n % 2] = raw + c_ref[at, :]
        return [jnp.max(table[n % 2], axis=1, keepdims=True) for table in (first, second)]

    mixed = {}
    peaks = scores(0)
    for n, (at, side) in enumerate(items):
        later = scores(n + 1) if n + 1 < len(items) else None
        for slot, (table, kept_ref) in enumerate(((first, e1_ref), (second, e2_ref))):
            weights = jnp.exp(table[n % 2] - peaks[slot]).astype(BF16)
            kept_ref[side, at, :] = weights
            both = product(weights, values)
            mixed[side, slot] = (both[:, :128], 1.0 / both[:, 128:])
        peaks = later
        if side == 1:
            for slot, value_ref, recip_ref in ((0, o_ref, r1_ref), (1, m_ref, r2_ref)):
                recip = jnp.where(low_lanes, mixed[0, slot][1], mixed[1, slot][1])
                recip_ref[at, :] = recip
                value_ref[at, :] = jnp.where(low_lanes, mixed[0, slot][0], mixed[1, slot][0]) * recip


def attend_forward(small, q, k, v, bias, count):
    row_count, width = q.shape
    key_count = k.shape[0]
    pairs = width // 128
    step_rows = max(64, min(row_count, (512 * 1024) // key_count))
    rows = min(256, step_rows)
    elements = 2 * pairs * row_count * key_count
    own = lambda p, i: (i, p)
    return pl.pallas_call(
        functools.partial(forward_body, rows),
        grid=(pairs, row_count // step_rows),
        in_specs=[
            pl.BlockSpec((16, 128), lambda p, i: (0, p)),
            pl.BlockSpec((step_rows, 128), own),
            pl.BlockSpec((key_count, 128), lambda p, i: (0, p)),
            pl.BlockSpec((key_count, 128), lambda p, i: (0, p)),
            pl.BlockSpec((step_rows, key_count), lambda p, i: (i, 0)),
            pl.BlockSpec((step_rows, key_count), lambda p, i: (i, 0)),
        ],
        out_specs=[pl.BlockSpec((step_rows, 128), own)] * 4
        + [pl.BlockSpec((2, step_rows, key_count), lambda p, i: (p, i, 0))] * 2,
        out_shape=[like((row_count, width), F32)] * 4 + [like((2 * pairs, row_count, key_count), BF16)] * 2,
        scratch_shapes=[pltpu.VMEM((2, rows, key_count), F32)] * 2,
        compiler_params=params(),
        cost_estimate=pl.CostEstimate(
            flops=elements * 64 * 2 * 3, transcendentals=2 * elements, bytes_accessed=4 * elements
        ),
        name="attend_forward",
    )(small, q, k, v, bias, count)


def middle_body(
    slices, me_ref, small_ref, tokens_ref, cot_ref, o_ref, m_ref, p0, p1, p2, p3,
    out_ref, gh1_ref, go_ref, gm_ref, gate_ref, g0, g1, g2, g3, h0, h1_ref, h2_ref, h3,
    w_out, w_memory, w_down, w_up, act, slope, gu, a2_turned, o_turned, m_turned, sem,
):
    rows, width = tokens_ref.shape
    shard = width // 4
    groups = w_down.shape[0] // width
    copies = []
    for r, pack in enumerate((p0, p1, p2, p3)):
        device = me_ref[0] ^ r
        place = pl.ds(pl.multiple_of(device * shard, shard), shard)
        down = pl.ds(pl.multiple_of(device * width, width), width)
        targets = [w_out.at[place], w_memory.at[place]] + [w_up.at[group, place] for group in range(groups)]
        pieces = [(pack.at[n * shard : (n + 1) * shard], target) for n, target in enumerate(targets)]
        pieces.append((pack.at[len(targets) * shard : len(targets) * shard + width], w_down.at[down]))
        copies.append([pltpu.make_async_copy(*piece, sem.at[r, n]) for n, piece in enumerate(pieces)])
    for part in zip(*copies):
        for copy in part:
            copy.start()
    gain = small_ref[1:2, :]
    gate_vec = small_ref[2:3, :]
    o_low = o_ref[...].astype(BF16)
    m_low = m_ref[...].astype(BF16)
    for copy in copies:
        copy[0].wait()
        copy[1].wait()
    h1 = tokens_ref[...].astype(F32) + product(o_low, w_out[...])
    mem = product(m_low, w_memory[...])
    o_turned[...] = o_low.T
    m_turned[...] = m_low.T
    unit, scale = spread(h1)
    a2 = (unit * gain).astype(BF16)
    a2_turned[...] = a2.T
    for copy in copies:
        for piece in copy[2:]:
            piece.wait()
    h2 = h1
    for group in range(groups):
        u = product(a2, w_up[group])
        square = u * u
        bent = jnp.tanh(CURVE * u * (1.0 + CUBIC * square))
        half = 0.5 * (1.0 + bent)
        active = (u * half).astype(BF16)
        slope[group] = half + 0.5 * u * (1.0 - bent * bent) * (CURVE * (1.0 + 3.0 * CUBIC * square))
        act[group] = active.T
        h2 = h2 + product(active, w_down[group * width : (group + 1) * width, :])
    gate = jax.nn.sigmoid(jnp.sum(h2 * gate_vec, axis=1, keepdims=True))
    apart = mem - h2
    out_ref[...] = (h2 + gate * apart).astype(BF16)
    c = cot_ref[...].astype(F32)
    grad_mem = (c * gate).astype(BF16)
    dz = jnp.sum(c * apart, axis=1, keepdims=True) * gate * (1.0 - gate)
    gh2 = c * (1.0 - gate) + dz * gate_vec
    gate_ref[...] = jnp.broadcast_to(jnp.sum(dz * h2, axis=0, keepdims=True), gate_ref.shape)
    gf = gh2.astype(BF16)
    gm_ref[...] = product(grad_mem, w_memory[...], NT).astype(BF16)
    ga2 = None
    for group in range(groups):
        back = product(gf, w_down[group * width : (group + 1) * width, :], NT)
        low = (back * slope[group]).astype(BF16)
        gu[group] = low
        more = product(low, w_up[group], NT)
        ga2 = more if ga2 is None else ga2 + more
    gh1 = gh2 + spread_back(unit, scale, ga2 * gain)
    gh1_ref[...] = gh1
    ga = gh1.astype(BF16)
    go_ref[...] = product(ga, w_out[...], NT).astype(BF16)
    for r, (grad_ref, up_ref) in enumerate(((g0, h0), (g1, h1_ref), (g2, h2_ref), (g3, h3))):
        device = me_ref[0] ^ r
        place = pl.ds(pl.multiple_of(device * shard, shard), shard)
        parts = [product(o_turned[place, :], ga), product(m_turned[place, :], grad_mem), product(act[device], gf)]
        lay_slices(grad_ref, slices, [part.astype(BF16) for part in parts])
        parts = [product(a2_turned[place, :], gu[group]) for group in range(groups)]
        lay_slices(up_ref, slices, [part.astype(BF16) for part in parts])


def lay_slices(target, slices, parts):
    first = 0
    for n in range(slices):
        for part in parts:
            height = part.shape[0] // slices
            target[first : first + height, :] = part[n * height : (n + 1) * height, :]
            first += height


def middle(slices, me, small, tokens, cotangent, o, m, packs, groups):
    rows, width = tokens.shape
    shard = width // 4
    vmem = pl.BlockSpec(memory_space=pltpu.VMEM)
    square = lambda dtype: pltpu.VMEM((width, width), dtype)
    return pl.pallas_call(
        functools.partial(middle_body, slices),
        in_specs=[scalar()] + [vmem] * 5 + [in_place()] * 4,
        out_specs=[vmem] * 13,
        out_shape=[
            like((rows, width), BF16),
            like((rows, width), F32),
            like((rows, width), BF16),
            like((rows, width), BF16),
            like((8, width), F32),
        ]
        + [like((2 * shard + width, width), BF16)] * 4
        + [like((groups * shard, width), BF16)] * 4,
        scratch_shapes=[
            square(BF16),
            square(BF16),
            pltpu.VMEM((groups * width, width), BF16),
            pltpu.VMEM((groups, width, width), BF16),
            pltpu.VMEM((groups, width, rows), BF16),
            pltpu.VMEM((groups, rows, width), F32),
            pltpu.VMEM((groups, rows, width), BF16),
            pltpu.VMEM((width, rows), BF16),
            pltpu.VMEM((width, rows), BF16),
            pltpu.VMEM((width, rows), BF16),
            pltpu.SemaphoreType.DMA((4, 3 + groups)),
        ],
        compiler_params=params(),
        cost_estimate=pl.CostEstimate(
            flops=2 * rows * width * width * 3 * 10, transcendentals=4 * rows * width, bytes_accessed=16000000
        ),
        name="middle",
    )(me, small, tokens, cotangent, o, m, *packs[:3], *on_chip(packs[3]))


def backward_body(
    several, rows, q_ref, k_ref, v_ref, go_ref, gm_ref, o_ref, m_ref, r1_ref, r2_ref, b_ref, e1_ref, e2_ref,
    gq_ref, gk_ref, gv_ref, gs_ref,
):
    low_lanes = lax.broadcasted_iota(jnp.int32, (rows, 128), 1) < 64
    keys = k_ref[...]
    vals = v_ref[...]
    totals = [None, None]
    for start in range(0, q_ref.shape[0], rows):
        at = pl.ds(start, rows)
        g1 = (go_ref[at, :].astype(F32) * r1_ref[at, :]).astype(BF16)
        g2 = (gm_ref[at, :].astype(F32) * r2_ref[at, :]).astype(BF16)
        t1 = g1.astype(F32) * o_ref[at, :]
        t2 = g2.astype(F32) * m_ref[at, :]
        q_turned = q_ref[at, :].T
        g1_turned = g1.T
        g2_turned = g2.T
        grads = []
        for side in range(2):
            mine = low_lanes == (side == 0)
            d1 = jnp.sum(jnp.where(mine, t1, 0.0), axis=1, keepdims=True)
            d2 = jnp.sum(jnp.where(mine, t2, 0.0), axis=1, keepdims=True)
            e1 = e1_ref[side, at, :]
            e2 = e2_ref[side, at, :]
            p1 = product(jnp.where(mine, g1, 0).astype(BF16), vals, NT)
            ds1 = e1.astype(F32) * (p1 - d1)
            slope_term = jnp.sum(ds1 * b_ref[at, :], axis=0, keepdims=True)
            p2 = product(jnp.where(mine, g2, 0).astype(BF16), vals, NT)
            ds = (ds1 + e2.astype(F32) * (p2 - d2)).astype(BF16)
            grads.append(product(ds, keys))
            head = slice(64 * side, 64 * side + 64)
            gk = product(q_turned[head, :], ds)
            gv = product(g1_turned[head, :], e1) + product(g2_turned[head, :], e2)
            if start > 0:
                gk, gv, slope_term = (have + more for have, more in zip(totals[side], (gk, gv, slope_term)))
            totals[side] = (gk, gv, slope_term)
        gq = jnp.where(low_lanes, grads[0], grads[1]) * 0.125
        if not several:
            gq_ref[at, :] = gq.astype(gq_ref.dtype)
        else:
            gq_ref[at, :] = jnp.where(pl.program_id(1) == 0, gq, gq_ref[at, :] + gq)
    gk_ref[...] = jnp.concatenate([totals[0][0], totals[1][0]], axis=0).astype(BF16).T
    gv_ref[...] = jnp.concatenate([totals[0][1], totals[1][1]], axis=0).astype(BF16).T
    for side in range(2):
        term = totals[side][2]
        parts = term[:, 0:128]
        for first in range(128, term.shape[1], 128):
            parts = parts + term[:, first : first + 128]
        if not several:
            gs_ref[side : side + 1, :] = parts
        else:
            gs_ref[side : side + 1, :] = jnp.where(pl.program_id(1) == 0, parts, gs_ref[side : side + 1, :] + parts)


def attend_backward(q, k, v, go, gm, saved, bias, first, pairs):
    o, m, r1, r2, e1, e2 = saved
    row_count = q.shape[0]
    key_count = k.shape[0]
    step_keys = min(1024, key_count)
    several = key_count > step_keys
    elements = 2 * pairs * row_count * key_count
    wide = pl.BlockSpec((row_count, 128), lambda p, c: (0, p + first))
    near = pl.BlockSpec((step_keys, 128), lambda p, c: (c, p + first))
    table = pl.BlockSpec((2, row_count, step_keys), lambda p, c: (p + first, 0, c))
    own = pl.BlockSpec((step_keys, 128), lambda p, c: (c, p))
    return pl.pallas_call(
        functools.partial(backward_body, several, 256),
        grid=(pairs, key_count // step_keys),
        in_specs=[wide, near, near, wide, wide, wide, wide, wide, wide]
        + [pl.BlockSpec((row_count, step_keys), lambda p, c: (0, c)), table, table],
        out_specs=[
            pl.BlockSpec((row_count, 128), lambda p, c: (0, p)),
            own,
            own,
            pl.BlockSpec((None, 8, 128), lambda p, c: (p, 0, 0)),
        ],
        out_shape=[
            like((row_count, 128 * pairs), F32 if several else BF16),
            like((key_count, 128 * pairs), BF16),
            like((key_count, 128 * pairs), BF16),
            like((pairs, 8, 128), F32),
        ],
        compiler_params=params(),
        cost_estimate=pl.CostEstimate(flops=elements * 64 * 2 * 6, transcendentals=0, bytes_accessed=4 * elements),
        name="attend_backward",
    )(q, k, v, go, gm, o, m, r1, r2, bias, e1, e2)


def weights_body(me_ref, turned_ref, gq_ref, gk_ref, gv_ref, gs_ref, gate_ref, *grad_refs):
    rows, width = gq_ref.shape
    shard = width // 4
    lane = lax.broadcasted_iota(jnp.int32, (16, shard), 1)
    row = lax.broadcasted_iota(jnp.int32, (16, shard), 0)
    for r in range(4):
        grad_ref = grad_refs[r]
        device = me_ref[0] ^ r
        start = pl.multiple_of(device * shard, shard)
        a1 = turned_ref[pl.ds(start, shard), :]
        grad_ref[:, 0:width] = product(a1[:, 0:rows], gq_ref[...].astype(BF16)).astype(BF16)
        grad_ref[:, width : 2 * width] = product(a1, gk_ref[...]).astype(BF16)
        grad_ref[:, 2 * width : 3 * width] = product(a1, gv_ref[...]).astype(BF16)
        sums = -jnp.sum(gs_ref[device, 0:2, :], axis=1, keepdims=True)
        block = jnp.where((row == 0) & (lane == 0), sums[0:1, :], 0.0)
        block = jnp.where((row == 0) & (lane == 1), sums[1:2, :], block)
        block = jnp.where(row == 1, gate_ref[0:1, pl.ds(start, shard)], block)
        grad_ref[:, 3 * width : 3 * width + shard] = jnp.zeros((shard, shard), BF16)
        grad_ref[0:16, 3 * width : 3 * width + shard] = block.astype(BF16)


def weight_grads(me, turned, gq, gk, gv, gs, gate):
    rows, width = gq.shape
    shard = width // 4
    vmem = pl.BlockSpec(memory_space=pltpu.VMEM)
    return pl.pallas_call(
        weights_body,
        in_specs=[scalar()] + [vmem] * 6,
        out_specs=[vmem] * 4,
        out_shape=[like((shard, 3 * width + shard), BF16)] * 4,
        compiler_params=params(),
        cost_estimate=pl.CostEstimate(
            flops=6 * gk.shape[0] * width * width, transcendentals=0, bytes_accessed=6000000
        ),
        name="weight_grads",
    )(me, turned, gq, gk, gv, gs, gate)


def rows_body(gq_ref, gk_ref, gv_ref, w_ref, near_ref, own_ref):
    rows, width = gq_ref.shape
    w_k = w_ref[:, width : 2 * width]
    w_v = w_ref[:, 2 * width : 3 * width]
    for first in range(rows, gk_ref.shape[0], rows):
        at = slice(first, first + rows)
        part = product(gk_ref[at, :], w_k, NT) + product(gv_ref[at, :], w_v, NT)
        near_ref[first - rows : first, :] = part.astype(BF16)
    own = product(gq_ref[...].astype(BF16), w_ref[:, 0:width], NT)
    own_ref[...] = own + product(gk_ref[0:rows, :], w_k, NT) + product(gv_ref[0:rows, :], w_v, NT)


def row_grads(gq, gk, gv, w):
    rows, width = gq.shape
    vmem = pl.BlockSpec(memory_space=pltpu.VMEM)
    return pl.pallas_call(
        rows_body,
        in_specs=[vmem] * 4,
        out_specs=[vmem] * 2,
        out_shape=[like((gk.shape[0] - rows, width), BF16), like((rows, width), F32)],
        compiler_params=params(),
        cost_estimate=pl.CostEstimate(
            flops=6 * gk.shape[0] * width * width, transcendentals=0, bytes_accessed=6000000
        ),
        name="row_grads",
    )(gq, gk, gv, w)


def row_sums(table, weight_ref, gain_ref):
    ones = jnp.ones((8, table.shape[1]), F32)
    sums = lax.dot_general(
        ones, table * weight_ref[...].astype(F32), NT, precision=lax.Precision.HIGHEST, preferred_element_type=F32
    )
    return sums[0:1, :] / gain_ref[...].astype(F32)


def assemble_body(
    near_ref, far_ref, own_a, own_b, other_a, by_ctx, by_seq, up_w_ref, gain_ref, out_ref, memory_ref, down_ref, up_ref, sum_ref
):
    width = out_ref.shape[1]
    groups = up_ref.shape[1] // width
    short = out_ref.shape[0] // 8
    tall = down_ref.shape[0] // 8
    size = own_a.shape[0] // 2
    for n, (part_ref, first_part) in enumerate(((own_a, 0), (own_b, 0), (other_a, 0), (by_ctx, 0), (by_seq, 1))):
        side = near_ref[0] if n < 2 else 1 - near_ref[0]
        pair = far_ref[0] if n % 2 == 0 and n < 4 else 1 - far_ref[0]
        for p in range(part_ref.shape[0] // size):
            place = 4 * side + 2 * pair + first_part + p
            at = pl.ds(pl.multiple_of(place * short, short), short)
            piece = part_ref[p * size : (p + 1) * size, :].astype(F32)
            out_ref[at, :] = piece[0:short, :]
            memory_ref[at, :] = piece[short : 2 * short, :]
            down_ref[pl.ds(pl.multiple_of(place * tall, tall), tall), :] = piece[2 * short : 2 * short + tall, :]
            for group in range(groups):
                first = 2 * short + tall + group * short
                up_ref[at, group * width : (group + 1) * width] = piece[first : first + short, :]
    sum_ref[...] = row_sums(up_ref[...], up_w_ref, gain_ref)


def assemble(near, far, parts, w_up, gain):
    width = parts[0].shape[1]
    shard, columns = w_up.shape
    vmem = pl.BlockSpec(memory_space=pltpu.VMEM)
    return pl.pallas_call(
        assemble_body,
        in_specs=[scalar(), scalar()] + [vmem] * 7,
        out_specs=[vmem] * 5,
        out_shape=[like((shard, width), F32)] * 2
        + [like((width, width), F32), like((shard, columns), F32), like((1, shard), F32)],
        compiler_params=params(),
        cost_estimate=pl.CostEstimate(flops=0, transcendentals=0, bytes_accessed=4000000),
        name="assemble",
    )(near, far, *on_chip(*parts), w_up, gain[None])


def close_body(near_ref, own_ref, other_ref, w_ref, gain_ref, qkv_ref, gain_sum_ref, gate_ref, slope_ref):
    half = own_ref.shape[0]
    wide = qkv_ref.shape[1]
    for n, part_ref in enumerate((own_ref, other_ref)):
        side = near_ref[0] if n == 0 else 1 - near_ref[0]
        qkv_ref[pl.ds(pl.multiple_of(side * half, half), half), :] = part_ref[:, 0:wide].astype(F32)
    first = jnp.where(near_ref[0] == 0, own_ref[0:16, wide:].astype(F32), other_ref[0:16, wide:].astype(F32))
    slope_ref[...] = first[0:1, 0 : slope_ref.shape[1]]
    gate_ref[...] = first[1:2, :]
    gain_sum_ref[...] = row_sums(qkv_ref[...], w_ref, gain_ref)


def close(near, own, other, w_qkv, gain, heads):
    shard, wide = w_qkv.shape
    vmem = pl.BlockSpec(memory_space=pltpu.VMEM)
    return pl.pallas_call(
        close_body,
        in_specs=[scalar()] + [vmem] * 4,
        out_specs=[vmem] * 4,
        out_shape=[like((shard, wide), F32), like((1, shard), F32), like((1, shard), F32), like((1, heads), F32)],
        compiler_params=params(),
        cost_estimate=pl.CostEstimate(flops=0, transcendentals=0, bytes_accessed=2000000),
        name="close",
    )(near, *on_chip(own, other), w_qkv, gain[None])


def finish_body(tokens_ref, small_ref, gh1_ref, own_ref, away_ref, out_ref):
    unit, scale = spread(tokens_ref[...].astype(F32))
    grad = (own_ref[...] + away_ref[...].astype(F32)) * small_ref[0:1, :]
    out_ref[...] = gh1_ref[...] + spread_back(unit, scale, grad)


def finish(tokens, small, gh1, own, away):
    vmem = pl.BlockSpec(memory_space=pltpu.VMEM)
    return pl.pallas_call(
        finish_body,
        in_specs=[vmem] * 5,
        out_specs=vmem,
        out_shape=like(gh1.shape, F32),
        compiler_params=params(),
        cost_estimate=pl.CostEstimate(flops=0, transcendentals=0, bytes_accessed=4000000),
        name="finish",
    )(tokens, small, gh1, own, *on_chip(away))


def on_device(
    tokens, cotangent, deal, memory_len, neighbours,
    w_qkv, w_out, w_up, w_down, w_memory, gain_attn, gain_ffn, gate_vec, slopes,
):
    _, row_count, width = tokens.shape
    tokens = tokens.reshape(row_count, width)
    cotangent = cotangent.reshape(row_count, width)
    neighbours = neighbours.reshape(row_count, -1)
    block_count = deal.shape[0]
    ctx_size = lax.axis_size("ctx")
    own_blocks = block_count // ctx_size
    block_len = row_count // own_blocks
    shard = gain_attn.shape[0]
    heads_here = slopes.shape[0]
    groups = w_up.shape[1] // width
    me = lax.axis_index("wt").astype(jnp.int32).reshape(1)
    fast = ctx_size == 2 and lax.axis_size("seq") == 4
    slices = 8 if fast else 1

    short = jnp.concatenate(
        [gain_attn[None], gain_ffn[None], gate_vec[None], jnp.pad(slopes, (0, shard - heads_here))[None]], axis=0
    )
    pack = jnp.concatenate([w_qkv, jnp.pad(short, ((0, shard - 4), (0, 0)))], axis=1)
    others = swap(tokens, "ctx", 1)
    for bit in bits_of("ctx")[1:]:
        both = jnp.concatenate([tokens, others], axis=0)
        others = jnp.concatenate([others, swap(both, "ctx", bit)], axis=0)
    pack_far = swap(pack, "wt", 2)
    pack_near = swap(pack, "wt", 1)
    wide = lay_rows(width, [(w_out, 0), (w_memory, 0)] + [(w_up, width * g) for g in range(groups)] + [(w_down, 0)])
    neighbours = hold(neighbours, wide)

    offsets = jnp.arange(block_len, dtype=jnp.int32)
    owners = lax.axis_index("ctx") ^ jnp.arange(ctx_size, dtype=jnp.int32)
    slots = (owners[:, None] * own_blocks + jnp.arange(own_blocks, dtype=jnp.int32)[None, :]).reshape(-1)
    block_ids = jnp.arange(block_count, dtype=jnp.int32)
    slot_hot = (slots[:, None] == block_ids[None, :]).astype(jnp.int32)
    key_blocks = jnp.sum(slot_hot * deal[None, :], axis=1)
    key_pos = (key_blocks[:, None] * block_len + offsets[None, :]).reshape(-1)
    my_blocks = key_blocks[:own_blocks]
    row_pos = key_pos[:row_count]
    memory_hot = (my_blocks[:, None] == block_ids[None, :]).astype(jnp.int32)
    my_memory = jnp.sum(memory_hot * memory_len, axis=1)
    row_start = jnp.repeat(my_blocks * block_len, block_len)
    row_low = row_start - jnp.repeat(my_memory, block_len)
    picks = neighbours.shape[1]
    hits = sum((neighbours[:, n : n + 1] == key_pos[None, :]).astype(F32) for n in range(picks))
    count = jnp.where(hits == 1.0, 0.0, ABSENT)
    for times in range(2, picks + 1):
        count = jnp.where(hits == float(times), math.log(times), count)
    pack_far, wide = lax.optimization_barrier((pack_far, wide, count))[:2]
    pack_both = swap(pack_far, "wt", 1)
    wide_far = swap(wide, "wt", 2)
    wide_near = swap(wide, "wt", 1)
    row_pos = hold(row_pos, pack_far)
    distance = jnp.log(jnp.abs(row_pos[:, None] - key_pos[None, :]).astype(F32) + 1.0)
    visible = (key_pos[None, :] >= row_low[:, None]) & (key_pos[None, :] < (row_start + block_len)[:, None])
    bias = jnp.where(visible, distance, HIDDEN)

    q, k, v, turned, full_qkv, small = project(
        me, tokens, hold(others, bias), (pack, pack_near, pack_far, pack_both)
    )
    saved = attend_forward(small, q, k, v, bias, count)
    wide_both = swap(hold(wide_far, saved[0]), "wt", 1)
    wides = (wide, wide_near, wide_far, wide_both)
    layer_out, gh1, go, gm, gate, g0, g1, g2, g3, h0, h1, h2, h3 = middle(
        slices, me, small, tokens, cotangent, saved[0], saved[1], wides, groups
    )

    all_pairs = width // 128
    g_far = add_low(g2, swap(g3, "wt", 1))
    g_one = swap(g1, "wt", 1)
    if fast:
        h_far = add_low(h2, swap(h3, "wt", 1))
        h_own = add_low(h0, swap(h1, "wt", 1))
        g_got = swap(g_far, "wt", 2)
        far_keep, far_got = send_half(h_far, "ctx", 1)
        own_keep, own_got = send_half(h_own, "ctx", 1)
        gq, gk, gv, gs = attend_backward(q, k, v, hold(go, g_far, h_far, h_own), gm, saved, bias, 0, all_pairs)
        gq, gk, gv, gs, g_got, far_got, own_got = lax.optimization_barrier(
            (gq, gk, gv, gs, g_got, far_got, own_got)
        )
        h_got = swap(add_low(far_keep, far_got), "wt", 2)
        g_keep, g_near = send_half(add_all(g0, [g_one, g_got]), "ctx", 1)
        q0, q1, q2, q3 = weight_grads(me, turned, hold(gq, g_keep), gk, gv, gs, gate)
        q_three, q_one = swap(q3, "wt", 1), swap(q1, "wt", 1)
        gq, q0, q2, g_near, h_got = lax.optimization_barrier((gq, q0, q2, g_near, h_got))
        q_far = add_low(q2, q_three)
        lower = add_low(g_keep, g_near).reshape(4, -1, width)
        higher = add_all(own_keep, [own_got, h_got]).reshape(4, -1, width)
        gh_keep, gh_got = send_half(jnp.concatenate([lower, higher], axis=1).reshape(-1, width), "seq", 1)
        near, own = row_grads(hold(gq, q_far, gh_keep), gk, gv, full_qkv)
        q_far = swap(q_far, "wt", 2)
        order = Order()
        near, gh_got = order.arrive(near, gh_got)
        gh = add_low(gh_keep, gh_got)
        gh_got = swap(gh, "seq", 2)
        q_keep, q_got = send_half(add_all(q0, [q_one, order.arrive(q_far)]), "ctx", 1)
        q_sum = add_low(q_keep, order.arrive(q_got))
        q_got = swap(q_sum, "seq", 1)
        away = swap(hold(near, q_sum), "ctx", 1)
        q_sum = add_low(q_sum, order.arrive(q_got))
        q_got = swap(q_sum, "seq", 2)
        own_a = add_low(gh, order.arrive(gh_got))
        own_b = swap(own_a, "seq", 1)
        other_a = swap(own_a, "ctx", 1)
        away = order.arrive(away)
        grad_tokens = finish(tokens, small, gh1, own, away)
        order.before = (grad_tokens,)
        q_sum = add_low(q_sum, order.arrive(q_got))
        q_other = swap(q_sum, "ctx", 1)
        own_b = order.arrive(own_b)
        other_a = order.arrive(other_a)
        cut = own_b.shape[0] // 2
        by_seq = swap(other_a[cut:], "seq", 1)
        by_ctx = swap(own_b[:cut], "ctx", 1)
        side = lax.axis_index("ctx").astype(jnp.int32).reshape(1)
        pair = side_of("seq", 1).astype(jnp.int32).reshape(1)
        by_seq = order.arrive(by_seq)
        t_qkv, *shorts = close(side, q_sum, order.arrive(q_other), w_qkv, gain_attn, heads_here)
        order.before = (t_qkv,)
        by_ctx = order.arrive(by_ctx)
        t_out, t_memory, t_down, t_up, t_gain_two = assemble(
            side, pair, (own_a, own_b, other_a, by_ctx, by_seq), w_up, gain_ffn
        )
        t_gain_one, t_gate, t_slopes, t_gain_two = (value.reshape(-1) for value in (*shorts, t_gain_two))
    else:
        h_far = add_low(h2, swap(h3, "wt", 1))
        h_one = swap(h1, "wt", 1)
        g_sum = add_all(g0, [g_one, swap(g_far, "wt", 2)])
        h_sum = add_all(h0, [h_one, swap(h_far, "wt", 2)])
        gq, gk, gv, gs = attend_backward(q, k, v, go, gm, saved, bias, 0, all_pairs)
        grads = weight_grads(me, turned, gq, gk, gv, gs, gate)
        near, own = row_grads(gq, gk, gv, full_qkv)
        for bit in reversed(bits_of("ctx")[1:]):
            both = jnp.concatenate([own.astype(BF16), near], axis=0)
            fold = bit * row_count
            folded = both[:fold].astype(F32) + swap(both[fold:], "ctx", bit).astype(F32)
            own, near = folded[:row_count], folded[row_count:].astype(BF16)
        away = swap(near, "ctx", 1)
        q_far = swap(add_low(grads[2], swap(grads[3], "wt", 1)), "wt", 2)
        q_sum = add_all(grads[0], [swap(grads[1], "wt", 1), q_far])
        q_sum = near_whole(far_both(near_halves(q_sum)))
        g_sum = near_whole(far_whole(far_halves(near_halves(g_sum))))
        h_sum = near_whole(far_whole(far_halves(near_halves(h_sum))))
        grad_tokens = finish(tokens, small, gh1, own, away)
        t_out = g_sum[:shard].astype(F32)
        t_memory = g_sum[shard : 2 * shard].astype(F32)
        t_down = g_sum[2 * shard : 2 * shard + width].astype(F32)
        t_up = jnp.concatenate([h_sum[shard * g : shard * (g + 1)] for g in range(groups)], axis=1).astype(F32)
        t_qkv = q_sum[:, : 3 * width].astype(F32)
        t_slopes = q_sum[0, 3 * width : 3 * width + heads_here].astype(F32)
        t_gate = q_sum[1, 3 * width : 3 * width + shard].astype(F32)
        t_gain_one = jnp.sum(t_qkv * w_qkv.astype(F32), axis=1) / gain_attn.astype(F32)
        t_gain_two = jnp.sum(t_up * w_up.astype(F32), axis=1) / gain_ffn.astype(F32)


    return (
        layer_out[None], grad_tokens[None], t_qkv, t_out, t_up, t_down, t_memory,
        t_gain_one, t_gain_two, t_gate, t_slopes,
    )


def solution(mesh):
    rows = P(("seq", "wt"), "ctx", None)
    weight = P("wt", None)
    vector = P("wt")
    return jax.shard_map(
        on_device,
        mesh=mesh,
        in_specs=(rows, rows, P(), P(("seq", "wt"), None), rows) + (weight,) * 5 + (vector,) * 4,
        out_specs=(rows, rows) + (weight,) * 5 + (vector,) * 4,
        check_vma=False,
    )
```

```python
import functools
import math
import jax
import jax.numpy as jnp
from jax import lax
from jax.experimental import pallas as pl
from jax.experimental.pallas import tpu as pltpu
from jax.sharding import PartitionSpec as P

EPSILON = 1e-05
F32 = jnp.float32
BF16 = jnp.bfloat16
NT = (((1,), (1,)), ((), ()))
NN = (((1,), (0,)), ((), ()))
HIDDEN = 1e12
ABSENT = -1e30
VMEM = 56 * 1024 * 1024
CURVE = math.sqrt(2.0 / math.pi)
CUBIC = 0.044715


def product(left, right, dims=NN):
    return lax.dot_general(left, right, dims, preferred_element_type=F32)


def params(limit=VMEM):
    return pltpu.CompilerParams(vmem_limit_bytes=limit)


def like(shape, dtype):
    return jax.ShapeDtypeStruct(shape, dtype)


def in_place():
    return pl.BlockSpec(memory_space=pl.ANY)


def on_chip(*values):
    return [pltpu.with_memory_space_constraint(value, pltpu.VMEM) for value in values]


def scalar():
    return pl.BlockSpec(memory_space=pltpu.SMEM)


def swap(value, axis, bit):
    size = lax.axis_size(axis)
    return lax.ppermute(value, axis, [(i, i ^ bit) for i in range(size)])


def bits_of(axis):
    bits = []
    bit = 1
    while bit < lax.axis_size(axis):
        bits.append(bit)
        bit *= 2
    return bits


def side_of(axis, bit):
    return (lax.axis_index(axis) // bit) % 2


def hold(value, *before):
    return lax.optimization_barrier((value,) + before)[0]


class Order:
    def __init__(self):
        self.before = ()

    def arrive(self, *values):
        held = lax.optimization_barrier(values + self.before)[: len(values)]
        self.before = held[:1]
        return held if len(held) > 1 else held[0]


def send_half(part, axis, bit):
    side = side_of(axis, bit)
    both = part.reshape((2, part.shape[0] // 2) + part.shape[1:])
    got = swap(lax.dynamic_index_in_dim(both, 1 - side, 0, False), axis, bit)
    return lax.dynamic_index_in_dim(both, side, 0, False), got


def place_half(part, other, axis, bit):
    high = side_of(axis, bit) == 1
    return jnp.concatenate([jnp.where(high, other, part), jnp.where(high, part, other)], axis=0)


def add_all(own, got):
    total = own.astype(F32)
    for value in got:
        total = total + value.astype(F32)
    return total.astype(BF16)


def add_low(left, right):
    return (left.astype(F32) + right.astype(F32)).astype(BF16)


def halve(part, axis, bit):
    side = side_of(axis, bit)
    both = part.reshape((2, part.shape[0] // 2) + part.shape[1:])
    got = swap(lax.dynamic_index_in_dim(both, 1 - side, 0, False), axis, bit)
    return add_low(lax.dynamic_index_in_dim(both, side, 0, False), got)


def widen(part, axis, bit):
    other = swap(part, axis, bit)
    high = side_of(axis, bit) == 1
    return jnp.concatenate([jnp.where(high, other, part), jnp.where(high, part, other)], axis=0)


def near_halves(part):
    for bit in bits_of("ctx"):
        part = halve(part, "ctx", bit)
    return part


def near_whole(part):
    for bit in reversed(bits_of("ctx")):
        part = widen(part, "ctx", bit)
    return part


def far_halves(part):
    for bit in bits_of("seq"):
        part = halve(part, "seq", bit)
    return part


def far_whole(part):
    for bit in reversed(bits_of("seq")):
        part = widen(part, "seq", bit)
    return part


def far_both(part):
    for bit in bits_of("seq"):
        part = add_low(part, swap(part, "seq", bit))
    return part


def spread(values):
    centred = values - jnp.mean(values, axis=-1, keepdims=True)
    scale = lax.rsqrt(jnp.mean(centred * centred, axis=-1, keepdims=True) + EPSILON)
    return centred * scale, scale


def spread_back(unit, scale, grad):
    along = jnp.mean(grad * unit, axis=-1, keepdims=True)
    return scale * (grad - jnp.mean(grad, axis=-1, keepdims=True) - unit * along)


def lay_rows(width, pieces):
    arrays = [piece[0] for piece in pieces]
    total = sum(array.shape[0] for array in arrays)

    def body(*refs):
        target, sem = refs[len(pieces) :]
        copies = []
        first = 0
        for n, (ref, (_, col)) in enumerate(zip(refs, pieces)):
            source = ref.at[:, col : col + width]
            copies.append(pltpu.make_async_copy(source, target.at[first : first + ref.shape[0]], sem.at[n]))
            first += ref.shape[0]
        for copy in copies:
            copy.start()
        for copy in copies:
            copy.wait()

    vmem = pl.BlockSpec(memory_space=pltpu.VMEM)
    return pl.pallas_call(
        body,
        in_specs=[vmem] * len(arrays),
        out_specs=in_place(),
        out_shape=like((total, width), BF16),
        scratch_shapes=[pltpu.SemaphoreType.DMA((len(arrays),))],
        compiler_params=params(),
        cost_estimate=pl.CostEstimate(flops=0, transcendentals=0, bytes_accessed=4 * total * width),
        name="lay_rows",
    )(*arrays)


def project_body(me_ref, own_ref, other_ref, p0, p1, p2, p3, q_ref, k_ref, v_ref, turned_ref, w_ref, small_ref, few, sem):
    step = pl.program_id(0)
    width = own_ref.shape[1]
    shard = p0.shape[0]

    copies = []
    shorts = []
    for r, pack in enumerate((p0, p1, p2, p3)):
        place = pl.multiple_of((me_ref[0] ^ r) * shard, shard)
        copies.append(pltpu.make_async_copy(pack.at[:, 0 : 3 * width], w_ref.at[pl.ds(place, shard), :], sem.at[2 * r]))
        source = pack.at[0:16, 3 * width : 3 * width + shard]
        shorts.append(pltpu.make_async_copy(source, few.at[:, pl.ds(place, shard)], sem.at[2 * r + 1]))

    @pl.when(step == 0)
    def _():
        for copy in shorts + copies:
            copy.start()

    tokens = jnp.where(step == 0, own_ref[...], other_ref[...]).astype(F32)
    unit, _ = spread(tokens)

    @pl.when(step == 0)
    def _():
        for copy in shorts:
            copy.wait()
        small_ref[...] = few[...].astype(F32)

    a1 = (unit * few[0:1, :].astype(F32)).astype(BF16)
    turned_ref[...] = a1.T

    @pl.when(step == 0)
    def _():
        for copy in copies:
            copy.wait()
        q = product(a1, w_ref[:, 0:width]).astype(BF16)
        q_ref[...] = (q.astype(F32) * 0.125).astype(BF16)

    k_ref[...] = product(a1, w_ref[:, width : 2 * width]).astype(BF16)
    v_ref[...] = product(a1, w_ref[:, 2 * width : 3 * width]).astype(BF16)


def project(me, own, others, packs):
    rows, width = own.shape
    steps = 1 + others.shape[0] // rows
    whole = lambda i: (0, 0)
    return pl.pallas_call(
        project_body,
        grid=(steps,),
        in_specs=[
            scalar(),
            pl.BlockSpec((rows, width), whole),
            pl.BlockSpec((rows, width), lambda i: (jnp.maximum(i - 1, 0), 0)),
        ]
        + [in_place()] * 4,
        out_specs=[
            pl.BlockSpec((rows, width), whole),
            pl.BlockSpec((rows, width), lambda i: (i, 0)),
            pl.BlockSpec((rows, width), lambda i: (i, 0)),
            pl.BlockSpec((width, rows), lambda i: (0, i)),
            pl.BlockSpec((width, 3 * width), whole),
            pl.BlockSpec((16, width), whole),
        ],
        out_shape=[
            like((rows, width), BF16),
            like((rows * steps, width), BF16),
            like((rows * steps, width), BF16),
            like((width, rows * steps), BF16),
            like((width, 3 * width), BF16),
            like((16, width), F32),
        ],
        scratch_shapes=[pltpu.VMEM((16, width), BF16), pltpu.SemaphoreType.DMA((8,))],
        compiler_params=params(),
        cost_estimate=pl.CostEstimate(flops=6 * rows * steps * width * width, transcendentals=0, bytes_accessed=6000000),
        name="project",
    )(me, own, others, *packs)


def forward_body(
    rows, small_ref, q_ref, k_ref, v_ref, b_ref, c_ref, o_ref, m_ref, r1_ref, r2_ref, e1_ref, e2_ref, first, second
):
    low_lanes = lax.broadcasted_iota(jnp.int32, (rows, 128), 1) < 64
    values = jnp.concatenate([v_ref[...], jnp.ones(v_ref.shape, BF16)], axis=1)
    items = [(pl.ds(start, rows), side) for start in range(0, q_ref.shape[0], rows) for side in range(2)]

    def scores(n):
        at, side = items[n]
        slope = small_ref[3:4, side : side + 1]
        q_head = jnp.where(low_lanes == (side == 0), q_ref[at, :], 0).astype(BF16)
        raw = product(q_head, k_ref[...], NT)
        first[n % 2] = raw - slope * b_ref[at, :]
        second[n % 2] = raw + c_ref[at, :]
        return [jnp.max(table[n % 2], axis=1, keepdims=True) for table in (first, second)]

    mixed = {}
    peaks = scores(0)
    for n, (at, side) in enumerate(items):
        later = scores(n + 1) if n + 1 < len(items) else None
        for slot, (table, kept_ref) in enumerate(((first, e1_ref), (second, e2_ref))):
            weights = jnp.exp(table[n % 2] - peaks[slot]).astype(BF16)
            kept_ref[side, at, :] = weights
            both = product(weights, values)
            mixed[side, slot] = (both[:, :128], 1.0 / both[:, 128:])
        peaks = later
        if side == 1:
            for slot, value_ref, recip_ref in ((0, o_ref, r1_ref), (1, m_ref, r2_ref)):
                recip = jnp.where(low_lanes, mixed[0, slot][1], mixed[1, slot][1])
                recip_ref[at, :] = recip
                value_ref[at, :] = jnp.where(low_lanes, mixed[0, slot][0], mixed[1, slot][0]) * recip


def attend_forward(small, q, k, v, bias, count):
    row_count, width = q.shape
    key_count = k.shape[0]
    pairs = width // 128
    step_rows = max(64, min(row_count, (512 * 1024) // key_count))
    rows = min(256, step_rows)
    elements = 2 * pairs * row_count * key_count
    own = lambda p, i: (i, p)
    return pl.pallas_call(
        functools.partial(forward_body, rows),
        grid=(pairs, row_count // step_rows),
        in_specs=[
            pl.BlockSpec((16, 128), lambda p, i: (0, p)),
            pl.BlockSpec((step_rows, 128), own),
            pl.BlockSpec((key_count, 128), lambda p, i: (0, p)),
            pl.BlockSpec((key_count, 128), lambda p, i: (0, p)),
            pl.BlockSpec((step_rows, key_count), lambda p, i: (i, 0)),
            pl.BlockSpec((step_rows, key_count), lambda p, i: (i, 0)),
        ],
        out_specs=[pl.BlockSpec((step_rows, 128), own)] * 4
        + [pl.BlockSpec((2, step_rows, key_count), lambda p, i: (p, i, 0))] * 2,
        out_shape=[like((row_count, width), F32)] * 4 + [like((2 * pairs, row_count, key_count), BF16)] * 2,
        scratch_shapes=[pltpu.VMEM((2, rows, key_count), F32)] * 2,
        compiler_params=params(),
        cost_estimate=pl.CostEstimate(
            flops=elements * 64 * 2 * 3, transcendentals=2 * elements, bytes_accessed=4 * elements
        ),
        name="attend_forward",
    )(small, q, k, v, bias, count)


def middle_body(
    slices, me_ref, small_ref, tokens_ref, cot_ref, o_ref, m_ref, p0, p1, p2, p3,
    out_ref, gh1_ref, go_ref, gm_ref, gate_ref, g0, g1, g2, g3, h0, h1_ref, h2_ref, h3,
    w_out, w_memory, w_down, w_up, act, slope, gu, a2_turned, o_turned, m_turned, sem,
):
    rows, width = tokens_ref.shape
    shard = width // 4
    groups = w_down.shape[0] // width
    copies = []
    for r, pack in enumerate((p0, p1, p2, p3)):
        device = me_ref[0] ^ r
        place = pl.ds(pl.multiple_of(device * shard, shard), shard)
        down = pl.ds(pl.multiple_of(device * width, width), width)
        targets = [w_out.at[place], w_memory.at[place]] + [w_up.at[group, place] for group in range(groups)]
        pieces = [(pack.at[n * shard : (n + 1) * shard], target) for n, target in enumerate(targets)]
        pieces.append((pack.at[len(targets) * shard : len(targets) * shard + width], w_down.at[down]))
        copies.append([pltpu.make_async_copy(*piece, sem.at[r, n]) for n, piece in enumerate(pieces)])
    for part in zip(*copies):
        for copy in part:
            copy.start()
    gain = small_ref[1:2, :]
    gate_vec = small_ref[2:3, :]
    o_low = o_ref[...].astype(BF16)
    m_low = m_ref[...].astype(BF16)
    for copy in copies:
        copy[0].wait()
        copy[1].wait()
    h1 = tokens_ref[...].astype(F32) + product(o_low, w_out[...])
    mem = product(m_low, w_memory[...])
    o_turned[...] = o_low.T
    m_turned[...] = m_low.T
    unit, scale = spread(h1)
    a2 = (unit * gain).astype(BF16)
    a2_turned[...] = a2.T
    for copy in copies:
        for piece in copy[2:]:
            piece.wait()
    h2 = h1
    for group in range(groups):
        u = product(a2, w_up[group])
        square = u * u
        bent = jnp.tanh(CURVE * u * (1.0 + CUBIC * square))
        half = 0.5 * (1.0 + bent)
        active = (u * half).astype(BF16)
        slope[group] = half + 0.5 * u * (1.0 - bent * bent) * (CURVE * (1.0 + 3.0 * CUBIC * square))
        act[group] = active.T
        h2 = h2 + product(active, w_down[group * width : (group + 1) * width, :])
    gate = jax.nn.sigmoid(jnp.sum(h2 * gate_vec, axis=1, keepdims=True))
    apart = mem - h2
    out_ref[...] = (h2 + gate * apart).astype(BF16)
    c = cot_ref[...].astype(F32)
    grad_mem = (c * gate).astype(BF16)
    dz = jnp.sum(c * apart, axis=1, keepdims=True) * gate * (1.0 - gate)
    gh2 = c * (1.0 - gate) + dz * gate_vec
    gate_ref[...] = jnp.broadcast_to(jnp.sum(dz * h2, axis=0, keepdims=True), gate_ref.shape)
    gf = gh2.astype(BF16)
    gm_ref[...] = product(grad_mem, w_memory[...], NT).astype(BF16)
    ga2 = None
    for group in range(groups):
        back = product(gf, w_down[group * width : (group + 1) * width, :], NT)
        low = (back * slope[group]).astype(BF16)
        gu[group] = low
        more = product(low, w_up[group], NT)
        ga2 = more if ga2 is None else ga2 + more
    gh1 = gh2 + spread_back(unit, scale, ga2 * gain)
    gh1_ref[...] = gh1
    ga = gh1.astype(BF16)
    go_ref[...] = product(ga, w_out[...], NT).astype(BF16)
    for r, (grad_ref, up_ref) in enumerate(((g0, h0), (g1, h1_ref), (g2, h2_ref), (g3, h3))):
        device = me_ref[0] ^ r
        place = pl.ds(pl.multiple_of(device * shard, shard), shard)
        parts = [product(o_turned[place, :], ga), product(m_turned[place, :], grad_mem), product(act[device], gf)]
        lay_slices(grad_ref, slices, [part.astype(BF16) for part in parts])
        parts = [product(a2_turned[place, :], gu[group]) for group in range(groups)]
        lay_slices(up_ref, slices, [part.astype(BF16) for part in parts])


def lay_slices(target, slices, parts):
    first = 0
    for n in range(slices):
        for part in parts:
            height = part.shape[0] // slices
            target[first : first + height, :] = part[n * height : (n + 1) * height, :]
            first += height


def middle(slices, me, small, tokens, cotangent, o, m, packs, groups):
    rows, width = tokens.shape
    shard = width // 4
    vmem = pl.BlockSpec(memory_space=pltpu.VMEM)
    square = lambda dtype: pltpu.VMEM((width, width), dtype)
    return pl.pallas_call(
        functools.partial(middle_body, slices),
        in_specs=[scalar()] + [vmem] * 5 + [in_place()] * 4,
        out_specs=[vmem] * 13,
        out_shape=[
            like((rows, width), BF16),
            like((rows, width), F32),
            like((rows, width), BF16),
            like((rows, width), BF16),
            like((8, width), F32),
        ]
        + [like((2 * shard + width, width), BF16)] * 4
        + [like((groups * shard, width), BF16)] * 4,
        scratch_shapes=[
            square(BF16),
            square(BF16),
            pltpu.VMEM((groups * width, width), BF16),
            pltpu.VMEM((groups, width, width), BF16),
            pltpu.VMEM((groups, width, rows), BF16),
            pltpu.VMEM((groups, rows, width), F32),
            pltpu.VMEM((groups, rows, width), BF16),
            pltpu.VMEM((width, rows), BF16),
            pltpu.VMEM((width, rows), BF16),
            pltpu.VMEM((width, rows), BF16),
            pltpu.SemaphoreType.DMA((4, 3 + groups)),
        ],
        compiler_params=params(),
        cost_estimate=pl.CostEstimate(
            flops=2 * rows * width * width * 3 * 10, transcendentals=4 * rows * width, bytes_accessed=16000000
        ),
        name="middle",
    )(me, small, tokens, cotangent, o, m, *packs[:3], *on_chip(packs[3]))


def backward_body(
    several, rows, q_ref, k_ref, v_ref, go_ref, gm_ref, o_ref, m_ref, r1_ref, r2_ref, b_ref, e1_ref, e2_ref,
    gq_ref, gk_ref, gv_ref, gs_ref,
):
    low_lanes = lax.broadcasted_iota(jnp.int32, (rows, 128), 1) < 64
    keys = k_ref[...]
    vals = v_ref[...]
    totals = [None, None]
    for start in range(0, q_ref.shape[0], rows):
        at = pl.ds(start, rows)
        g1 = (go_ref[at, :].astype(F32) * r1_ref[at, :]).astype(BF16)
        g2 = (gm_ref[at, :].astype(F32) * r2_ref[at, :]).astype(BF16)
        t1 = g1.astype(F32) * o_ref[at, :]
        t2 = g2.astype(F32) * m_ref[at, :]
        q_turned = q_ref[at, :].T
        g1_turned = g1.T
        g2_turned = g2.T
        grads = []
        for side in range(2):
            mine = low_lanes == (side == 0)
            d1 = jnp.sum(jnp.where(mine, t1, 0.0), axis=1, keepdims=True)
            d2 = jnp.sum(jnp.where(mine, t2, 0.0), axis=1, keepdims=True)
            e1 = e1_ref[side, at, :]
            e2 = e2_ref[side, at, :]
            p1 = product(jnp.where(mine, g1, 0).astype(BF16), vals, NT)
            ds1 = e1.astype(F32) * (p1 - d1)
            slope_term = jnp.sum(ds1 * b_ref[at, :], axis=0, keepdims=True)
            p2 = product(jnp.where(mine, g2, 0).astype(BF16), vals, NT)
            ds = (ds1 + e2.astype(F32) * (p2 - d2)).astype(BF16)
            grads.append(product(ds, keys))
            head = slice(64 * side, 64 * side + 64)
            gk = product(q_turned[head, :], ds)
            gv = product(g1_turned[head, :], e1) + product(g2_turned[head, :], e2)
            if start > 0:
                gk, gv, slope_term = (have + more for have, more in zip(totals[side], (gk, gv, slope_term)))
            totals[side] = (gk, gv, slope_term)
        gq = jnp.where(low_lanes, grads[0], grads[1]) * 0.125
        if not several:
            gq_ref[at, :] = gq.astype(gq_ref.dtype)
        else:
            gq_ref[at, :] = jnp.where(pl.program_id(1) == 0, gq, gq_ref[at, :] + gq)
    gk_ref[...] = jnp.concatenate([totals[0][0], totals[1][0]], axis=0).astype(BF16).T
    gv_ref[...] = jnp.concatenate([totals[0][1], totals[1][1]], axis=0).astype(BF16).T
    for side in range(2):
        term = totals[side][2]
        parts = term[:, 0:128]
        for first in range(128, term.shape[1], 128):
            parts = parts + term[:, first : first + 128]
        if not several:
            gs_ref[side : side + 1, :] = parts
        else:
            gs_ref[side : side + 1, :] = jnp.where(pl.program_id(1) == 0, parts, gs_ref[side : side + 1, :] + parts)


def attend_backward(q, k, v, go, gm, saved, bias, first, pairs):
    o, m, r1, r2, e1, e2 = saved
    row_count = q.shape[0]
    key_count = k.shape[0]
    step_keys = min(1024, key_count)
    several = key_count > step_keys
    elements = 2 * pairs * row_count * key_count
    wide = pl.BlockSpec((row_count, 128), lambda p, c: (0, p + first))
    near = pl.BlockSpec((step_keys, 128), lambda p, c: (c, p + first))
    table = pl.BlockSpec((2, row_count, step_keys), lambda p, c: (p + first, 0, c))
    own = pl.BlockSpec((step_keys, 128), lambda p, c: (c, p))
    return pl.pallas_call(
        functools.partial(backward_body, several, 256),
        grid=(pairs, key_count // step_keys),
        in_specs=[wide, near, near, wide, wide, wide, wide, wide, wide]
        + [pl.BlockSpec((row_count, step_keys), lambda p, c: (0, c)), table, table],
        out_specs=[
            pl.BlockSpec((row_count, 128), lambda p, c: (0, p)),
            own,
            own,
            pl.BlockSpec((None, 8, 128), lambda p, c: (p, 0, 0)),
        ],
        out_shape=[
            like((row_count, 128 * pairs), F32 if several else BF16),
            like((key_count, 128 * pairs), BF16),
            like((key_count, 128 * pairs), BF16),
            like((pairs, 8, 128), F32),
        ],
        compiler_params=params(),
        cost_estimate=pl.CostEstimate(flops=elements * 64 * 2 * 6, transcendentals=0, bytes_accessed=4 * elements),
        name="attend_backward",
    )(q, k, v, go, gm, o, m, r1, r2, bias, e1, e2)


def weights_body(me_ref, turned_ref, gq_ref, gk_ref, gv_ref, gs_ref, gate_ref, *grad_refs):
    rows, width = gq_ref.shape
    shard = width // 4
    lane = lax.broadcasted_iota(jnp.int32, (16, shard), 1)
    row = lax.broadcasted_iota(jnp.int32, (16, shard), 0)
    for r in range(4):
        grad_ref = grad_refs[r]
        device = me_ref[0] ^ r
        start = pl.multiple_of(device * shard, shard)
        a1 = turned_ref[pl.ds(start, shard), :]
        grad_ref[:, 0:width] = product(a1[:, 0:rows], gq_ref[...].astype(BF16)).astype(BF16)
        grad_ref[:, width : 2 * width] = product(a1, gk_ref[...]).astype(BF16)
        grad_ref[:, 2 * width : 3 * width] = product(a1, gv_ref[...]).astype(BF16)
        sums = -jnp.sum(gs_ref[device, 0:2, :], axis=1, keepdims=True)
        block = jnp.where((row == 0) & (lane == 0), sums[0:1, :], 0.0)
        block = jnp.where((row == 0) & (lane == 1), sums[1:2, :], block)
        block = jnp.where(row == 1, gate_ref[0:1, pl.ds(start, shard)], block)
        grad_ref[:, 3 * width : 3 * width + shard] = jnp.zeros((shard, shard), BF16)
        grad_ref[0:16, 3 * width : 3 * width + shard] = block.astype(BF16)


def weight_grads(me, turned, gq, gk, gv, gs, gate):
    rows, width = gq.shape
    shard = width // 4
    vmem = pl.BlockSpec(memory_space=pltpu.VMEM)
    return pl.pallas_call(
        weights_body,
        in_specs=[scalar()] + [vmem] * 6,
        out_specs=[vmem] * 4,
        out_shape=[like((shard, 3 * width + shard), BF16)] * 4,
        compiler_params=params(),
        cost_estimate=pl.CostEstimate(
            flops=6 * gk.shape[0] * width * width, transcendentals=0, bytes_accessed=6000000
        ),
        name="weight_grads",
    )(me, turned, gq, gk, gv, gs, gate)


def rows_body(gq_ref, gk_ref, gv_ref, w_ref, near_ref, own_ref):
    rows, width = gq_ref.shape
    w_k = w_ref[:, width : 2 * width]
    w_v = w_ref[:, 2 * width : 3 * width]
    for first in range(rows, gk_ref.shape[0], rows):
        at = slice(first, first + rows)
        part = product(gk_ref[at, :], w_k, NT) + product(gv_ref[at, :], w_v, NT)
        near_ref[first - rows : first, :] = part.astype(BF16)
    own = product(gq_ref[...].astype(BF16), w_ref[:, 0:width], NT)
    own_ref[...] = own + product(gk_ref[0:rows, :], w_k, NT) + product(gv_ref[0:rows, :], w_v, NT)


def row_grads(gq, gk, gv, w):
    rows, width = gq.shape
    vmem = pl.BlockSpec(memory_space=pltpu.VMEM)
    return pl.pallas_call(
        rows_body,
        in_specs=[vmem] * 4,
        out_specs=[vmem] * 2,
        out_shape=[like((gk.shape[0] - rows, width), BF16), like((rows, width), F32)],
        compiler_params=params(),
        cost_estimate=pl.CostEstimate(
            flops=6 * gk.shape[0] * width * width, transcendentals=0, bytes_accessed=6000000
        ),
        name="row_grads",
    )(gq, gk, gv, w)


def row_sums(table, weight_ref, gain_ref):
    ones = jnp.ones((8, table.shape[1]), F32)
    sums = lax.dot_general(
        ones, table * weight_ref[...].astype(F32), NT, precision=lax.Precision.HIGHEST, preferred_element_type=F32
    )
    return sums[0:1, :] / gain_ref[...].astype(F32)


def assemble_body(
    near_ref, far_ref, own_a, own_b, other_a, by_ctx, by_seq, up_w_ref, gain_ref, out_ref, memory_ref, down_ref, up_ref, sum_ref
):
    width = out_ref.shape[1]
    groups = up_ref.shape[1] // width
    short = out_ref.shape[0] // 8
    tall = down_ref.shape[0] // 8
    size = own_a.shape[0] // 2
    for n, (part_ref, first_part) in enumerate(((own_a, 0), (own_b, 0), (other_a, 0), (by_ctx, 0), (by_seq, 1))):
        side = near_ref[0] if n < 2 else 1 - near_ref[0]
        pair = far_ref[0] if n % 2 == 0 and n < 4 else 1 - far_ref[0]
        for p in range(part_ref.shape[0] // size):
            place = 4 * side + 2 * pair + first_part + p
            at = pl.ds(pl.multiple_of(place * short, short), short)
            piece = part_ref[p * size : (p + 1) * size, :].astype(F32)
            out_ref[at, :] = piece[0:short, :]
            memory_ref[at, :] = piece[short : 2 * short, :]
            down_ref[pl.ds(pl.multiple_of(place * tall, tall), tall), :] = piece[2 * short : 2 * short + tall, :]
            for group in range(groups):
                first = 2 * short + tall + group * short
                up_ref[at, group * width : (group + 1) * width] = piece[first : first + short, :]
    sum_ref[...] = row_sums(up_ref[...], up_w_ref, gain_ref)


def assemble(near, far, parts, w_up, gain):
    width = parts[0].shape[1]
    shard, columns = w_up.shape
    vmem = pl.BlockSpec(memory_space=pltpu.VMEM)
    return pl.pallas_call(
        assemble_body,
        in_specs=[scalar(), scalar()] + [vmem] * 7,
        out_specs=[vmem] * 5,
        out_shape=[like((shard, width), F32)] * 2
        + [like((width, width), F32), like((shard, columns), F32), like((1, shard), F32)],
        compiler_params=params(),
        cost_estimate=pl.CostEstimate(flops=0, transcendentals=0, bytes_accessed=4000000),
        name="assemble",
    )(near, far, *on_chip(*parts), w_up, gain[None])


def close_body(near_ref, own_ref, other_ref, w_ref, gain_ref, qkv_ref, gain_sum_ref, gate_ref, slope_ref):
    half = own_ref.shape[0]
    wide = qkv_ref.shape[1]
    for n, part_ref in enumerate((own_ref, other_ref)):
        side = near_ref[0] if n == 0 else 1 - near_ref[0]
        qkv_ref[pl.ds(pl.multiple_of(side * half, half), half), :] = part_ref[:, 0:wide].astype(F32)
    first = jnp.where(near_ref[0] == 0, own_ref[0:16, wide:].astype(F32), other_ref[0:16, wide:].astype(F32))
    slope_ref[...] = first[0:1, 0 : slope_ref.shape[1]]
    gate_ref[...] = first[1:2, :]
    gain_sum_ref[...] = row_sums(qkv_ref[...], w_ref, gain_ref)


def close(near, own, other, w_qkv, gain, heads):
    shard, wide = w_qkv.shape
    vmem = pl.BlockSpec(memory_space=pltpu.VMEM)
    return pl.pallas_call(
        close_body,
        in_specs=[scalar()] + [vmem] * 4,
        out_specs=[vmem] * 4,
        out_shape=[like((shard, wide), F32), like((1, shard), F32), like((1, shard), F32), like((1, heads), F32)],
        compiler_params=params(),
        cost_estimate=pl.CostEstimate(flops=0, transcendentals=0, bytes_accessed=2000000),
        name="close",
    )(near, *on_chip(own, other), w_qkv, gain[None])


def finish_body(tokens_ref, small_ref, gh1_ref, own_ref, away_ref, out_ref):
    unit, scale = spread(tokens_ref[...].astype(F32))
    grad = (own_ref[...] + away_ref[...].astype(F32)) * small_ref[0:1, :]
    out_ref[...] = gh1_ref[...] + spread_back(unit, scale, grad)


def finish(tokens, small, gh1, own, away):
    vmem = pl.BlockSpec(memory_space=pltpu.VMEM)
    return pl.pallas_call(
        finish_body,
        in_specs=[vmem] * 5,
        out_specs=vmem,
        out_shape=like(gh1.shape, F32),
        compiler_params=params(),
        cost_estimate=pl.CostEstimate(flops=0, transcendentals=0, bytes_accessed=4000000),
        name="finish",
    )(tokens, small, gh1, own, *on_chip(away))


def on_device(
    tokens, cotangent, deal, memory_len, neighbours,
    w_qkv, w_out, w_up, w_down, w_memory, gain_attn, gain_ffn, gate_vec, slopes,
):
    _, row_count, width = tokens.shape
    tokens = tokens.reshape(row_count, width)
    cotangent = cotangent.reshape(row_count, width)
    neighbours = neighbours.reshape(row_count, -1)
    block_count = deal.shape[0]
    ctx_size = lax.axis_size("ctx")
    own_blocks = block_count // ctx_size
    block_len = row_count // own_blocks
    shard = gain_attn.shape[0]
    heads_here = slopes.shape[0]
    groups = w_up.shape[1] // width
    me = lax.axis_index("wt").astype(jnp.int32).reshape(1)
    fast = ctx_size == 2 and lax.axis_size("seq") == 4
    slices = 8 if fast else 1

    short = jnp.concatenate(
        [gain_attn[None], gain_ffn[None], gate_vec[None], jnp.pad(slopes, (0, shard - heads_here))[None]], axis=0
    )
    pack = jnp.concatenate([w_qkv, jnp.pad(short, ((0, shard - 4), (0, 0)))], axis=1)
    others = swap(tokens, "ctx", 1)
    for bit in bits_of("ctx")[1:]:
        both = jnp.concatenate([tokens, others], axis=0)
        others = jnp.concatenate([others, swap(both, "ctx", bit)], axis=0)
    pack_far = swap(pack, "wt", 2)
    pack_near = swap(pack, "wt", 1)
    wide = lay_rows(width, [(w_out, 0), (w_memory, 0)] + [(w_up, width * g) for g in range(groups)] + [(w_down, 0)])
    neighbours = hold(neighbours, wide)

    offsets = jnp.arange(block_len, dtype=jnp.int32)
    owners = lax.axis_index("ctx") ^ jnp.arange(ctx_size, dtype=jnp.int32)
    slots = (owners[:, None] * own_blocks + jnp.arange(own_blocks, dtype=jnp.int32)[None, :]).reshape(-1)
    block_ids = jnp.arange(block_count, dtype=jnp.int32)
    slot_hot = (slots[:, None] == block_ids[None, :]).astype(jnp.int32)
    key_blocks = jnp.sum(slot_hot * deal[None, :], axis=1)
    key_pos = (key_blocks[:, None] * block_len + offsets[None, :]).reshape(-1)
    my_blocks = key_blocks[:own_blocks]
    row_pos = key_pos[:row_count]
    memory_hot = (my_blocks[:, None] == block_ids[None, :]).astype(jnp.int32)
    my_memory = jnp.sum(memory_hot * memory_len, axis=1)
    row_start = jnp.repeat(my_blocks * block_len, block_len)
    row_low = row_start - jnp.repeat(my_memory, block_len)
    picks = neighbours.shape[1]
    hits = sum((neighbours[:, n : n + 1] == key_pos[None, :]).astype(F32) for n in range(picks))
    count = jnp.where(hits == 1.0, 0.0, ABSENT)
    for times in range(2, picks + 1):
        count = jnp.where(hits == float(times), math.log(times), count)
    pack_far, wide = lax.optimization_barrier((pack_far, wide, count))[:2]
    pack_both = swap(pack_far, "wt", 1)
    wide_far = swap(wide, "wt", 2)
    wide_near = swap(wide, "wt", 1)
    row_pos = hold(row_pos, pack_far)
    distance = jnp.log(jnp.abs(row_pos[:, None] - key_pos[None, :]).astype(F32) + 1.0)
    visible = (key_pos[None, :] >= row_low[:, None]) & (key_pos[None, :] < (row_start + block_len)[:, None])
    bias = jnp.where(visible, distance, HIDDEN)

    q, k, v, turned, full_qkv, small = project(
        me, tokens, hold(others, bias), (pack, pack_near, pack_far, pack_both)
    )
    saved = attend_forward(small, q, k, v, bias, count)
    wide_both = swap(hold(wide_far, saved[0]), "wt", 1)
    wides = (wide, wide_near, wide_far, wide_both)
    layer_out, gh1, go, gm, gate, g0, g1, g2, g3, h0, h1, h2, h3 = middle(
        slices, me, small, tokens, cotangent, saved[0], saved[1], wides, groups
    )

    all_pairs = width // 128
    g_far = add_low(g2, swap(g3, "wt", 1))
    g_one = swap(g1, "wt", 1)
    if fast:
        h_far = add_low(h2, swap(h3, "wt", 1))
        h_own = add_low(h0, swap(h1, "wt", 1))
        g_got = swap(g_far, "wt", 2)
        both = jnp.concatenate([h_far.reshape(2, -1, width), h_own.reshape(2, -1, width)], axis=1)
        both_keep, both_got = send_half(both.reshape(-1, width), "ctx", 1)
        gq, gk, gv, gs = attend_backward(q, k, v, hold(go, g_far, both_keep), gm, saved, bias, 0, all_pairs)
        gq, gk, gv, gs, g_got, both_got = lax.optimization_barrier((gq, gk, gv, gs, g_got, both_got))
        cut = both_got.shape[0] // 2
        far_keep, own_keep = both_keep[:cut], both_keep[cut:]
        far_got, own_got = both_got[:cut], both_got[cut:]
        h_got = swap(add_low(far_keep, far_got), "wt", 2)
        g_keep, g_near = send_half(add_all(g0, [g_one, g_got]), "ctx", 1)
        q0, q1, q2, q3 = weight_grads(me, turned, hold(gq, g_keep), gk, gv, gs, gate)
        q_three, q_one = swap(q3, "wt", 1), swap(q1, "wt", 1)
        gq, q0, q2, g_near, h_got = lax.optimization_barrier((gq, q0, q2, g_near, h_got))
        q_far = add_low(q2, q_three)
        lower = add_low(g_keep, g_near).reshape(4, -1, width)
        higher = add_all(own_keep, [own_got, h_got]).reshape(4, -1, width)
        gh_keep, gh_got = send_half(jnp.concatenate([lower, higher], axis=1).reshape(-1, width), "seq", 1)
        near, own = row_grads(hold(gq, q_far, gh_keep), gk, gv, full_qkv)
        q_far = swap(q_far, "wt", 2)
        order = Order()
        near, gh_got = order.arrive(near, gh_got)
        gh = add_low(gh_keep, gh_got)
        gh_got = swap(gh, "seq", 2)
        q_keep, q_got = send_half(add_all(q0, [q_one, order.arrive(q_far)]), "ctx", 1)
        q_sum = add_low(q_keep, order.arrive(q_got))
        q_got = swap(q_sum, "seq", 1)
        away = swap(hold(near, q_sum), "ctx", 1)
        q_got, gh_got = order.arrive(q_got, gh_got)
        own_a = add_low(gh, gh_got)
        q_sum = add_low(q_sum, q_got)
        q_got = swap(hold(q_sum, own_a), "seq", 2)
        own_b = swap(own_a, "seq", 1)
        other_a = swap(own_a, "ctx", 1)
        away = order.arrive(away)
        grad_tokens = finish(tokens, small, gh1, own, away)
        order.before = (grad_tokens,)
        q_sum = add_low(q_sum, order.arrive(q_got))
        q_other = swap(q_sum, "ctx", 1)
        own_b = order.arrive(own_b)
        other_a = order.arrive(other_a)
        cut = own_b.shape[0] // 2
        by_seq = swap(other_a[cut:], "seq", 1)
        by_ctx = swap(own_b[:cut], "ctx", 1)
        side = lax.axis_index("ctx").astype(jnp.int32).reshape(1)
        pair = side_of("seq", 1).astype(jnp.int32).reshape(1)
        t_qkv, *shorts = close(side, q_sum, order.arrive(q_other), w_qkv, gain_attn, heads_here)
        order.before = (t_qkv,)
        by_ctx, by_seq = order.arrive(by_ctx, by_seq)
        t_out, t_memory, t_down, t_up, t_gain_two = assemble(
            side, pair, (own_a, own_b, other_a, by_ctx, by_seq), w_up, gain_ffn
        )
        t_gain_one, t_gate, t_slopes, t_gain_two = (value.reshape(-1) for value in (*shorts, t_gain_two))
    else:
        h_far = add_low(h2, swap(h3, "wt", 1))
        h_one = swap(h1, "wt", 1)
        g_sum = add_all(g0, [g_one, swap(g_far, "wt", 2)])
        h_sum = add_all(h0, [h_one, swap(h_far, "wt", 2)])
        gq, gk, gv, gs = attend_backward(q, k, v, go, gm, saved, bias, 0, all_pairs)
        grads = weight_grads(me, turned, gq, gk, gv, gs, gate)
        near, own = row_grads(gq, gk, gv, full_qkv)
        for bit in reversed(bits_of("ctx")[1:]):
            both = jnp.concatenate([own.astype(BF16), near], axis=0)
            fold = bit * row_count
            folded = both[:fold].astype(F32) + swap(both[fold:], "ctx", bit).astype(F32)
            own, near = folded[:row_count], folded[row_count:].astype(BF16)
        away = swap(near, "ctx", 1)
        q_far = swap(add_low(grads[2], swap(grads[3], "wt", 1)), "wt", 2)
        q_sum = add_all(grads[0], [swap(grads[1], "wt", 1), q_far])
        q_sum = near_whole(far_both(near_halves(q_sum)))
        g_sum = near_whole(far_whole(far_halves(near_halves(g_sum))))
        h_sum = near_whole(far_whole(far_halves(near_halves(h_sum))))
        grad_tokens = finish(tokens, small, gh1, own, away)
        t_out = g_sum[:shard].astype(F32)
        t_memory = g_sum[shard : 2 * shard].astype(F32)
        t_down = g_sum[2 * shard : 2 * shard + width].astype(F32)
        t_up = jnp.concatenate([h_sum[shard * g : shard * (g + 1)] for g in range(groups)], axis=1).astype(F32)
        t_qkv = q_sum[:, : 3 * width].astype(F32)
        t_slopes = q_sum[0, 3 * width : 3 * width + heads_here].astype(F32)
        t_gate = q_sum[1, 3 * width : 3 * width + shard].astype(F32)
        t_gain_one = jnp.sum(t_qkv * w_qkv.astype(F32), axis=1) / gain_attn.astype(F32)
        t_gain_two = jnp.sum(t_up * w_up.astype(F32), axis=1) / gain_ffn.astype(F32)


    return (
        layer_out[None], grad_tokens[None], t_qkv, t_out, t_up, t_down, t_memory,
        t_gain_one, t_gain_two, t_gate, t_slopes,
    )


def solution(mesh):
    rows = P(("seq", "wt"), "ctx", None)
    weight = P("wt", None)
    vector = P("wt")
    return jax.shard_map(
        on_device,
        mesh=mesh,
        in_specs=(rows, rows, P(), P(("seq", "wt"), None), rows) + (weight,) * 5 + (vector,) * 4,
        out_specs=(rows, rows) + (weight,) * 5 + (vector,) * 4,
        check_vma=False,
    )
```

```python
import functools
import math
import jax
import jax.numpy as jnp
from jax import lax
from jax.experimental import pallas as pl
from jax.experimental.pallas import tpu as pltpu
from jax.sharding import PartitionSpec as P

EPSILON = 1e-05
F32 = jnp.float32
BF16 = jnp.bfloat16
NT = (((1,), (1,)), ((), ()))
NN = (((1,), (0,)), ((), ()))
HIDDEN = 1e12
ABSENT = -1e30
VMEM = 56 * 1024 * 1024
CURVE = math.sqrt(2.0 / math.pi)
CUBIC = 0.044715


def product(left, right, dims=NN):
    return lax.dot_general(left, right, dims, preferred_element_type=F32)


def params(limit=VMEM):
    return pltpu.CompilerParams(vmem_limit_bytes=limit)


def like(shape, dtype):
    return jax.ShapeDtypeStruct(shape, dtype)


def in_place():
    return pl.BlockSpec(memory_space=pl.ANY)


def on_chip(*values):
    return [pltpu.with_memory_space_constraint(value, pltpu.VMEM) for value in values]


def scalar():
    return pl.BlockSpec(memory_space=pltpu.SMEM)


def swap(value, axis, bit):
    size = lax.axis_size(axis)
    return lax.ppermute(value, axis, [(i, i ^ bit) for i in range(size)])


def bits_of(axis):
    bits = []
    bit = 1
    while bit < lax.axis_size(axis):
        bits.append(bit)
        bit *= 2
    return bits


def side_of(axis, bit):
    return (lax.axis_index(axis) // bit) % 2


def hold(value, *before):
    return lax.optimization_barrier((value,) + before)[0]


class Order:
    def __init__(self):
        self.before = ()

    def arrive(self, *values):
        held = lax.optimization_barrier(values + self.before)[: len(values)]
        self.before = held[:1]
        return held if len(held) > 1 else held[0]


def send_half(part, axis, bit):
    side = side_of(axis, bit)
    both = part.reshape((2, part.shape[0] // 2) + part.shape[1:])
    got = swap(lax.dynamic_index_in_dim(both, 1 - side, 0, False), axis, bit)
    return lax.dynamic_index_in_dim(both, side, 0, False), got


def place_half(part, other, axis, bit):
    high = side_of(axis, bit) == 1
    return jnp.concatenate([jnp.where(high, other, part), jnp.where(high, part, other)], axis=0)


def add_all(own, got):
    total = own.astype(F32)
    for value in got:
        total = total + value.astype(F32)
    return total.astype(BF16)


def add_low(left, right):
    return (left.astype(F32) + right.astype(F32)).astype(BF16)


def halve(part, axis, bit):
    side = side_of(axis, bit)
    both = part.reshape((2, part.shape[0] // 2) + part.shape[1:])
    got = swap(lax.dynamic_index_in_dim(both, 1 - side, 0, False), axis, bit)
    return add_low(lax.dynamic_index_in_dim(both, side, 0, False), got)


def widen(part, axis, bit):
    other = swap(part, axis, bit)
    high = side_of(axis, bit) == 1
    return jnp.concatenate([jnp.where(high, other, part), jnp.where(high, part, other)], axis=0)


def near_halves(part):
    for bit in bits_of("ctx"):
        part = halve(part, "ctx", bit)
    return part


def near_whole(part):
    for bit in reversed(bits_of("ctx")):
        part = widen(part, "ctx", bit)
    return part


def far_halves(part):
    for bit in bits_of("seq"):
        part = halve(part, "seq", bit)
    return part


def far_whole(part):
    for bit in reversed(bits_of("seq")):
        part = widen(part, "seq", bit)
    return part


def far_both(part):
    for bit in bits_of("seq"):
        part = add_low(part, swap(part, "seq", bit))
    return part


def spread(values):
    centred = values - jnp.mean(values, axis=-1, keepdims=True)
    scale = lax.rsqrt(jnp.mean(centred * centred, axis=-1, keepdims=True) + EPSILON)
    return centred * scale, scale


def spread_back(unit, scale, grad):
    along = jnp.mean(grad * unit, axis=-1, keepdims=True)
    return scale * (grad - jnp.mean(grad, axis=-1, keepdims=True) - unit * along)


def lay_rows(width, pieces):
    arrays = [piece[0] for piece in pieces]
    total = sum(array.shape[0] for array in arrays)

    def body(*refs):
        target, sem = refs[len(pieces) :]
        copies = []
        first = 0
        for n, (ref, (_, col)) in enumerate(zip(refs, pieces)):
            source = ref.at[:, col : col + width]
            copies.append(pltpu.make_async_copy(source, target.at[first : first + ref.shape[0]], sem.at[n]))
            first += ref.shape[0]
        for copy in copies:
            copy.start()
        for copy in copies:
            copy.wait()

    vmem = pl.BlockSpec(memory_space=pltpu.VMEM)
    return pl.pallas_call(
        body,
        in_specs=[vmem] * len(arrays),
        out_specs=in_place(),
        out_shape=like((total, width), BF16),
        scratch_shapes=[pltpu.SemaphoreType.DMA((len(arrays),))],
        compiler_params=params(),
        cost_estimate=pl.CostEstimate(flops=0, transcendentals=0, bytes_accessed=4 * total * width),
        name="lay_rows",
    )(*arrays)


def project_body(me_ref, own_ref, other_ref, p0, p1, p2, p3, q_ref, k_ref, v_ref, turned_ref, w_ref, small_ref, few, sem):
    step = pl.program_id(0)
    width = own_ref.shape[1]
    shard = p0.shape[0]

    copies = []
    shorts = []
    for r, pack in enumerate((p0, p1, p2, p3)):
        place = pl.multiple_of((me_ref[0] ^ r) * shard, shard)
        copies.append(pltpu.make_async_copy(pack.at[:, 0 : 3 * width], w_ref.at[pl.ds(place, shard), :], sem.at[2 * r]))
        source = pack.at[0:16, 3 * width : 3 * width + shard]
        shorts.append(pltpu.make_async_copy(source, few.at[:, pl.ds(place, shard)], sem.at[2 * r + 1]))

    @pl.when(step == 0)
    def _():
        for copy in shorts + copies:
            copy.start()

    tokens = jnp.where(step == 0, own_ref[...], other_ref[...]).astype(F32)
    unit, _ = spread(tokens)

    @pl.when(step == 0)
    def _():
        for copy in shorts:
            copy.wait()
        small_ref[...] = few[...].astype(F32)

    a1 = (unit * few[0:1, :].astype(F32)).astype(BF16)
    turned_ref[...] = a1.T

    @pl.when(step == 0)
    def _():
        for copy in copies:
            copy.wait()
        q = product(a1, w_ref[:, 0:width]).astype(BF16)
        q_ref[...] = (q.astype(F32) * 0.125).astype(BF16)

    k_ref[...] = product(a1, w_ref[:, width : 2 * width]).astype(BF16)
    v_ref[...] = product(a1, w_ref[:, 2 * width : 3 * width]).astype(BF16)


def project(me, own, others, packs):
    rows, width = own.shape
    steps = 1 + others.shape[0] // rows
    whole = lambda i: (0, 0)
    return pl.pallas_call(
        project_body,
        grid=(steps,),
        in_specs=[
            scalar(),
            pl.BlockSpec((rows, width), whole),
            pl.BlockSpec((rows, width), lambda i: (jnp.maximum(i - 1, 0), 0)),
        ]
        + [in_place()] * 4,
        out_specs=[
            pl.BlockSpec((rows, width), whole),
            pl.BlockSpec((rows, width), lambda i: (i, 0)),
            pl.BlockSpec((rows, width), lambda i: (i, 0)),
            pl.BlockSpec((width, rows), lambda i: (0, i)),
            pl.BlockSpec((width, 3 * width), whole),
            pl.BlockSpec((16, width), whole),
        ],
        out_shape=[
            like((rows, width), BF16),
            like((rows * steps, width), BF16),
            like((rows * steps, width), BF16),
            like((width, rows * steps), BF16),
            like((width, 3 * width), BF16),
            like((16, width), F32),
        ],
        scratch_shapes=[pltpu.VMEM((16, width), BF16), pltpu.SemaphoreType.DMA((8,))],
        compiler_params=params(),
        cost_estimate=pl.CostEstimate(flops=6 * rows * steps * width * width, transcendentals=0, bytes_accessed=6000000),
        name="project",
    )(me, own, others, *packs)


def forward_body(
    rows, small_ref, q_ref, k_ref, v_ref, b_ref, c_ref, o_ref, m_ref, r1_ref, r2_ref, e1_ref, e2_ref, first, second
):
    low_lanes = lax.broadcasted_iota(jnp.int32, (rows, 128), 1) < 64
    values = jnp.concatenate([v_ref[...], jnp.ones(v_ref.shape, BF16)], axis=1)
    items = [(pl.ds(start, rows), side) for start in range(0, q_ref.shape[0], rows) for side in range(2)]

    def scores(n):
        at, side = items[n]
        slope = small_ref[3:4, side : side + 1]
        q_head = jnp.where(low_lanes == (side == 0), q_ref[at, :], 0).astype(BF16)
        raw = product(q_head, k_ref[...], NT)
        first[n % 2] = raw - slope * b_ref[at, :]
        second[n % 2] = raw + c_ref[at, :]
        return [jnp.max(table[n % 2], axis=1, keepdims=True) for table in (first, second)]

    mixed = {}
    peaks = scores(0)
    for n, (at, side) in enumerate(items):
        later = scores(n + 1) if n + 1 < len(items) else None
        for slot, (table, kept_ref) in enumerate(((first, e1_ref), (second, e2_ref))):
            weights = jnp.exp(table[n % 2] - peaks[slot]).astype(BF16)
            kept_ref[side, at, :] = weights
            both = product(weights, values)
            mixed[side, slot] = (both[:, :128], 1.0 / both[:, 128:])
        peaks = later
        if side == 1:
            for slot, value_ref, recip_ref in ((0, o_ref, r1_ref), (1, m_ref, r2_ref)):
                recip = jnp.where(low_lanes, mixed[0, slot][1], mixed[1, slot][1])
                recip_ref[at, :] = recip
                value_ref[at, :] = jnp.where(low_lanes, mixed[0, slot][0], mixed[1, slot][0]) * recip


def attend_forward(small, q, k, v, bias, count):
    row_count, width = q.shape
    key_count = k.shape[0]
    pairs = width // 128
    step_rows = max(64, min(row_count, (512 * 1024) // key_count))
    rows = min(256, step_rows)
    elements = 2 * pairs * row_count * key_count
    own = lambda p, i: (i, p)
    return pl.pallas_call(
        functools.partial(forward_body, rows),
        grid=(pairs, row_count // step_rows),
        in_specs=[
            pl.BlockSpec((16, 128), lambda p, i: (0, p)),
            pl.BlockSpec((step_rows, 128), own),
            pl.BlockSpec((key_count, 128), lambda p, i: (0, p)),
            pl.BlockSpec((key_count, 128), lambda p, i: (0, p)),
            pl.BlockSpec((step_rows, key_count), lambda p, i: (i, 0)),
            pl.BlockSpec((step_rows, key_count), lambda p, i: (i, 0)),
        ],
        out_specs=[pl.BlockSpec((step_rows, 128), own)] * 4
        + [pl.BlockSpec((2, step_rows, key_count), lambda p, i: (p, i, 0))] * 2,
        out_shape=[like((row_count, width), F32)] * 4 + [like((2 * pairs, row_count, key_count), BF16)] * 2,
        scratch_shapes=[pltpu.VMEM((2, rows, key_count), F32)] * 2,
        compiler_params=params(),
        cost_estimate=pl.CostEstimate(
            flops=elements * 64 * 2 * 3, transcendentals=2 * elements, bytes_accessed=4 * elements
        ),
        name="attend_forward",
    )(small, q, k, v, bias, count)


def middle_body(
    slices, me_ref, small_ref, tokens_ref, cot_ref, o_ref, m_ref, p0, p1, p2, p3,
    out_ref, gh1_ref, go_ref, gm_ref, gate_ref, g0, g1, g2, g3, h0, h1_ref, h2_ref, h3,
    w_out, w_memory, w_down, w_up, act, slope, gu, a2_turned, o_turned, m_turned, sem,
):
    rows, width = tokens_ref.shape
    shard = width // 4
    groups = w_down.shape[0] // width
    copies = []
    for r, pack in enumerate((p0, p1, p2, p3)):
        device = me_ref[0] ^ r
        place = pl.ds(pl.multiple_of(device * shard, shard), shard)
        down = pl.ds(pl.multiple_of(device * width, width), width)
        targets = [w_out.at[place], w_memory.at[place]] + [w_up.at[group, place] for group in range(groups)]
        pieces = [(pack.at[n * shard : (n + 1) * shard], target) for n, target in enumerate(targets)]
        pieces.append((pack.at[len(targets) * shard : len(targets) * shard + width], w_down.at[down]))
        copies.append([pltpu.make_async_copy(*piece, sem.at[r, n]) for n, piece in enumerate(pieces)])
    for part in zip(*copies):
        for copy in part:
            copy.start()
    gain = small_ref[1:2, :]
    gate_vec = small_ref[2:3, :]
    o_low = o_ref[...].astype(BF16)
    m_low = m_ref[...].astype(BF16)
    for copy in copies:
        copy[0].wait()
        copy[1].wait()
    h1 = tokens_ref[...].astype(F32) + product(o_low, w_out[...])
    mem = product(m_low, w_memory[...])
    o_turned[...] = o_low.T
    m_turned[...] = m_low.T
    unit, scale = spread(h1)
    a2 = (unit * gain).astype(BF16)
    a2_turned[...] = a2.T
    for copy in copies:
        for piece in copy[2:]:
            piece.wait()
    h2 = h1
    for group in range(groups):
        u = product(a2, w_up[group])
        square = u * u
        bent = jnp.tanh(CURVE * u * (1.0 + CUBIC * square))
        half = 0.5 * (1.0 + bent)
        active = (u * half).astype(BF16)
        slope[group] = half + 0.5 * u * (1.0 - bent * bent) * (CURVE * (1.0 + 3.0 * CUBIC * square))
        act[group] = active.T
        h2 = h2 + product(active, w_down[group * width : (group + 1) * width, :])
    gate = jax.nn.sigmoid(jnp.sum(h2 * gate_vec, axis=1, keepdims=True))
    apart = mem - h2
    out_ref[...] = (h2 + gate * apart).astype(BF16)
    c = cot_ref[...].astype(F32)
    grad_mem = (c * gate).astype(BF16)
    dz = jnp.sum(c * apart, axis=1, keepdims=True) * gate * (1.0 - gate)
    gh2 = c * (1.0 - gate) + dz * gate_vec
    gate_ref[...] = jnp.broadcast_to(jnp.sum(dz * h2, axis=0, keepdims=True), gate_ref.shape)
    gf = gh2.astype(BF16)
    gm_ref[...] = product(grad_mem, w_memory[...], NT).astype(BF16)
    ga2 = None
    for group in range(groups):
        back = product(gf, w_down[group * width : (group + 1) * width, :], NT)
        low = (back * slope[group]).astype(BF16)
        gu[group] = low
        more = product(low, w_up[group], NT)
        ga2 = more if ga2 is None else ga2 + more
    gh1 = gh2 + spread_back(unit, scale, ga2 * gain)
    gh1_ref[...] = gh1
    ga = gh1.astype(BF16)
    go_ref[...] = product(ga, w_out[...], NT).astype(BF16)
    for r, (grad_ref, up_ref) in enumerate(((g0, h0), (g1, h1_ref), (g2, h2_ref), (g3, h3))):
        device = me_ref[0] ^ r
        place = pl.ds(pl.multiple_of(device * shard, shard), shard)
        parts = [product(o_turned[place, :], ga), product(m_turned[place, :], grad_mem), product(act[device], gf)]
        lay_slices(grad_ref, slices, [part.astype(BF16) for part in parts])
        parts = [product(a2_turned[place, :], gu[group]) for group in range(groups)]
        lay_slices(up_ref, slices, [part.astype(BF16) for part in parts])


def lay_slices(target, slices, parts):
    first = 0
    for n in range(slices):
        for part in parts:
            height = part.shape[0] // slices
            target[first : first + height, :] = part[n * height : (n + 1) * height, :]
            first += height


def middle(slices, me, small, tokens, cotangent, o, m, packs, groups):
    rows, width = tokens.shape
    shard = width // 4
    vmem = pl.BlockSpec(memory_space=pltpu.VMEM)
    square = lambda dtype: pltpu.VMEM((width, width), dtype)
    return pl.pallas_call(
        functools.partial(middle_body, slices),
        in_specs=[scalar()] + [vmem] * 5 + [in_place()] * 4,
        out_specs=[vmem] * 13,
        out_shape=[
            like((rows, width), BF16),
            like((rows, width), F32),
            like((rows, width), BF16),
            like((rows, width), BF16),
            like((8, width), F32),
        ]
        + [like((2 * shard + width, width), BF16)] * 4
        + [like((groups * shard, width), BF16)] * 4,
        scratch_shapes=[
            square(BF16),
            square(BF16),
            pltpu.VMEM((groups * width, width), BF16),
            pltpu.VMEM((groups, width, width), BF16),
            pltpu.VMEM((groups, width, rows), BF16),
            pltpu.VMEM((groups, rows, width), F32),
            pltpu.VMEM((groups, rows, width), BF16),
            pltpu.VMEM((width, rows), BF16),
            pltpu.VMEM((width, rows), BF16),
            pltpu.VMEM((width, rows), BF16),
            pltpu.SemaphoreType.DMA((4, 3 + groups)),
        ],
        compiler_params=params(),
        cost_estimate=pl.CostEstimate(
            flops=2 * rows * width * width * 3 * 10, transcendentals=4 * rows * width, bytes_accessed=16000000
        ),
        name="middle",
    )(me, small, tokens, cotangent, o, m, *packs[:3], *on_chip(packs[3]))


def backward_body(
    several, rows, q_ref, k_ref, v_ref, go_ref, gm_ref, o_ref, m_ref, r1_ref, r2_ref, b_ref, e1_ref, e2_ref,
    gq_ref, gk_ref, gv_ref, gs_ref,
):
    low_lanes = lax.broadcasted_iota(jnp.int32, (rows, 128), 1) < 64
    keys = k_ref[...]
    vals = v_ref[...]
    totals = [None, None]
    for start in range(0, q_ref.shape[0], rows):
        at = pl.ds(start, rows)
        g1 = (go_ref[at, :].astype(F32) * r1_ref[at, :]).astype(BF16)
        g2 = (gm_ref[at, :].astype(F32) * r2_ref[at, :]).astype(BF16)
        t1 = g1.astype(F32) * o_ref[at, :]
        t2 = g2.astype(F32) * m_ref[at, :]
        q_turned = q_ref[at, :].T
        g1_turned = g1.T
        g2_turned = g2.T
        grads = []
        for side in range(2):
            mine = low_lanes == (side == 0)
            d1 = jnp.sum(jnp.where(mine, t1, 0.0), axis=1, keepdims=True)
            d2 = jnp.sum(jnp.where(mine, t2, 0.0), axis=1, keepdims=True)
            e1 = e1_ref[side, at, :]
            e2 = e2_ref[side, at, :]
            p1 = product(jnp.where(mine, g1, 0).astype(BF16), vals, NT)
            ds1 = e1.astype(F32) * (p1 - d1)
            slope_term = jnp.sum(ds1 * b_ref[at, :], axis=0, keepdims=True)
            p2 = product(jnp.where(mine, g2, 0).astype(BF16), vals, NT)
            ds = (ds1 + e2.astype(F32) * (p2 - d2)).astype(BF16)
            grads.append(product(ds, keys))
            head = slice(64 * side, 64 * side + 64)
            gk = product(q_turned[head, :], ds)
            gv = product(g1_turned[head, :], e1) + product(g2_turned[head, :], e2)
            if start > 0:
                gk, gv, slope_term = (have + more for have, more in zip(totals[side], (gk, gv, slope_term)))
            totals[side] = (gk, gv, slope_term)
        gq = jnp.where(low_lanes, grads[0], grads[1]) * 0.125
        if not several:
            gq_ref[at, :] = gq.astype(gq_ref.dtype)
        else:
            gq_ref[at, :] = jnp.where(pl.program_id(1) == 0, gq, gq_ref[at, :] + gq)
    gk_ref[...] = jnp.concatenate([totals[0][0], totals[1][0]], axis=0).astype(BF16).T
    gv_ref[...] = jnp.concatenate([totals[0][1], totals[1][1]], axis=0).astype(BF16).T
    for side in range(2):
        term = totals[side][2]
        parts = term[:, 0:128]
        for first in range(128, term.shape[1], 128):
            parts = parts + term[:, first : first + 128]
        if not several:
            gs_ref[side : side + 1, :] = parts
        else:
            gs_ref[side : side + 1, :] = jnp.where(pl.program_id(1) == 0, parts, gs_ref[side : side + 1, :] + parts)


def attend_backward(q, k, v, go, gm, saved, bias, first, pairs):
    o, m, r1, r2, e1, e2 = saved
    row_count = q.shape[0]
    key_count = k.shape[0]
    step_keys = min(1024, key_count)
    several = key_count > step_keys
    elements = 2 * pairs * row_count * key_count
    wide = pl.BlockSpec((row_count, 128), lambda p, c: (0, p + first))
    near = pl.BlockSpec((step_keys, 128), lambda p, c: (c, p + first))
    table = pl.BlockSpec((2, row_count, step_keys), lambda p, c: (p + first, 0, c))
    own = pl.BlockSpec((step_keys, 128), lambda p, c: (c, p))
    return pl.pallas_call(
        functools.partial(backward_body, several, 256),
        grid=(pairs, key_count // step_keys),
        in_specs=[wide, near, near, wide, wide, wide, wide, wide, wide]
        + [pl.BlockSpec((row_count, step_keys), lambda p, c: (0, c)), table, table],
        out_specs=[
            pl.BlockSpec((row_count, 128), lambda p, c: (0, p)),
            own,
            own,
            pl.BlockSpec((None, 8, 128), lambda p, c: (p, 0, 0)),
        ],
        out_shape=[
            like((row_count, 128 * pairs), F32 if several else BF16),
            like((key_count, 128 * pairs), BF16),
            like((key_count, 128 * pairs), BF16),
            like((pairs, 8, 128), F32),
        ],
        compiler_params=params(),
        cost_estimate=pl.CostEstimate(flops=elements * 64 * 2 * 6, transcendentals=0, bytes_accessed=4 * elements),
        name="attend_backward",
    )(q, k, v, go, gm, o, m, r1, r2, bias, e1, e2)


def weights_body(me_ref, turned_ref, gq_ref, gk_ref, gv_ref, gs_ref, gate_ref, *grad_refs):
    rows, width = gq_ref.shape
    shard = width // 4
    lane = lax.broadcasted_iota(jnp.int32, (16, shard), 1)
    row = lax.broadcasted_iota(jnp.int32, (16, shard), 0)
    for r in range(4):
        grad_ref = grad_refs[r]
        device = me_ref[0] ^ r
        start = pl.multiple_of(device * shard, shard)
        a1 = turned_ref[pl.ds(start, shard), :]
        grad_ref[:, 0:width] = product(a1[:, 0:rows], gq_ref[...].astype(BF16)).astype(BF16)
        grad_ref[:, width : 2 * width] = product(a1, gk_ref[...]).astype(BF16)
        grad_ref[:, 2 * width : 3 * width] = product(a1, gv_ref[...]).astype(BF16)
        sums = -jnp.sum(gs_ref[device, 0:2, :], axis=1, keepdims=True)
        block = jnp.where((row == 0) & (lane == 0), sums[0:1, :], 0.0)
        block = jnp.where((row == 0) & (lane == 1), sums[1:2, :], block)
        block = jnp.where(row == 1, gate_ref[0:1, pl.ds(start, shard)], block)
        grad_ref[:, 3 * width : 3 * width + shard] = jnp.zeros((shard, shard), BF16)
        grad_ref[0:16, 3 * width : 3 * width + shard] = block.astype(BF16)


def weight_grads(me, turned, gq, gk, gv, gs, gate):
    rows, width = gq.shape
    shard = width // 4
    vmem = pl.BlockSpec(memory_space=pltpu.VMEM)
    return pl.pallas_call(
        weights_body,
        in_specs=[scalar()] + [vmem] * 6,
        out_specs=[vmem] * 4,
        out_shape=[like((shard, 3 * width + shard), BF16)] * 4,
        compiler_params=params(),
        cost_estimate=pl.CostEstimate(
            flops=6 * gk.shape[0] * width * width, transcendentals=0, bytes_accessed=6000000
        ),
        name="weight_grads",
    )(me, turned, gq, gk, gv, gs, gate)


def rows_body(gq_ref, gk_ref, gv_ref, w_ref, near_ref, own_ref):
    rows, width = gq_ref.shape
    w_k = w_ref[:, width : 2 * width]
    w_v = w_ref[:, 2 * width : 3 * width]
    for first in range(rows, gk_ref.shape[0], rows):
        at = slice(first, first + rows)
        part = product(gk_ref[at, :], w_k, NT) + product(gv_ref[at, :], w_v, NT)
        near_ref[first - rows : first, :] = part.astype(BF16)
    own = product(gq_ref[...].astype(BF16), w_ref[:, 0:width], NT)
    own_ref[...] = own + product(gk_ref[0:rows, :], w_k, NT) + product(gv_ref[0:rows, :], w_v, NT)


def row_grads(gq, gk, gv, w):
    rows, width = gq.shape
    vmem = pl.BlockSpec(memory_space=pltpu.VMEM)
    return pl.pallas_call(
        rows_body,
        in_specs=[vmem] * 4,
        out_specs=[vmem] * 2,
        out_shape=[like((gk.shape[0] - rows, width), BF16), like((rows, width), F32)],
        compiler_params=params(),
        cost_estimate=pl.CostEstimate(
            flops=6 * gk.shape[0] * width * width, transcendentals=0, bytes_accessed=6000000
        ),
        name="row_grads",
    )(gq, gk, gv, w)


def row_sums(table, weight_ref, gain_ref):
    ones = jnp.ones((8, table.shape[1]), F32)
    sums = lax.dot_general(
        ones, table * weight_ref[...].astype(F32), NT, precision=lax.Precision.HIGHEST, preferred_element_type=F32
    )
    return sums[0:1, :] / gain_ref[...].astype(F32)


def assemble_body(
    near_ref, far_ref, own_a, own_b, other_a, by_ctx, by_seq, up_w_ref, gain_ref, out_ref, memory_ref, down_ref, up_ref, sum_ref
):
    width = out_ref.shape[1]
    groups = up_ref.shape[1] // width
    short = out_ref.shape[0] // 8
    tall = down_ref.shape[0] // 8
    size = own_a.shape[0] // 2
    for n, (part_ref, first_part) in enumerate(((own_a, 0), (own_b, 0), (other_a, 0), (by_ctx, 0), (by_seq, 1))):
        side = near_ref[0] if n < 2 else 1 - near_ref[0]
        pair = far_ref[0] if n % 2 == 0 and n < 4 else 1 - far_ref[0]
        for p in range(part_ref.shape[0] // size):
            place = 4 * side + 2 * pair + first_part + p
            at = pl.ds(pl.multiple_of(place * short, short), short)
            piece = part_ref[p * size : (p + 1) * size, :].astype(F32)
            out_ref[at, :] = piece[0:short, :]
            memory_ref[at, :] = piece[short : 2 * short, :]
            down_ref[pl.ds(pl.multiple_of(place * tall, tall), tall), :] = piece[2 * short : 2 * short + tall, :]
            for group in range(groups):
                first = 2 * short + tall + group * short
                up_ref[at, group * width : (group + 1) * width] = piece[first : first + short, :]
    sum_ref[...] = row_sums(up_ref[...], up_w_ref, gain_ref)


def assemble(near, far, parts, w_up, gain):
    width = parts[0].shape[1]
    shard, columns = w_up.shape
    vmem = pl.BlockSpec(memory_space=pltpu.VMEM)
    return pl.pallas_call(
        assemble_body,
        in_specs=[scalar(), scalar()] + [vmem] * 7,
        out_specs=[vmem] * 5,
        out_shape=[like((shard, width), F32)] * 2
        + [like((width, width), F32), like((shard, columns), F32), like((1, shard), F32)],
        compiler_params=params(),
        cost_estimate=pl.CostEstimate(flops=0, transcendentals=0, bytes_accessed=4000000),
        name="assemble",
    )(near, far, *on_chip(*parts), w_up, gain[None])


def close_body(near_ref, own_ref, other_ref, w_ref, gain_ref, qkv_ref, gain_sum_ref, gate_ref, slope_ref):
    half = own_ref.shape[0]
    wide = qkv_ref.shape[1]
    for n, part_ref in enumerate((own_ref, other_ref)):
        side = near_ref[0] if n == 0 else 1 - near_ref[0]
        qkv_ref[pl.ds(pl.multiple_of(side * half, half), half), :] = part_ref[:, 0:wide].astype(F32)
    first = jnp.where(near_ref[0] == 0, own_ref[0:16, wide:].astype(F32), other_ref[0:16, wide:].astype(F32))
    slope_ref[...] = first[0:1, 0 : slope_ref.shape[1]]
    gate_ref[...] = first[1:2, :]
    gain_sum_ref[...] = row_sums(qkv_ref[...], w_ref, gain_ref)


def close(near, own, other, w_qkv, gain, heads):
    shard, wide = w_qkv.shape
    vmem = pl.BlockSpec(memory_space=pltpu.VMEM)
    return pl.pallas_call(
        close_body,
        in_specs=[scalar()] + [vmem] * 4,
        out_specs=[vmem] * 4,
        out_shape=[like((shard, wide), F32), like((1, shard), F32), like((1, shard), F32), like((1, heads), F32)],
        compiler_params=params(),
        cost_estimate=pl.CostEstimate(flops=0, transcendentals=0, bytes_accessed=2000000),
        name="close",
    )(near, *on_chip(own, other), w_qkv, gain[None])


def finish_body(tokens_ref, small_ref, gh1_ref, own_ref, away_ref, out_ref):
    unit, scale = spread(tokens_ref[...].astype(F32))
    grad = (own_ref[...] + away_ref[...].astype(F32)) * small_ref[0:1, :]
    out_ref[...] = gh1_ref[...] + spread_back(unit, scale, grad)


def finish(tokens, small, gh1, own, away):
    vmem = pl.BlockSpec(memory_space=pltpu.VMEM)
    return pl.pallas_call(
        finish_body,
        in_specs=[vmem] * 5,
        out_specs=vmem,
        out_shape=like(gh1.shape, F32),
        compiler_params=params(),
        cost_estimate=pl.CostEstimate(flops=0, transcendentals=0, bytes_accessed=4000000),
        name="finish",
    )(tokens, small, gh1, own, *on_chip(away))


def on_device(
    tokens, cotangent, deal, memory_len, neighbours,
    w_qkv, w_out, w_up, w_down, w_memory, gain_attn, gain_ffn, gate_vec, slopes,
):
    _, row_count, width = tokens.shape
    tokens = tokens.reshape(row_count, width)
    cotangent = cotangent.reshape(row_count, width)
    neighbours = neighbours.reshape(row_count, -1)
    block_count = deal.shape[0]
    ctx_size = lax.axis_size("ctx")
    own_blocks = block_count // ctx_size
    block_len = row_count // own_blocks
    shard = gain_attn.shape[0]
    heads_here = slopes.shape[0]
    groups = w_up.shape[1] // width
    me = lax.axis_index("wt").astype(jnp.int32).reshape(1)
    fast = ctx_size == 2 and lax.axis_size("seq") == 4
    slices = 8 if fast else 1

    short = jnp.concatenate(
        [gain_attn[None], gain_ffn[None], gate_vec[None], jnp.pad(slopes, (0, shard - heads_here))[None]], axis=0
    )
    pack = jnp.concatenate([w_qkv, jnp.pad(short, ((0, shard - 4), (0, 0)))], axis=1)
    others = swap(tokens, "ctx", 1)
    for bit in bits_of("ctx")[1:]:
        both = jnp.concatenate([tokens, others], axis=0)
        others = jnp.concatenate([others, swap(both, "ctx", bit)], axis=0)
    pack_far = swap(pack, "wt", 2)
    pack_near = swap(pack, "wt", 1)
    wide = lay_rows(width, [(w_out, 0), (w_memory, 0)] + [(w_up, width * g) for g in range(groups)] + [(w_down, 0)])
    neighbours = hold(neighbours, wide)

    offsets = jnp.arange(block_len, dtype=jnp.int32)
    owners = lax.axis_index("ctx") ^ jnp.arange(ctx_size, dtype=jnp.int32)
    slots = (owners[:, None] * own_blocks + jnp.arange(own_blocks, dtype=jnp.int32)[None, :]).reshape(-1)
    block_ids = jnp.arange(block_count, dtype=jnp.int32)
    slot_hot = (slots[:, None] == block_ids[None, :]).astype(jnp.int32)
    key_blocks = jnp.sum(slot_hot * deal[None, :], axis=1)
    key_pos = (key_blocks[:, None] * block_len + offsets[None, :]).reshape(-1)
    my_blocks = key_blocks[:own_blocks]
    row_pos = key_pos[:row_count]
    memory_hot = (my_blocks[:, None] == block_ids[None, :]).astype(jnp.int32)
    my_memory = jnp.sum(memory_hot * memory_len, axis=1)
    row_start = jnp.repeat(my_blocks * block_len, block_len)
    row_low = row_start - jnp.repeat(my_memory, block_len)
    picks = neighbours.shape[1]
    hits = sum((neighbours[:, n : n + 1] == key_pos[None, :]).astype(F32) for n in range(picks))
    count = jnp.where(hits == 1.0, 0.0, ABSENT)
    for times in range(2, picks + 1):
        count = jnp.where(hits == float(times), math.log(times), count)
    pack_far, wide = lax.optimization_barrier((pack_far, wide, count))[:2]
    pack_both = swap(pack_far, "wt", 1)
    wide_far = swap(wide, "wt", 2)
    wide_near = swap(wide, "wt", 1)
    row_pos = hold(row_pos, pack_far)
    distance = jnp.log(jnp.abs(row_pos[:, None] - key_pos[None, :]).astype(F32) + 1.0)
    visible = (key_pos[None, :] >= row_low[:, None]) & (key_pos[None, :] < (row_start + block_len)[:, None])
    bias = jnp.where(visible, distance, HIDDEN)

    q, k, v, turned, full_qkv, small = project(
        me, tokens, hold(others, bias), (pack, pack_near, pack_far, pack_both)
    )
    saved = attend_forward(small, q, k, v, bias, count)
    wide_both = swap(hold(wide_far, saved[0]), "wt", 1)
    wides = (wide, wide_near, wide_far, wide_both)
    layer_out, gh1, go, gm, gate, g0, g1, g2, g3, h0, h1, h2, h3 = middle(
        slices, me, small, tokens, cotangent, saved[0], saved[1], wides, groups
    )

    all_pairs = width // 128
    g_far = add_low(g2, swap(g3, "wt", 1))
    g_one = swap(g1, "wt", 1)
    if fast:
        h_far = add_low(h2, swap(h3, "wt", 1))
        h_own = add_low(h0, swap(h1, "wt", 1))
        g_got = swap(g_far, "wt", 2)
        both = jnp.concatenate([h_far.reshape(2, -1, width), h_own.reshape(2, -1, width)], axis=1)
        both_keep, both_got = send_half(both.reshape(-1, width), "ctx", 1)
        gq, gk, gv, gs = attend_backward(q, k, v, hold(go, g_far, both_keep), gm, saved, bias, 0, all_pairs)
        gq, gk, gv, gs, g_got, both_got = lax.optimization_barrier((gq, gk, gv, gs, g_got, both_got))
        cut = both_got.shape[0] // 2
        far_keep, own_keep = both_keep[:cut], both_keep[cut:]
        far_got, own_got = both_got[:cut], both_got[cut:]
        h_got = swap(add_low(far_keep, far_got), "wt", 2)
        g_keep, g_near = send_half(add_all(g0, [g_one, g_got]), "ctx", 1)
        q0, q1, q2, q3 = weight_grads(me, turned, hold(gq, g_keep), gk, gv, gs, gate)
        q_three, q_one = swap(q3, "wt", 1), swap(q1, "wt", 1)
        gq, q0, q2, g_near, h_got = lax.optimization_barrier((gq, q0, q2, g_near, h_got))
        q_far = add_low(q2, q_three)
        lower = add_low(g_keep, g_near).reshape(4, -1, width)
        higher = add_all(own_keep, [own_got, h_got]).reshape(4, -1, width)
        gh_keep, gh_got = send_half(jnp.concatenate([lower, higher], axis=1).reshape(-1, width), "seq", 1)
        near, own = row_grads(hold(gq, q_far, gh_keep), gk, gv, full_qkv)
        q_far = swap(q_far, "wt", 2)
        order = Order()
        near, gh_got = order.arrive(near, gh_got)
        gh = add_low(gh_keep, gh_got)
        gh_got = swap(gh, "seq", 2)
        q_keep, q_got = send_half(add_all(q0, [q_one, order.arrive(q_far)]), "ctx", 1)
        q_sum = add_low(q_keep, order.arrive(q_got))
        q_got = swap(q_sum, "seq", 1)
        away = swap(hold(near, gh), "ctx", 1)
        q_got, gh_got = order.arrive(q_got, gh_got)
        own_a = add_low(gh, gh_got)
        q_sum = add_low(q_sum, q_got)
        q_got = swap(hold(q_sum, own_a), "seq", 2)
        own_b = swap(own_a, "seq", 1)
        other_a = swap(own_a, "ctx", 1)
        away = order.arrive(away)
        grad_tokens = finish(tokens, small, gh1, own, away)
        order.before = (grad_tokens,)
        q_sum = add_low(q_sum, order.arrive(q_got))
        q_other = swap(q_sum, "ctx", 1)
        own_b = order.arrive(own_b)
        other_a = order.arrive(other_a)
        cut = own_b.shape[0] // 2
        by_seq = swap(other_a[cut:], "seq", 1)
        by_ctx = swap(own_b[:cut], "ctx", 1)
        side = lax.axis_index("ctx").astype(jnp.int32).reshape(1)
        pair = side_of("seq", 1).astype(jnp.int32).reshape(1)
        t_qkv, *shorts = close(side, q_sum, order.arrive(q_other), w_qkv, gain_attn, heads_here)
        order.before = (t_qkv,)
        by_ctx, by_seq = order.arrive(by_ctx, by_seq)
        t_out, t_memory, t_down, t_up, t_gain_two = assemble(
            side, pair, (own_a, own_b, other_a, by_ctx, by_seq), w_up, gain_ffn
        )
        t_gain_one, t_gate, t_slopes, t_gain_two = (value.reshape(-1) for value in (*shorts, t_gain_two))
    else:
        h_far = add_low(h2, swap(h3, "wt", 1))
        h_one = swap(h1, "wt", 1)
        g_sum = add_all(g0, [g_one, swap(g_far, "wt", 2)])
        h_sum = add_all(h0, [h_one, swap(h_far, "wt", 2)])
        gq, gk, gv, gs = attend_backward(q, k, v, go, gm, saved, bias, 0, all_pairs)
        grads = weight_grads(me, turned, gq, gk, gv, gs, gate)
        near, own = row_grads(gq, gk, gv, full_qkv)
        for bit in reversed(bits_of("ctx")[1:]):
            both = jnp.concatenate([own.astype(BF16), near], axis=0)
            fold = bit * row_count
            folded = both[:fold].astype(F32) + swap(both[fold:], "ctx", bit).astype(F32)
            own, near = folded[:row_count], folded[row_count:].astype(BF16)
        away = swap(near, "ctx", 1)
        q_far = swap(add_low(grads[2], swap(grads[3], "wt", 1)), "wt", 2)
        q_sum = add_all(grads[0], [swap(grads[1], "wt", 1), q_far])
        q_sum = near_whole(far_both(near_halves(q_sum)))
        g_sum = near_whole(far_whole(far_halves(near_halves(g_sum))))
        h_sum = near_whole(far_whole(far_halves(near_halves(h_sum))))
        grad_tokens = finish(tokens, small, gh1, own, away)
        t_out = g_sum[:shard].astype(F32)
        t_memory = g_sum[shard : 2 * shard].astype(F32)
        t_down = g_sum[2 * shard : 2 * shard + width].astype(F32)
        t_up = jnp.concatenate([h_sum[shard * g : shard * (g + 1)] for g in range(groups)], axis=1).astype(F32)
        t_qkv = q_sum[:, : 3 * width].astype(F32)
        t_slopes = q_sum[0, 3 * width : 3 * width + heads_here].astype(F32)
        t_gate = q_sum[1, 3 * width : 3 * width + shard].astype(F32)
        t_gain_one = jnp.sum(t_qkv * w_qkv.astype(F32), axis=1) / gain_attn.astype(F32)
        t_gain_two = jnp.sum(t_up * w_up.astype(F32), axis=1) / gain_ffn.astype(F32)


    return (
        layer_out[None], grad_tokens[None], t_qkv, t_out, t_up, t_down, t_memory,
        t_gain_one, t_gain_two, t_gate, t_slopes,
    )


def solution(mesh):
    rows = P(("seq", "wt"), "ctx", None)
    weight = P("wt", None)
    vector = P("wt")
    return jax.shard_map(
        on_device,
        mesh=mesh,
        in_specs=(rows, rows, P(), P(("seq", "wt"), None), rows) + (weight,) * 5 + (vector,) * 4,
        out_specs=(rows, rows) + (weight,) * 5 + (vector,) * 4,
        check_vma=False,
    )
```
